32 devices in a mesh: fsdp: 32 (over z, y, x, core).
Axes of the slice: x: 2, y: 2, z: 4, core: 2. Of those that a mesh axis runs over, the one named last changes fastest.
Arguments:
- tokens: bfloat16 [16384, 1024], P('fsdp'), may hold values from -6 to 6
- attention_gain: float32 [1024], P('fsdp'), may hold values from 0.5 to 1.5
- query_weight: float32 [1024, 1024], P('fsdp'), may hold values from -0.09375 to 0.09375
- key_weight: float32 [1024, 1024], P('fsdp'), may hold values from -0.09375 to 0.09375
- value_weight: float32 [1024, 1024], P('fsdp'), may hold values from -0.1875 to 0.1875
- output_weight: float32 [1024, 1024], P('fsdp'), may hold values from -0.5 to 0.5
- feedforward_gain: float32 [1024], P('fsdp'), may hold values from 0.5 to 1.5
- inner_weight: float32 [1024, 4096], P('fsdp'), may hold values from -0.1875 to 0.1875
- outer_weight: float32 [4096, 1024], P('fsdp'), may hold values from -0.125 to 0.125
- bias_table: float32 [32, 16], replicated, may hold values from -4 to 4
- segment_ids: int32 [16384], P('fsdp'), may hold values from 0 to 255, as said below
- positions: int32 [16384], P('fsdp'), may hold values from 0 to 255, as said below
- cotangent: bfloat16 [16384, 1024], P('fsdp'), may hold values from -6 to 6
Outputs:
- layer_output: bfloat16 [16384, 1024], P('fsdp')
- tokens_gradient: bfloat16 [16384, 1024], P('fsdp')
- attention_gain_gradient: float32 [1024], P('fsdp')
- query_gradient: float32 [1024, 1024], P('fsdp')
- key_gradient: float32 [1024, 1024], P('fsdp')
- value_gradient: float32 [1024, 1024], P('fsdp')
- output_gradient: float32 [1024, 1024], P('fsdp')
- feedforward_gain_gradient: float32 [1024], P('fsdp')
- inner_gradient: float32 [1024, 4096], P('fsdp')
- outer_gradient: float32 [4096, 1024], P('fsdp')
- table_gradient: float32 [32, 16], replicated
The draws below stay inside these ranges and needn't reach their ends.
Inputs may be any that keep to these rules, and one draw needn't show every extreme that they name: `segment_ids`: in each packed sequence of 256 consecutive tokens the number starts at 0 and rises by 0 or 1 from one token to the next. In the last packed sequence every token is a document of its own. `positions`: the number of tokens since the start of the token's document; a document starts at the start of each packed sequence and wherever segment_ids rises. The first packed sequence is one whole document.
All inputs are finite; a program needn't handle non-finite values.
Results may differ from the reference program's by a relative error of at most 0.013.
The reference program's roundings to bfloat16 on the way count: a program that leaves them out, or rounds other values in their place, can miss the bound.
Values may be sent and summed in bfloat16 or wider, within the bound.
No kernel may reach another device: no remote copies, remote signals or barrier semaphores. Data moves between devices by JAX's collectives and lax.ppermute only.
A program may use at most 192 MiB of HBM per device.

```python
import math
import jax
import jax.numpy as jnp
from jax import lax

D = 1024
HEADS = 16
HEAD = 64
FF = 4096
NB = 32
SEQ = 256
TOKENS = 16384


def document_layout(key):
    base = jax.random.fold_in(key, 11)
    rate_key, tick_key = jax.random.split(base)
    sequences = TOKENS // SEQ
    powers = jax.random.randint(rate_key, (sequences, 1), 1, 9)
    rate_rows = jnp.left_shift(jnp.ones_like(powers), powers)
    tick_rows = jax.random.randint(tick_key, (sequences, SEQ), 0, 1 << 20)
    column = jnp.arange(SEQ, dtype=jnp.int32)[None, :]
    row_index = jnp.arange(sequences, dtype=jnp.int32)[:, None]
    starts = jnp.logical_or(tick_rows % rate_rows == 0, column == 0)
    starts = jnp.logical_and(starts, jnp.logical_or(row_index != 0, column == 0))
    starts = jnp.logical_or(starts, row_index == sequences - 1)
    segment_rows = jnp.cumsum(starts.astype(jnp.int32), axis=1) - 1
    first_index = lax.cummax(jnp.where(starts, column, 0), axis=1)
    return (segment_rows.reshape(-1).astype(jnp.int32), (column - first_index).reshape(-1).astype(jnp.int32))


def draw_segment_ids(key, part):
    return document_layout(key)[0]


def draw_positions(key, part):
    return document_layout(key)[1]


def block_levels(stream_key, extent, cuts, least, largest):
    def one(dim, blocks):
        heights = jax.random.uniform(jax.random.fold_in(jax.random.fold_in(stream_key, 6), dim), (blocks,), jnp.float32, least / len(cuts), largest / len(cuts))
        return jnp.repeat(jnp.exp(heights), extent[dim] // blocks).reshape((-1,) + (1,) * (len(extent) - dim - 1))

    level = one(*cuts[0])
    for cut in cuts[1:]:
        level = level * one(*cut)
    return level


def bell_draw(stream_key, extent, deviation, bound, cuts=(), kind=jnp.bfloat16):
    array = deviation * jax.random.normal(stream_key, extent, jnp.float32)
    if cuts:
        array = array * block_levels(stream_key, extent, cuts, -0.22, 0.18)
    return jnp.clip(array, -bound, bound).astype(kind)


def setup_inputs(seed: int = 0) -> dict:
    key_list = jax.random.split(jax.random.key(seed), 14)
    return {
        "tokens": bell_draw(key_list[0], (TOKENS, D), 1.0, 6.0, ((0, 32),)),
        "attention_gain": jnp.clip(1.0 + 0.1 * jax.random.normal(key_list[1], (D,), jnp.float32), 0.5, 1.5),
        "query_weight": bell_draw(key_list[2], (D, D), (4 * D) ** -0.5, 0.09375, ((0, 32),), jnp.float32),
        "key_weight": bell_draw(key_list[3], (D, D), (4 * D) ** -0.5, 0.09375, ((0, 32),), jnp.float32),
        "value_weight": bell_draw(key_list[4], (D, D), D ** -0.5, 0.1875, ((0, 32),), jnp.float32),
        "output_weight": bell_draw(key_list[5], (D, D), (D // 8) ** -0.5, 0.5, ((0, 32),), jnp.float32),
        "feedforward_gain": jnp.clip(1.0 + 0.1 * jax.random.normal(key_list[6], (D,), jnp.float32), 0.5, 1.5),
        "inner_weight": bell_draw(key_list[7], (D, FF), D ** -0.5, 0.1875, ((0, 32),), jnp.float32),
        "outer_weight": bell_draw(key_list[8], (FF, D), (FF // 2) ** -0.5, 0.125, ((0, 32),), jnp.float32),
        "bias_table": bell_draw(key_list[9], (NB, HEADS), 1.0, 4.0, (), jnp.float32),
        "segment_ids": draw_segment_ids(jax.random.fold_in(key_list[13], 71), 0),
        "positions": draw_positions(jax.random.fold_in(key_list[13], 71), 0),
        "cotangent": bell_draw(key_list[12], (TOKENS, D), 1.0, 6.0, ((0, 32),)),
    }


@jax.custom_vjp
def low(v):
    return lax.optimization_barrier(v.astype(jnp.bfloat16)).astype(jnp.float32)

@jax.custom_vjp
def low_back(v):
    return v

def low_keep(v):
    return (low(v), None)

def low_pass(kept, grad):
    return (grad,)

def back_keep(v):
    return (v, None)

def back_low(kept, grad):
    return (low(grad),)
low.defvjp(low_keep, low_pass)
low_back.defvjp(back_keep, back_low)
EPSILON = 1e-06
MASKED = -1000000000.0
LIMITS = (12, 16, 23, 32, 46, 64, 91)
HIGHEST = lax.Precision.HIGHEST

def bucket_of(relative):
    distance = jnp.abs(relative)
    counted = jnp.zeros_like(distance)
    for threshold in LIMITS:
        counted = counted + (distance >= threshold).astype(jnp.int32)
    inside = jnp.where(distance < 8, distance, 8 + counted)
    return inside + jnp.where(relative > 0, 16, 0).astype(jnp.int32)

def norm_scale(values, gain):
    factor = lax.rsqrt(lax.optimization_barrier(jnp.mean(values * values, axis=-1, keepdims=True)) + EPSILON)
    return values * factor * gain

def forward_layer(params, inputs, segments, places):
    query_weight, key_weight, value_weight, output_weight, attention_gain, inner_weight, outer_weight, feedforward_gain, bias_table = params
    groups, length, width = inputs.shape
    normed_one = low(norm_scale(inputs, low(attention_gain)))

    def project(weight):
        made = jnp.einsum('gsd,de->gse', normed_one, low(weight), precision=HIGHEST)
        return low(low_back(made)).reshape(groups, length, HEADS, HEAD)
    queries = project(query_weight)
    key_rows = project(key_weight)
    value_rows = project(value_weight)
    allowed = segments[:, :, None] == segments[:, None, :]
    relative = places[:, None, :] - places[:, :, None]
    offsets = jnp.arange(2 * length - 1, dtype=jnp.int32) - (length - 1)
    lookup = (bucket_of(offsets)[:, None] == jnp.arange(NB, dtype=jnp.int32)[None, :]).astype(jnp.float32)
    distance_table = jnp.dot(lookup, bias_table, precision=HIGHEST)
    biases = jnp.moveaxis(jnp.take(distance_table, (relative + (length - 1)).astype(jnp.int32), axis=0), 3, 1)
    scores = jnp.einsum('gqhe,gkhe->ghqk', queries, key_rows, precision=HIGHEST) + biases
    scores = low_back(jnp.where(allowed[:, None], scores, MASKED))
    row_top = lax.optimization_barrier(jnp.max(scores, axis=-1, keepdims=True))
    exponent = jnp.exp(scores - row_top)
    softmax_rows = low(exponent / lax.optimization_barrier(jnp.sum(exponent, axis=-1, keepdims=True)))
    context = jnp.einsum('ghqk,gkhe->gqhe', softmax_rows, value_rows, precision=HIGHEST).reshape(groups, length, width)
    context = low(low_back(context))
    attended = low_back(jnp.einsum('gsd,de->gse', context, low(output_weight), precision=HIGHEST))
    middle = inputs + attended
    normed_two = low(norm_scale(middle, low(feedforward_gain)))
    inner = low_back(jnp.einsum('gsd,df->gsf', normed_two, low(inner_weight), precision=HIGHEST))
    hidden = low(jax.nn.gelu(inner, approximate=False))
    return middle + low_back(jnp.einsum('gsf,fd->gsd', hidden, low(outer_weight), precision=HIGHEST))

def reference(tokens, attention_gain, query_weight, key_weight, value_weight, output_weight, feedforward_gain, inner_weight, outer_weight, bias_table, segment_ids, positions, cotangent):
    sequences = TOKENS // SEQ
    per_group = math.gcd(sequences, max(1, 2048 // SEQ))
    group_count = sequences // per_group
    params = tuple((weight.astype(jnp.float32) for weight in (query_weight, key_weight, value_weight, output_weight, attention_gain, inner_weight, outer_weight, feedforward_gain, bias_table)))
    inputs = tokens.astype(jnp.float32).reshape(group_count, per_group, SEQ, D)
    upstream = cotangent.astype(jnp.float32).reshape(group_count, per_group, SEQ, D)
    segments = segment_ids.reshape(group_count, per_group, SEQ)
    places = positions.reshape(group_count, per_group, SEQ)

    def step_group(totals, pieces):
        inputs_group, upstream_group, segments_group, places_group = pieces

        def local_layer(weights, values):
            return forward_layer(weights, values, segments_group, places_group)
        outputs, pullback = jax.vjp(local_layer, params, inputs_group)
        weight_grads, input_grads = pullback(upstream_group)
        totals = jax.tree.map(jnp.add, totals, weight_grads)
        return (totals, (outputs.astype(jnp.bfloat16), input_grads.astype(jnp.bfloat16)))
    zeros = jax.tree.map(jnp.zeros_like, params)
    totals, stacked = lax.scan(step_group, zeros, (inputs, upstream, segments, places))
    outputs, input_grads = stacked
    return (outputs.reshape(TOKENS, D), input_grads.reshape(TOKENS, D), totals[4], totals[0], totals[1], totals[2], totals[3], totals[7], totals[5], totals[6], totals[8])
```

```python
import functools
import math

import jax
import jax.numpy as jnp
from jax import lax
from jax.experimental import pallas as pl
from jax.experimental.pallas import tpu as pltpu
from jax.sharding import PartitionSpec as P

AXIS = "fsdp"
HEADS = 16
HEAD = 64
NB = 32
SEQ = 256
SPAN = 2 * SEQ
LANES = 128
EPSILON = 1e-06
MASKED = -1000000000.0
LIMITS = (12, 16, 23, 32, 46, 64, 91)
HIGHEST = lax.Precision.HIGHEST
BF16 = jnp.bfloat16
F32 = jnp.float32
MIB = 1 << 20
VMEM_LIMIT = 56 * MIB
ANY = pl.BlockSpec(memory_space=pl.ANY)
VM = pl.BlockSpec(memory_space=pltpu.VMEM)


def bucket_of(relative):
    distance = jnp.abs(relative)
    counted = jnp.zeros_like(distance)
    for threshold in LIMITS:
        counted = counted + (distance >= threshold).astype(jnp.int32)
    inside = jnp.where(distance < 8, distance, 8 + counted)
    return inside + jnp.where(relative > 0, 16, 0).astype(jnp.int32)


def offset_lookup():
    k = lax.broadcasted_iota(jnp.int32, (8, SPAN, NB), 1)
    b = lax.broadcasted_iota(jnp.int32, (8, SPAN, NB), 0)
    c = lax.broadcasted_iota(jnp.int32, (8, SPAN, NB), 2)
    offset = k - b
    offset = jnp.where(offset >= SEQ, offset - SPAN, offset)
    return (bucket_of(offset) == c).astype(F32)


def bit_orders(n):
    if n == 32:
        x, y, z0, z1 = 1, 2, 3, 4
        return ((z0, z1, y, x, 0), (z1, x, z0, y, 0), (z1, y, x, z0, 0))
    high = list(range(1, n.bit_length() - 1))
    return tuple(tuple(high[k % len(high) :] + high[: k % len(high)] + [0]) for k in range(3))


def swap(array, bit, n):
    return lax.ppermute(array, AXIS, [(i, i ^ (1 << bit)) for i in range(n)])


def relative(bits, t):
    return sum(1 << b for k, b in enumerate(bits) if (t >> k) & 1)


def gather_stream(own, bits, n):
    have = own[None]
    for b in bits[:-2]:
        have = jnp.concatenate([have, swap(have, b, n)], axis=0)
    far = swap(have, bits[-2], n)
    return [have, far, swap(have, bits[-1], n), swap(far, bits[-1], n)]


def scatter_stream(send, keep, bits, n):
    total = keep.astype(F32) + swap(send, bits[-1], n).astype(F32)
    for b in reversed(bits[:-1]):
        half = total.shape[0] // 2
        given = swap(total[half:].astype(BF16), b, n)
        total = total[:half] + given.astype(F32)
    return total[0]


def sum_all(values, n):
    for b in range(n.bit_length() - 1):
        values = values + swap(values, b, n)
    return values


class Layout:
    def __init__(self, n, rows, cuts, orders):
        self.n, self.rows = n, rows
        self.cuts, self.orders = cuts, orders
        self.paired = n & (n - 1) == 0 and n >= 8 and rows % 16 == 0
        if not self.paired:
            self.cuts, self.orders = (cuts[-1],), (None,)

    def spans(self):
        return tuple(zip((0,) + tuple(self.cuts[:-1]), self.cuts))

    def gather(self, block):
        if not self.paired:
            return [lax.all_gather(block, AXIS, axis=0, tiled=True)]
        out = []
        for (lo, hi), bits in zip(self.spans(), self.orders):
            out += gather_stream(block[:, lo:hi], bits, self.n)
        return out

    def count(self):
        return 4 * len(self.cuts) if self.paired else 1

    def load(self, me, refs, full, sems):
        if not self.paired:
            copy = pltpu.make_async_copy(refs[0], full, sems.at[0])
            copy.start()
            return [copy.wait]
        waits = []
        for s, ((lo, hi), bits) in enumerate(zip(self.spans(), self.orders)):
            for q in range(4):
                ref = refs[4 * s + q]
                for j in range(self.n // 4):
                    row = pl.multiple_of((me ^ relative(bits, q * (self.n // 4) + j)) * self.rows, self.rows)
                    pltpu.make_async_copy(
                        ref.at[j], full.at[pl.ds(row, self.rows), lo:hi], sems.at[s]
                    ).start()
            view = full.at[:, lo:hi]
            waits.append(pltpu.make_async_copy(view, view, sems.at[s]).wait)
        return waits

    def out_shapes(self):
        if not self.paired:
            return [jax.ShapeDtypeStruct((self.n * self.rows, self.cuts[-1]), BF16)]
        half = self.n // 2
        return [
            jax.ShapeDtypeStruct((half, self.rows, hi - lo), BF16)
            for lo, hi in self.spans()
            for _ in range(2)
        ]

    def store(self, me, stage, refs, sems, s):
        if not self.paired:
            copy = pltpu.make_async_copy(stage, refs[0], sems.at[0])
            copy.start()
            return [copy.wait]
        lo, hi = self.spans()[s]
        half = self.n // 2
        waits = []
        for part in (1, 0):
            ref = refs[2 * s + 1 - part]
            for j in range(half):
                row = pl.multiple_of((me ^ relative(self.orders[s], part * half + j)) * self.rows, self.rows)
                pltpu.make_async_copy(
                    stage.at[pl.ds(row, self.rows), lo:hi], ref.at[j], sems.at[2 * s + part]
                ).start()
            waits.append(pltpu.make_async_copy(ref, ref, sems.at[2 * s + part]).wait)
        return waits

    def scatter(self, parts):
        if not self.paired:
            return lax.psum_scatter(parts[0].astype(F32), AXIS, scatter_dimension=0, tiled=True)
        pieces = [
            scatter_stream(parts[2 * s], parts[2 * s + 1], bits, self.n)
            for s, bits in enumerate(self.orders)
        ]
        return jnp.concatenate(pieces, axis=1)


def dot(a, b):
    return lax.dot_general(a, b, (((1,), (0,)), ((), ())), preferred_element_type=F32)


def dot_nt(a, b):
    return lax.dot_general(a, b, (((1,), (1,)), ((), ())), preferred_element_type=F32)


def dot_tn(a, b):
    return lax.dot_general(a, b, (((0,), (0,)), ((), ())), preferred_element_type=F32)


def row_scale(values):
    return lax.rsqrt(jnp.mean(values * values, axis=-1, keepdims=True) + EPSILON)


def toeplitz(base):
    return jnp.concatenate(
        [(pltpu.roll(base, 8 * a, 1) if a else base)[:, :SEQ] for a in range(SEQ // 8)], axis=0
    )


def diagonals(scores):
    total = None
    for a in range(SEQ // 8):
        rows = scores[8 * a : 8 * a + 8]
        rows = jnp.concatenate([rows, jnp.zeros((8, SPAN - SEQ), F32)], axis=1)
        if a:
            rows = pltpu.roll(rows, SPAN - 8 * a, 1)
        total = rows if total is None else total + rows
    return total


def transposed(values):
    return values.T


def copy_out(copies, sems, k, source, target):
    copy = pltpu.make_async_copy(source, target, sems.at[k])
    copy.start()
    copies.append(copy)


def attention_kernel(lay, seqs, width, *refs):
    m = lay.count()
    x_ref, segc_ref, segr_ref, base_ref = refs[:4]
    blocks = refs[4 : 4 + m]
    (wa_out, gain_ref, q_out, k_out, v_out, p_out, h1t_out, ct_out, x1_ref, h2_ref, h2t_ref) = refs[4 + m : 15 + m]
    wa, h1, q_s, k_s, v_s, c_s, p_s, h1t, ct, lsem, osem, psem = refs[15 + m :]
    me = lax.axis_index(AXIS)
    waits = lay.load(me, blocks, wa, lsem)
    for wait in waits:
        wait()
    copies = []
    copy_out(copies, osem, 0, wa, wa_out)
    gains = wa[:, 4 * width : 4 * width + LANES].astype(F32).T
    gain_ref[...] = gains[:8]
    x = x_ref[...].astype(F32)
    h1[...] = (x * row_scale(x) * gains[0:1]).astype(BF16)
    for k, (ref, out) in enumerate(((q_s, q_out), (k_s, k_out), (v_s, v_out))):
        for c in range(0, width, 512):
            ref[:, c : c + 512] = dot(h1[...], wa[:, k * width + c : k * width + c + 512]).astype(BF16)
        copy_out(copies, osem, 1 + k, ref, out)
    h1t[...] = transposed(h1[...])
    copy_out(copies, osem, 4, h1t, h1t_out)

    def pair(p, carry):
        lanes = pl.ds(pl.multiple_of(p * LANES, LANES), LANES)
        first = lax.broadcasted_iota(jnp.int32, (SEQ, LANES), 1) < HEAD
        biases = [toeplitz(base_ref[2 * p + o]) for o in range(2)]
        for s in range(seqs):
            rows = slice(s * SEQ, (s + 1) * SEQ)
            q2, k2, v2 = q_s[rows, lanes], k_s[rows, lanes], v_s[rows, lanes]
            allowed = segc_ref[rows, :] == segr_ref[s : s + 1, :]
            made = []
            for o in range(2):
                mine = jnp.where(first == (o == 0), q2, jnp.zeros_like(q2))
                scores = jnp.where(allowed, dot_nt(mine, k2) + biases[o], MASKED)
                exponent = jnp.exp(scores - jnp.max(scores, axis=-1, keepdims=True))
                prob = exponent * (1.0 / jnp.sum(exponent, axis=-1, keepdims=True))
                p_s[s, 2 * p + o] = prob
                made.append(dot(prob.astype(BF16), v2))
            c_s[rows, lanes] = jnp.where(first, made[0], made[1]).astype(BF16)
            pltpu.make_async_copy(p_s.at[s, pl.ds(2 * p, 2)], p_out.at[s, pl.ds(2 * p, 2)], psem).start()
        return carry

    lax.fori_loop(0, HEADS // 2, pair, 0)
    ct[...] = transposed(c_s[...])
    copy_out(copies, osem, 5, ct, ct_out)
    for c in range(0, width, 512):
        x1_ref[:, c : c + 512] = x_ref[:, c : c + 512].astype(F32) + dot(
            c_s[...], wa[:, 3 * width + c : 3 * width + c + 512]
        )
    x1 = x1_ref[...]
    h2 = (x1 * row_scale(x1) * gains[1:2]).astype(BF16)
    h2_ref[...] = h2
    h2t_ref[...] = transposed(h2)
    for copy in copies:
        copy.wait()
    pltpu.make_async_copy(p_s, p_out, psem).wait()


def attention_forward(lay, x, segments, base, blocks):
    tokens, width = x.shape
    seqs = tokens // SEQ
    wide = lay.cuts[-1]
    sds = jax.ShapeDtypeStruct
    shapes = [
        sds((width, wide), BF16),
        sds((8, width), F32),
        sds((tokens, width), BF16),
        sds((tokens, width), BF16),
        sds((tokens, width), BF16),
        sds((seqs, HEADS, SEQ, SEQ), F32),
        sds((width, tokens), BF16),
        sds((width, tokens), BF16),
        sds((tokens, width), F32),
        sds((tokens, width), BF16),
        sds((width, tokens), BF16),
    ]
    flops = 2 * tokens * width * 4 * width + 4 * tokens * SEQ * width
    return pl.pallas_call(
        functools.partial(attention_kernel, lay, seqs, width),
        out_shape=shapes,
        in_specs=[VM] * 4 + [ANY] * len(blocks),
        out_specs=[ANY, VM] + [ANY] * 6 + [VM] * 3,
        scratch_shapes=[
            pltpu.VMEM((width, wide), BF16),
            pltpu.VMEM((tokens, width), BF16),
            pltpu.VMEM((tokens, width), BF16),
            pltpu.VMEM((tokens, width), BF16),
            pltpu.VMEM((tokens, width), BF16),
            pltpu.VMEM((tokens, width), BF16),
            pltpu.VMEM((seqs, HEADS, SEQ, SEQ), F32),
            pltpu.VMEM((width, tokens), BF16),
            pltpu.VMEM((width, tokens), BF16),
            pltpu.SemaphoreType.DMA((max(1, len(lay.cuts)),)),
            pltpu.SemaphoreType.DMA((6,)),
            pltpu.SemaphoreType.DMA,
        ],
        compiler_params=pltpu.CompilerParams(vmem_limit_bytes=VMEM_LIMIT),
        cost_estimate=pl.CostEstimate(flops=flops, transcendentals=tokens * SEQ * HEADS, bytes_accessed=40 * MIB),
        name="attention_forward",
    )(x, segments.reshape(tokens, 1), segments.reshape(seqs, SEQ), base, *blocks)


def inner_kernel(lay, lay_out, chunk, *refs):
    m, k = lay.count(), len(lay_out.out_shapes())
    h2_ref, e_ref = refs[:2]
    blocks = refs[2 : 2 + m]
    z_out, g_out = refs[2 + m : 4 + m]
    grads = refs[4 + m : 4 + m + k]
    wi, z_s, g_s, stage, lsem, osem, gsem = refs[4 + m + k :]
    me = lax.axis_index(AXIS)
    for wait in lay.load(me, blocks, wi, lsem):
        wait()
    hidden = wi.shape[1]

    def step(c, carry):
        cols = pl.ds(pl.multiple_of(c * chunk, chunk), chunk)
        u = dot(h2_ref[...], wi[:, cols])
        cdf = 0.5 * (1.0 + lax.erf(u * (1.0 / math.sqrt(2.0))))
        z = (u * cdf).astype(BF16)
        z_s[:, cols] = z
        g_s[:, cols] = cdf + u * jnp.exp(-0.5 * u * u) * (1.0 / math.sqrt(2.0 * math.pi))
        stage[cols, :] = dot(transposed(z), e_ref[...]).astype(BF16)
        pltpu.make_async_copy(z_s.at[:, cols], z_out.at[:, cols], osem.at[0]).start()
        pltpu.make_async_copy(g_s.at[:, cols], g_out.at[:, cols], osem.at[1]).start()
        return carry

    lax.fori_loop(0, hidden // chunk, step, 0)
    waits = []
    for s in range(len(lay_out.cuts)):
        waits += lay_out.store(me, stage, grads, gsem, s)
    pltpu.make_async_copy(z_s, z_out, osem.at[0]).wait()
    pltpu.make_async_copy(g_s, g_out, osem.at[1]).wait()
    for wait in waits:
        wait()


def inner_forward(lay, lay_out, h2, cotangent, blocks, hidden):
    tokens, width = h2.shape
    sds = jax.ShapeDtypeStruct
    grads = lay_out.out_shapes()
    return pl.pallas_call(
        functools.partial(inner_kernel, lay, lay_out, 512),
        out_shape=[sds((tokens, hidden), BF16), sds((tokens, hidden), F32)] + grads,
        in_specs=[VM] * 2 + [ANY] * len(blocks),
        out_specs=[ANY] * (2 + len(grads)),
        scratch_shapes=[
            pltpu.VMEM((width, hidden), BF16),
            pltpu.VMEM((tokens, hidden), BF16),
            pltpu.VMEM((tokens, hidden), F32),
            pltpu.VMEM((hidden, width), BF16),
            pltpu.SemaphoreType.DMA((max(1, len(lay.cuts)),)),
            pltpu.SemaphoreType.DMA((2,)),
            pltpu.SemaphoreType.DMA((2 * len(lay_out.cuts),)),
        ],
        compiler_params=pltpu.CompilerParams(vmem_limit_bytes=VMEM_LIMIT),
        cost_estimate=pl.CostEstimate(
            flops=4 * tokens * width * hidden, transcendentals=2 * tokens * hidden, bytes_accessed=32 * MIB
        ),
        name="feedforward_inner",
    )(h2, cotangent, *blocks)


def outer_kernel(lay_i, lay_f, lay_g, lay_o, chunk, *refs):
    mi, mf = lay_i.count(), lay_f.count()
    kg, ko = len(lay_g.out_shapes()), len(lay_o.out_shapes())
    e_ref, x1_ref, h2t_ref, gain_ref, g_in, ct_in = refs[:6]
    at = 6
    inner, outer = refs[at : at + mi], refs[at + mi : at + mi + mf]
    at += mi + mf
    dx1_ref, da_ref, dgain_ref = refs[at : at + 3]
    grads, grads_o = refs[at + 3 : at + 3 + kg], refs[at + 3 + kg : at + 3 + kg + ko]
    wi, wf, g_s, ct, stage, stage_o, lsem, isem, gsem, osem = refs[at + 3 + kg + ko :]
    me = lax.axis_index(AXIS)
    hidden = wi.shape[1]
    waits = lay_f.load(me, outer, wf, lsem.at[0]) + lay_i.load(me, inner, wi, lsem.at[1])
    steps = hidden // chunk
    for c in range(steps):
        cols = slice(c * chunk, (c + 1) * chunk)
        pltpu.make_async_copy(g_in.at[:, cols], g_s.at[:, cols], isem.at[c]).start()
    ct_copy = pltpu.make_async_copy(ct_in, ct, isem.at[steps])
    ct_copy.start()
    for wait in waits:
        wait()
    e = e_ref[...]
    dh2 = None
    done = []
    sent = 0
    for c in range(steps):
        cols = slice(c * chunk, (c + 1) * chunk)
        pltpu.make_async_copy(g_in.at[:, cols], g_s.at[:, cols], isem.at[c]).wait()
        du = (dot_nt(e, wf[cols, :]) * g_s[:, cols]).astype(BF16)
        stage[:, cols] = dot(h2t_ref[...], du).astype(BF16)
        part = dot_nt(du, wi[:, cols])
        if dh2 is None:
            dx1_ref[...] = part
            dh2 = True
        else:
            dx1_ref[...] += part
        if lay_g.paired:
            while sent < len(lay_g.cuts) and lay_g.cuts[sent] <= (c + 1) * chunk:
                done += lay_g.store(me, stage, grads, gsem, sent)
                sent += 1
    if not lay_g.paired:
        done += lay_g.store(me, stage, grads, gsem, 0)
    dh2 = dx1_ref[...]
    x1 = x1_ref[...]
    gain = gain_ref[1:2, :]
    scale = row_scale(x1)
    dgain_ref[...] = jnp.broadcast_to(jnp.sum(dh2 * (x1 * scale), axis=0, keepdims=True), dgain_ref.shape)
    mean = jnp.mean(x1 * gain * dh2, axis=-1, keepdims=True)
    dx1 = e.astype(F32) + scale * gain * dh2 - x1 * (scale * scale * scale) * mean
    dx1_ref[...] = dx1
    da = dx1.astype(BF16)
    da_ref[...] = da
    ct_copy.wait()
    stage_o[...] = dot(ct[...], da).astype(BF16)
    for s in range(len(lay_o.cuts)):
        done += lay_o.store(me, stage_o, grads_o, osem, s)
    for wait in done:
        wait()


def outer_backward(lay_i, lay_f, lay_g, lay_o, cotangent, x1, h2t, gain, g, ct, inner, outer, hidden):
    tokens, width = x1.shape
    chunk = 512
    sds = jax.ShapeDtypeStruct
    grads, grads_o = lay_g.out_shapes(), lay_o.out_shapes()
    return pl.pallas_call(
        functools.partial(outer_kernel, lay_i, lay_f, lay_g, lay_o, chunk),
        out_shape=[sds((tokens, width), F32), sds((tokens, width), BF16), sds((8, width), F32)] + grads + grads_o,
        in_specs=[VM] * 4 + [ANY] * (2 + len(inner) + len(outer)),
        out_specs=[VM] * 3 + [ANY] * (len(grads) + len(grads_o)),
        scratch_shapes=[
            pltpu.VMEM((width, hidden), BF16),
            pltpu.VMEM((hidden, width), BF16),
            pltpu.VMEM((tokens, hidden), F32),
            pltpu.VMEM((width, tokens), BF16),
            pltpu.VMEM((width, hidden), BF16),
            pltpu.VMEM((width, width), BF16),
            pltpu.SemaphoreType.DMA((2, 4)),
            pltpu.SemaphoreType.DMA((hidden // chunk + 1,)),
            pltpu.SemaphoreType.DMA((8,)),
            pltpu.SemaphoreType.DMA((8,)),
        ],
        compiler_params=pltpu.CompilerParams(vmem_limit_bytes=VMEM_LIMIT),
        cost_estimate=pl.CostEstimate(
            flops=6 * tokens * width * hidden + 2 * tokens * width * width,
            transcendentals=tokens,
            bytes_accessed=48 * MIB,
        ),
        name="feedforward_outer",
    )(cotangent, x1, h2t, gain, g, ct, *inner, *outer)


def scores_kernel(lay, seqs, width, *refs):
    k = len(lay.out_shapes())
    da_ref, q_ref, k_ref, v_ref, h1t_ref, wa_in, p_in = refs[:7]
    dq_ref, dk_ref, dv_ref, table_ref = refs[7:11]
    grads = refs[11 : 11 + k]
    wo, p_s, dc, stage, isem, psem, gsem = refs[11 + k :]
    me = lax.axis_index(AXIS)
    wo_copy = pltpu.make_async_copy(wa_in.at[:, 3 * width : 4 * width], wo, isem)
    wo_copy.start()
    for p in range(HEADS // 2):
        pltpu.make_async_copy(p_in.at[:, 2 * p : 2 * p + 2], p_s.at[:, 2 * p : 2 * p + 2], psem.at[p]).start()
    wo_copy.wait()
    for c in range(0, width, 512):
        dc[:, c : c + 512] = dot_nt(da_ref[...], wo[c : c + 512, :]).astype(BF16)

    def pair(p, carry):
        lanes = pl.ds(pl.multiple_of(p * LANES, LANES), LANES)
        heads = pl.ds(2 * p, 2)
        first = lax.broadcasted_iota(jnp.int32, (SEQ, LANES), 1) < HEAD
        pltpu.make_async_copy(p_in.at[:, heads], p_s.at[:, heads], psem.at[p]).wait()
        for o in range(2):
            total = None
            for s in range(seqs):
                rows = slice(s * SEQ, (s + 1) * SEQ)
                dc2, q2, k2, v2 = dc[rows, lanes], q_ref[rows, lanes], k_ref[rows, lanes], v_ref[rows, lanes]
                prob = p_s[s, 2 * p + o]
                mine = jnp.where(first == (o == 0), dc2, jnp.zeros_like(dc2))
                dprob = dot_nt(mine, v2)
                inner = jnp.sum(prob * dprob, axis=-1, keepdims=True)
                ds = (prob * (dprob - inner)).astype(BF16)
                wide = ds.astype(F32)
                total = wide if total is None else total + wide
                dv = dot(transposed(prob.astype(BF16)), dc2).astype(BF16)
                dq = dot(ds, k2).astype(BF16)
                dk = dot(transposed(ds), q2).astype(BF16)
                for ref, value in ((dv_ref, dv), (dq_ref, dq), (dk_ref, dk)):
                    if o == 0:
                        ref[rows, lanes] = value
                    else:
                        ref[rows, lanes] = jnp.where(first, ref[rows, lanes], value)
            table_ref[2 * p + o] = diagonals(total)
        return carry

    lax.fori_loop(0, HEADS // 2, pair, 0)
    for j, ref in enumerate((dq_ref, dk_ref, dv_ref)):
        for c in range(0, width, 512):
            stage[:, j * width + c : j * width + c + 512] = dot(h1t_ref[...], ref[:, c : c + 512]).astype(BF16)
    waits = []
    for s in range(len(lay.cuts)):
        waits += lay.store(me, stage, grads, gsem, s)
    for wait in waits:
        wait()


def scores_backward(lay, da, q, k, v, h1t, wa, p):
    tokens, width = da.shape
    seqs = tokens // SEQ
    sds = jax.ShapeDtypeStruct
    grads = lay.out_shapes()
    return pl.pallas_call(
        functools.partial(scores_kernel, lay, seqs, width),
        out_shape=[sds((tokens, width), BF16)] * 3 + [sds((HEADS, 8, SPAN), F32)] + grads,
        in_specs=[VM] * 5 + [ANY] * 2,
        out_specs=[VM] * 4 + [ANY] * len(grads),
        scratch_shapes=[
            pltpu.VMEM((width, width), BF16),
            pltpu.VMEM((seqs, HEADS, SEQ, SEQ), F32),
            pltpu.VMEM((tokens, width), BF16),
            pltpu.VMEM((width, 3 * width), BF16),
            pltpu.SemaphoreType.DMA,
            pltpu.SemaphoreType.DMA((HEADS // 2,)),
            pltpu.SemaphoreType.DMA((8,)),
        ],
        compiler_params=pltpu.CompilerParams(vmem_limit_bytes=VMEM_LIMIT),
        cost_estimate=pl.CostEstimate(
            flops=2 * tokens * width * 4 * width + 8 * tokens * SEQ * width,
            transcendentals=0,
            bytes_accessed=32 * MIB,
        ),
        name="attention_backward",
    )(da, q, k, v, h1t, wa, p)


def inputs_kernel(width, *refs):
    x_ref, dx1_ref, gain_ref, dq_ref, dk_ref, dv_ref, wa_in, dx_ref, dgain_ref, wa, dh, sem = refs
    copies = []
    for j in range(3):
        cols = slice(j * width, (j + 1) * width)
        copy_out(copies, sem, j, wa_in.at[:, cols], wa.at[:, cols])
    for j, ref in enumerate((dq_ref, dk_ref, dv_ref)):
        copies[j].wait()
        for c in range(0, width, 512):
            part = dot_nt(ref[...], wa[c : c + 512, j * width : (j + 1) * width])
            if j:
                dh[:, c : c + 512] += part
            else:
                dh[:, c : c + 512] = part
    x = x_ref[...].astype(F32)
    gain = gain_ref[0:1, :]
    scale = row_scale(x)
    dh1 = dh[...]
    dgain_ref[...] = jnp.broadcast_to(jnp.sum(dh1 * (x * scale), axis=0, keepdims=True), dgain_ref.shape)
    mean = jnp.mean(x * gain * dh1, axis=-1, keepdims=True)
    dx_ref[...] = (dx1_ref[...] + scale * gain * dh1 - x * (scale * scale * scale) * mean).astype(BF16)


def inputs_backward(x, dx1, gain, dq, dk, dv, wa):
    tokens, width = x.shape
    sds = jax.ShapeDtypeStruct
    return pl.pallas_call(
        functools.partial(inputs_kernel, width),
        out_shape=[sds((tokens, width), BF16), sds((8, width), F32)],
        in_specs=[VM] * 6 + [ANY],
        out_specs=[VM] * 2,
        scratch_shapes=[
            pltpu.VMEM((width, 3 * width), BF16),
            pltpu.VMEM((tokens, width), F32),
            pltpu.SemaphoreType.DMA((3,)),
        ],
        compiler_params=pltpu.CompilerParams(vmem_limit_bytes=VMEM_LIMIT),
        cost_estimate=pl.CostEstimate(
            flops=6 * tokens * width * width, transcendentals=tokens, bytes_accessed=16 * MIB
        ),
        name="inputs_backward",
    )(x, dx1, gain, dq, dk, dv, wa)


def output_kernel(lay, *refs):
    m = lay.count()
    x1_ref, z_ref = refs[:2]
    blocks = refs[2 : 2 + m]
    out_ref, wf, sem = refs[2 + m :]
    me = lax.axis_index(AXIS)
    for wait in lay.load(me, blocks, wf, sem):
        wait()
    width = wf.shape[1]
    for c in range(0, width, 512):
        cols = slice(c, c + 512)
        out_ref[:, cols] = (x1_ref[:, cols] + dot(z_ref[...], wf[:, cols])).astype(BF16)


def layer_output(lay, x1, z, blocks):
    tokens, width = x1.shape
    hidden = z.shape[1]
    return pl.pallas_call(
        functools.partial(output_kernel, lay),
        out_shape=jax.ShapeDtypeStruct((tokens, width), BF16),
        in_specs=[VM] * 2 + [ANY] * len(blocks),
        out_specs=VM,
        scratch_shapes=[
            pltpu.VMEM((hidden, width), BF16),
            pltpu.SemaphoreType.DMA((max(1, len(lay.cuts)),)),
        ],
        compiler_params=pltpu.CompilerParams(vmem_limit_bytes=VMEM_LIMIT),
        cost_estimate=pl.CostEstimate(
            flops=2 * tokens * width * hidden, transcendentals=0, bytes_accessed=16 * MIB
        ),
        name="layer_output",
    )(x1, z, *blocks)


def per_device(
    n,
    tokens,
    attention_gain,
    query_weight,
    key_weight,
    value_weight,
    output_weight,
    feedforward_gain,
    inner_weight,
    outer_weight,
    bias_table,
    segment_ids,
    positions,
    cotangent,
):
    del positions
    width = tokens.shape[1]
    hidden = inner_weight.shape[1]
    rows = query_weight.shape[0]
    first, second, third = bit_orders(n)
    lay_a = Layout(n, rows, (1536, 3072, 4 * width + LANES), (first, second, third))
    lay_i = Layout(n, rows, (hidden // 2, hidden), (first, second))
    lay_f = Layout(n, outer_weight.shape[0], (width // 2, width), (third, first))
    lay_df = Layout(n, outer_weight.shape[0], (width // 2, width), (first, second))
    lay_di = Layout(n, rows, (hidden // 2, hidden), (third, second))
    lay_do = Layout(n, rows, (width,), (first,))
    lay_da = Layout(n, rows, (width, 2 * width, 3 * width), (first, second, third))

    gains = jnp.pad(jnp.stack([attention_gain, feedforward_gain], axis=1), ((0, 0), (0, LANES - 2)))
    block_a = jnp.concatenate(
        [query_weight, key_weight, value_weight, output_weight, gains], axis=1
    ).astype(BF16)
    sources_a = lay_a.gather(block_a)
    sources_i = lay_i.gather(inner_weight.astype(BF16))
    sources_f = lay_f.gather(outer_weight.astype(BF16))
    lookup = offset_lookup()
    base = jnp.einsum("bkc,ch->hbk", lookup, bias_table, precision=HIGHEST)

    wa, gain, q, k, v, p, h1t, ct, x1, h2, h2t = attention_forward(lay_a, tokens, segment_ids, base, sources_a)
    z, g, *parts_f = inner_forward(lay_i, lay_df, h2, cotangent, sources_i, hidden)
    outer_gradient = lay_df.scatter(parts_f)
    dx1, da, dgain2, *parts = outer_backward(
        lay_i, lay_f, lay_di, lay_do, cotangent, x1, h2t, gain, g, ct, sources_i, sources_f, hidden
    )
    split = len(lay_di.out_shapes())
    inner_gradient = lay_di.scatter(parts[:split])
    output_gradient = lay_do.scatter(parts[split:])
    dq, dk, dv, diagonal, *parts_a = scores_backward(lay_da, da, q, k, v, h1t, wa, p)
    projections = lay_da.scatter(parts_a)
    tokens_gradient, dgain1 = inputs_backward(tokens, dx1, gain, dq, dk, dv, wa)
    table = jnp.einsum("hbk,bkc->ch", diagonal, lookup, precision=HIGHEST)
    small = jnp.concatenate([dgain1[0], dgain2[0], table.reshape(-1)])
    small = sum_all(small, n) if n & (n - 1) == 0 else lax.psum(small, AXIS)
    start = lax.axis_index(AXIS) * rows
    result = layer_output(lay_f, x1, z, sources_f)
    return (
        result,
        tokens_gradient,
        lax.dynamic_slice(small, (start,), (rows,)),
        projections[:, :width],
        projections[:, width : 2 * width],
        projections[:, 2 * width :],
        output_gradient,
        lax.dynamic_slice(small, (width + start,), (rows,)),
        inner_gradient,
        outer_gradient,
        small[2 * width :].reshape(NB, HEADS),
    )


def solution(mesh):
    n = mesh.shape[AXIS]
    matrix, vector = P(AXIS, None), P(AXIS)
    return jax.shard_map(
        functools.partial(per_device, n),
        mesh=mesh,
        in_specs=(
            matrix,
            vector,
            matrix,
            matrix,
            matrix,
            matrix,
            vector,
            matrix,
            matrix,
            P(),
            vector,
            vector,
            matrix,
        ),
        out_specs=(
            matrix,
            matrix,
            vector,
            matrix,
            matrix,
            matrix,
            matrix,
            vector,
            matrix,
            matrix,
            P(),
        ),
        check_vma=False,
    )
```

```python
import functools
import math

import jax
import jax.numpy as jnp
from jax import lax
from jax.experimental import pallas as pl
from jax.experimental.pallas import tpu as pltpu
from jax.sharding import PartitionSpec as P

AXIS = "fsdp"
HEADS = 16
HEAD = 64
NB = 32
SEQ = 256
SPAN = 2 * SEQ
LANES = 128
GROUP = 256
EPSILON = 1e-06
MASKED = -1000000000.0
LIMITS = (12, 16, 23, 32, 46, 64, 91)
HIGHEST = lax.Precision.HIGHEST
BF16 = jnp.bfloat16
F32 = jnp.float32
MIB = 1 << 20
VMEM_LIMIT = 62 * MIB
ORDERS = {
    "a0": ("zZyx", "Zzxy"),
    "a1": ("Zxzy", "xyZz"),
    "i0": ("yZxz", "xZzy"),
    "i1": ("Zzxy", "zxyZ"),
    "f0": ("zZxy", "Zyxz"),
    "g": ("xZzy", "yxZz"),
    "h": ("Zyzx", "zyZx"),
    "j": ("Zzyx", "xZzy"),
    "p": ("Zzyx", "zyxZ"),
    "q": ("zZxy", "Zzyx"),
}
SPLIT = {"a": 67, "i": 67}
SCHEDULE = (
    ("a0", "a1"),
    ("a0", "a1", "i0", "i1"),
    ("a0", "a1", "i0", "i1", "f0"),
    ("a0", "a1"),
    ("a0", "a1", "i0", "i1", "f0"),
    "K1a",
    ("i0", "i1", "f0"),
    "K1b",
    ("i0", "i1", "f0"),
    "K2a",
    ("f0",),
    ("f0", "g"),
    "K2ba",
    ("g", "h"),
    "K2bb",
    ("g", "h", "j"),
    "K3a",
    ("g", "h", "j", "p"),
    "K3b",
    ("g", "h", "j", "p", "q"),
    "K4",
    ("g", "h", "j", "p", "q", "s"),
    "K5",
    ("h", "j", "p", "q", "s"),
    ("j", "p", "q", "s"),
    ("p", "q", "s"),
    ("q", "s"),
)
ANY = pl.BlockSpec(memory_space=pl.ANY)
VM = pl.BlockSpec(memory_space=pltpu.VMEM)


def bucket_of(relative):
    distance = jnp.abs(relative)
    counted = jnp.zeros_like(distance)
    for threshold in LIMITS:
        counted = counted + (distance >= threshold).astype(jnp.int32)
    inside = jnp.where(distance < 8, distance, 8 + counted)
    return inside + jnp.where(relative > 0, 16, 0).astype(jnp.int32)


def offset_lookup():
    k = lax.broadcasted_iota(jnp.int32, (8, SPAN, NB), 1)
    b = lax.broadcasted_iota(jnp.int32, (8, SPAN, NB), 0)
    c = lax.broadcasted_iota(jnp.int32, (8, SPAN, NB), 2)
    offset = k - b
    offset = jnp.where(offset >= SEQ, offset - SPAN, offset)
    return (bucket_of(offset) == c).astype(F32)


def bit_orders(n, rows, wanted):
    if n & (n - 1) or n < 8 or rows % 16:
        return {name: None for name in wanted}
    high = list(range(1, n.bit_length() - 1))
    if n == 32:
        number = {"x": 1, "y": 2, "z": 3, "Z": 4}
        return {name: tuple([number[c] for c in order] + [0] for order in pair) for name, pair in wanted.items()}
    return {name: (high + [0], high[1:] + high[:1] + [0]) for name in wanted}


def swap(array, bits, n):
    return lax.ppermute(array, AXIS, [(i, i ^ (1 << bits[i & 1])) for i in range(n)])


def relative(bits, t):
    return sum(1 << b for k, b in enumerate(bits) if (t >> k) & 1)


def block_row(me, orders, t, n, rows):
    one, two = (relative(order, t) for order in (orders if t < n // 2 else orders[::-1]))
    return pl.multiple_of((me ^ (one + (me & 1) * (two - one))) * rows, rows)


def after(value, *others):
    return lax.optimization_barrier((value, *others))[0] if others else value


def round_kernel(plan, *refs):
    count = sum(len(kinds) for _, kinds in plan)
    inputs, outs = list(refs[:count]), refs[count:]
    for (kind, kinds), out in zip(plan, outs):
        terms = [inputs.pop(0) for _ in kinds]
        if kind == "join":
            half = terms[0].shape[0]
            out[:half] = terms[0][...]
            out[half:] = terms[1][...]
        elif kind == "small" and len(terms) == 4:
            out[...] = (terms[0][...] + terms[1][...]) + (terms[2][...] + terms[3][...])
        else:
            total = terms[0][...].astype(F32)
            for term in terms[1:]:
                total = total + term[...].astype(F32)
            out[...] = total.astype(out.dtype)


def do_round(jobs):
    plan, specs, arrays, shapes, out_specs = [], [], [], [], []
    moved = 0
    for kind, terms, size, index, dtype in jobs:
        if kind == "small":
            specs += [pl.BlockSpec(term.shape, lambda i: (0, 0)) for term in terms]
            shapes.append(jax.ShapeDtypeStruct(terms[0].shape, dtype))
            out_specs.append(specs[-1])
        else:
            rows, cols = terms[0].shape[1] // 2, terms[0].shape[2]
            specs += [pl.BlockSpec((size, rows, cols), lambda i, k=index: (k, i, 0)) for _ in terms]
            made = 2 * size if kind == "join" else size
            shapes.append(jax.ShapeDtypeStruct((made, 2 * rows, cols), dtype))
            out_specs.append(pl.BlockSpec((made, rows, cols), lambda i: (0, i, 0)))
            moved += 2 * (len(terms) + 1) * size * 2 * rows * cols
        plan.append((kind, (0,) * len(terms)))
        arrays += terms
    return pl.pallas_call(
        functools.partial(round_kernel, tuple(plan)),
        grid=(2,),
        out_shape=shapes,
        in_specs=specs,
        out_specs=out_specs,
        compiler_params=pltpu.CompilerParams(vmem_limit_bytes=VMEM_LIMIT),
        cost_estimate=pl.CostEstimate(flops=moved, transcendentals=0, bytes_accessed=moved),
        name="exchange_round",
    )(*arrays)


class Gather:
    def __init__(self, own, orders, n, early):
        self.have, self.orders, self.n, self.last = own[None], orders, n, len(orders[0]) - 1
        self.step, self.parts, self.flights, self.early = 0, None, [self.have], early

    def waits(self):
        return self.flights

    def job(self):
        if 0 < self.step < self.last:
            return "join", [self.have, self.flights[0]], self.have.shape[0], 0, BF16
        return None

    def advance(self, made=None):
        if self.step > self.last:
            self.parts = [self.have, self.far, *self.near, *self.flights]
            return self.flights
        bits = [order[self.step] for order in self.orders]
        core = [order[self.last] for order in self.orders]
        if self.step == self.last:
            self.far, *self.near = self.flights
            self.flights = [swap(self.far, bits, self.n)]
            if not self.near:
                self.flights.insert(0, swap(after(self.have, self.far), bits, self.n))
        else:
            if self.step == 0:
                self.have = self.flights[0]
            else:
                self.have = jnp.concatenate([self.have, self.flights[0]], axis=0) if made is None else made
            self.flights = [swap(self.have, bits, self.n)]
            if self.early and self.step == self.last - 1:
                self.flights.append(swap(self.have, core, self.n))
        self.step += 1
        return [self.far if self.step > self.last else self.have]

    def finish(self):
        while self.parts is None:
            self.advance()
        return self.parts


class Scatter:
    def __init__(self, send, keep, orders, n):
        self.orders, self.n, self.step = orders, n, len(orders[0]) - 1
        self.terms, self.flights, self.result = [keep], [send], None
        self.first = self.step

    def waits(self):
        return self.flights

    def job(self):
        if self.step == self.first:
            return None
        half = 1 << max(self.step, 0)
        return "sum", self.terms + self.flights, half, int(self.step >= 0), BF16 if self.step >= 0 else F32

    def advance(self, made=None):
        send = self.flights[0]
        if self.step < self.first:
            _, terms, half, index, dtype = self.job()
            send = sum(term[half * index : half * (index + 1)].astype(F32) for term in terms) if made is None else made
            self.terms = terms
            if self.step < 0:
                self.result = send[0]
                return [send]
        send = send.astype(BF16)
        self.flights = [swap(send, [order[self.step] for order in self.orders], self.n)]
        self.step -= 1
        return [send]

    def finish(self):
        while self.result is None:
            self.advance()
        return self.result


class SumAll:
    def __init__(self, values, n):
        bits = list(range(n.bit_length() - 1))
        self.masks = [(1 << b,) for b in bits[:-2]] + [tuple(m << bits[-2] for m in (1, 2, 3))]
        self.values, self.n, self.step, self.result, self.flights = values, n, 0, None, [values]

    def waits(self):
        return self.flights

    def job(self):
        return ("small", [self.values, *self.flights], 0, 0, F32) if self.step else None

    def advance(self, made=None):
        if self.step == 0:
            (self.values,) = self.flights
        elif made is None:
            self.values = self.total()
        else:
            self.values = made
        if self.step == len(self.masks):
            self.result = self.values
        else:
            pairs = [[(i, i ^ mask) for i in range(self.n)] for mask in self.masks[self.step]]
            self.flights = [lax.ppermute(self.values, AXIS, pair) for pair in pairs]
        self.step += 1
        return [self.values]

    def total(self):
        if len(self.flights) == 1:
            return self.values + self.flights[0]
        one, two, three = self.flights
        return (self.values + one) + (two + three)

    def finish(self):
        while self.result is None:
            self.advance()
        return self.result


class Layout:
    def __init__(self, n, rows, cuts, orders):
        self.n, self.rows = n, rows
        self.cuts, self.orders = cuts, orders
        self.paired = orders[0] is not None

    def spans(self):
        return tuple(zip((0,) + tuple(self.cuts[:-1]), self.cuts))

    def count(self):
        return 4 * len(self.cuts) if self.paired else 1

    def load(self, me, refs, full, sems, half=None, cols=None):
        size = full.shape[0]
        begin, end = cols or (0, self.cuts[-1])
        if not self.paired:
            first = 0 if half is None else half * size
            copy = pltpu.make_async_copy(refs[0].at[first : first + size, begin:end], full, sems)
            copy.start()
            return copy.wait
        for s, ((lo, hi), orders) in enumerate(zip(self.spans(), self.orders)):
            low, high = max(lo, begin), min(hi, end)
            if low >= high:
                continue
            for t in range(self.n):
                ref = refs[4 * s + t // (self.n // 4)].at[t % (self.n // 4), :, low - lo : high - lo]
                row = block_row(me, orders, t, self.n, self.rows)

                def start(row, ref=ref, low=low, high=high):
                    target = full.at[pl.ds(row, self.rows), low - begin : high - begin]
                    pltpu.make_async_copy(ref, target, sems).start()

                if half is None:
                    start(row)
                else:
                    row = pl.multiple_of(row - half * size, self.rows)
                    pl.when(jnp.logical_and(row >= 0, row < size))(functools.partial(start, row))
        return pltpu.make_async_copy(full, full, sems).wait

    def out_shapes(self):
        if not self.paired:
            return [jax.ShapeDtypeStruct((self.n * self.rows, self.cuts[-1]), BF16)]
        return [jax.ShapeDtypeStruct((self.n // 2, self.rows, self.cuts[-1]), BF16)] * 2

    def store(self, me, stage, refs, sem, cols=None):
        begin, end = cols or (0, self.cuts[-1])
        if not self.paired:
            copy = pltpu.make_async_copy(stage.at[:, begin:end], refs[0].at[:, begin:end], sem)
            copy.start()
            return copy.wait
        half = self.n // 2
        for t in [*range(half, self.n), *range(half)]:
            row = block_row(me, self.orders[0], t, self.n, self.rows)
            target = refs[0 if t >= half else 1].at[t % half, :, begin:end]
            pltpu.make_async_copy(stage.at[pl.ds(row, self.rows), begin:end], target, sem).start()
        view = stage.at[:, begin:end]
        return pltpu.make_async_copy(view, view, sem).wait


def dot(a, b):
    return lax.dot_general(a, b, (((1,), (0,)), ((), ())), preferred_element_type=F32)


def dot_nt(a, b):
    return lax.dot_general(a, b, (((1,), (1,)), ((), ())), preferred_element_type=F32)


def dot_tn(a, b):
    return lax.dot_general(a, b, (((0,), (0,)), ((), ())), preferred_element_type=F32)


def row_scale(values):
    return lax.rsqrt(jnp.mean(values * values, axis=-1, keepdims=True) + EPSILON)


def toeplitz(base):
    return jnp.concatenate(
        [(pltpu.roll(base, 8 * a, 1) if a else base)[:, :SEQ] for a in range(SEQ // 8)], axis=0
    )


def diagonals(scores):
    total = None
    for a in range(SEQ // 8):
        rows = scores[8 * a : 8 * a + 8]
        rows = jnp.concatenate([rows, jnp.zeros((8, SPAN - SEQ), F32)], axis=1)
        if a:
            rows = pltpu.roll(rows, SPAN - 8 * a, 1)
        total = rows if total is None else total + rows
    return total


def transposed(values):
    return values.T


def copy_out(copies, sems, k, source, target):
    copy = pltpu.make_async_copy(source, target, sems.at[k])
    copy.start()
    copies.append(copy)


def pack_kernel(spans, *refs):
    q_ref, k_ref, v_ref, o_ref, one_ref, two_ref = refs[:6]
    rows, width = q_ref.shape
    line = lax.broadcasted_iota(jnp.int32, (LANES, rows), 0)
    gains = jnp.where(line == 0, one_ref[...], jnp.where(line == 1, two_ref[...], 0.0)).T
    for (low, high), out in zip(spans, refs[6:]):
        for k, ref in enumerate((q_ref, k_ref, v_ref, o_ref, gains)):
            begin, end = max(low, k * width), min(high, k * width + ref.shape[1])
            if begin < end:
                out[:, begin - low : end - low] = ref[:, begin - k * width : end - k * width].astype(BF16)


def pack(lay, weights, gains):
    rows = weights[0].shape[0]
    return pl.pallas_call(
        functools.partial(pack_kernel, lay.spans()),
        out_shape=[jax.ShapeDtypeStruct((rows, high - low), BF16) for low, high in lay.spans()],
        in_specs=[VM] * 6,
        out_specs=[VM] * len(lay.cuts),
        name="pack",
    )(*weights, *(gain.reshape(1, rows) for gain in gains))


def attend(seqs, h1, weights, segments_ref, base_ref, q_ref, k_ref, v_ref, p_ref, c_ref, ct_ref):
    for ref, weight in zip((q_ref, k_ref, v_ref), weights):
        ref[...] = dot(h1, weight).astype(BF16)
    first = lax.broadcasted_iota(jnp.int32, (SEQ, LANES), 1) < HEAD
    for p in range(GROUP // LANES):
        lanes = slice(p * LANES, (p + 1) * LANES)
        biases = [toeplitz(base_ref[2 * p + o]) for o in range(2)]
        for s in range(seqs):
            rows = slice(s * SEQ, (s + 1) * SEQ)
            q2, k2, v2 = q_ref[rows, lanes], k_ref[rows, lanes], v_ref[rows, lanes]
            line = jnp.broadcast_to(segments_ref[s : s + 1, :], (SEQ, SEQ))
            allowed = line.T == line
            made = []
            for o in range(2):
                mine = jnp.where(first == (o == 0), q2, jnp.zeros_like(q2))
                scores = jnp.where(allowed, dot_nt(mine, k2) + biases[o], MASKED)
                exponent = jnp.exp(scores - jnp.max(scores, axis=-1, keepdims=True))
                prob = exponent * (1.0 / jnp.sum(exponent, axis=-1, keepdims=True))
                p_ref[s, 2 * p + o] = prob
                made.append(dot(prob.astype(BF16), v2))
            c_ref[rows, lanes] = jnp.where(first, made[0], made[1]).astype(BF16)
    ct_ref[...] = transposed(c_ref[...])


def early_kernel(lay, seqs, width, steps, *refs):
    m = lay.count()
    x_ref, segments_ref, base_ref = refs[:3]
    blocks = refs[3 : 3 + m]
    wa_out, gain_ref, h1_ref, h1t_ref = refs[3 + m : 7 + m]
    outs = refs[7 + m : 13 + m]
    wa, sems = refs[13 + m :]
    step = pl.program_id(0)

    @pl.when(step == 0)
    def _():
        lay.load(lax.axis_index(AXIS), blocks, wa, sems.at[0])()
        pltpu.make_async_copy(wa, wa_out, sems.at[0]).start()
        gains = wa[:, 4 * width : 4 * width + LANES].astype(F32).T
        gain_ref[...] = gains[:8]
        x = x_ref[...].astype(F32)
        h1 = (x * row_scale(x) * gains[0:1]).astype(BF16)
        h1_ref[...] = h1
        h1t_ref[...] = transposed(h1)

    weights = [wa[:, pl.ds(pl.multiple_of(j * width + step * GROUP, GROUP), GROUP)] for j in range(3)]
    attend(seqs, h1_ref[...], weights, segments_ref, base_ref, *outs)

    @pl.when(step == steps - 1)
    def _():
        pltpu.make_async_copy(wa, wa_out, sems.at[0]).wait()


def late_kernel(seqs, steps, *refs):
    h1_ref, wq_ref, wk_ref, wv_ref, segments_ref, base_ref, x_ref, gain_ref, context_ref, wo_ref = refs[:10]
    outs, (x1_ref, h2_ref, h2t_ref, context) = refs[10:16], refs[16:]
    attend(seqs, h1_ref[...], (wq_ref[...], wk_ref[...], wv_ref[...]), segments_ref, base_ref, *outs)
    step = pl.program_id(0)
    context[:, pl.ds(pl.multiple_of(step * GROUP, GROUP), GROUP)] = outs[4][...]

    @pl.when(step == steps - 1)
    def _():
        width = x_ref.shape[1]
        early = context_ref.shape[1]
        for c in range(0, width, 512):
            cols = slice(c, c + 512)
            x1_ref[:, cols] = (
                x_ref[:, cols].astype(F32)
                + dot(context_ref[...], wo_ref[:early, cols])
                + dot(context[...], wo_ref[early:, cols])
            )
        x1 = x1_ref[...]
        h2 = (x1 * row_scale(x1) * gain_ref[1:2, :]).astype(BF16)
        h2_ref[...] = h2
        h2t_ref[...] = transposed(h2)


def attention_outputs(tokens, width, count):
    sds = jax.ShapeDtypeStruct
    seqs, heads = tokens // SEQ, GROUP // HEAD
    shapes = [sds((tokens, count * GROUP), BF16)] * 3
    specs = [pl.BlockSpec((tokens, GROUP), lambda i: (0, i))] * 3
    shapes.append(sds((seqs, count * heads, SEQ, SEQ), F32))
    specs.append(pl.BlockSpec((seqs, heads, SEQ, SEQ), lambda i: (0, i, 0, 0)))
    shapes.append(sds((tokens, count * GROUP), BF16))
    specs.append(pl.BlockSpec((tokens, GROUP), lambda i: (0, i)))
    shapes.append(sds((count * GROUP, tokens), BF16))
    specs.append(pl.BlockSpec((GROUP, tokens), lambda i: (i, 0)))
    return shapes, specs


def whole(shape):
    return pl.BlockSpec(shape, lambda i: (0,) * len(shape))


def attention_cost(tokens, width, count):
    share = count * GROUP
    return pl.CostEstimate(
        flops=2 * tokens * width * 3 * share + 16 * tokens * SEQ * share,
        transcendentals=tokens * SEQ * share // HEAD,
        bytes_accessed=(6 * width * share + 8 * tokens * share + 4 * tokens * SEQ * share // HEAD),
    )


def attention_early(lay, x, segments, base, blocks, count):
    tokens, width = x.shape
    seqs, wide, heads = tokens // SEQ, lay.cuts[-1], GROUP // HEAD
    sds = jax.ShapeDtypeStruct
    shapes, specs = attention_outputs(tokens, width, count)
    return pl.pallas_call(
        functools.partial(early_kernel, lay, seqs, width, count),
        grid=(count,),
        out_shape=[sds((width, wide), BF16), sds((8, width), F32), sds((tokens, width), BF16), sds((width, tokens), BF16)]
        + shapes,
        in_specs=[
            whole((tokens, width)),
            whole((seqs, SEQ)),
            pl.BlockSpec((heads, 8, SPAN), lambda i: (i, 0, 0)),
        ]
        + [ANY] * len(blocks),
        out_specs=[ANY, whole((8, width)), whole((tokens, width)), whole((width, tokens))] + specs,
        scratch_shapes=[pltpu.VMEM((width, wide), BF16), pltpu.SemaphoreType.DMA((4,))],
        compiler_params=pltpu.CompilerParams(vmem_limit_bytes=VMEM_LIMIT),
        cost_estimate=attention_cost(tokens, width, count),
        name="attention_early",
    )(x, segments.reshape(seqs, SEQ), base, *blocks)


def attention_late(h1, wa, segments, base, count, x, gain, context):
    tokens, width = h1.shape
    seqs, heads, skip = tokens // SEQ, GROUP // HEAD, width // GROUP - count
    shapes, specs = attention_outputs(tokens, width, count)
    per = width // GROUP
    sds = jax.ShapeDtypeStruct
    return pl.pallas_call(
        functools.partial(late_kernel, seqs, count),
        grid=(count,),
        out_shape=shapes + [sds((tokens, width), F32), sds((tokens, width), BF16), sds((width, tokens), BF16)],
        in_specs=[whole((tokens, width))]
        + [pl.BlockSpec((width, GROUP), lambda i, j=j: (0, j * per + skip + i)) for j in range(3)]
        + [
            whole((seqs, SEQ)),
            pl.BlockSpec((heads, 8, SPAN), lambda i: (skip + i, 0, 0)),
            whole((tokens, width)),
            whole((8, width)),
            whole(context.shape),
            pl.BlockSpec((width, width), lambda i: (0, 3)),
        ],
        out_specs=specs + [whole((tokens, width)), whole((tokens, width)), whole((width, tokens))],
        scratch_shapes=[pltpu.VMEM((tokens, count * GROUP), BF16)],
        compiler_params=pltpu.CompilerParams(vmem_limit_bytes=VMEM_LIMIT),
        cost_estimate=attention_cost(tokens, width, count),
        name="attention_late",
    )(h1, wa, wa, wa, segments.reshape(seqs, SEQ), base, x, gain, context, wa)


def inner_kernel(lay, lay_out, chunk, *refs):
    m, k = lay.count(), len(lay_out.out_shapes())
    h2_ref, e_ref = refs[:2]
    blocks = refs[2 : 2 + m]
    z_out, g_out = refs[2 + m : 4 + m]
    grads = refs[4 + m : 4 + m + k]
    wi, z_s, g_s, stage, lsem, osem, gsem = refs[4 + m + k :]
    me = lax.axis_index(AXIS)
    hidden = wi.shape[1]
    parts = 4
    size = hidden // parts
    waits = [
        lay.load(me, blocks, wi.at[:, p * size : (p + 1) * size], lsem.at[p], cols=(p * size, (p + 1) * size))
        for p in range(parts)
    ]

    def step(c, carry):
        cols = pl.ds(pl.multiple_of(c * chunk, chunk), chunk)
        u = dot(h2_ref[...], wi[:, cols])
        cdf = 0.5 * (1.0 + lax.erf(u * (1.0 / math.sqrt(2.0))))
        z = (u * cdf).astype(BF16)
        z_s[:, cols] = z
        g_s[:, cols] = cdf + u * jnp.exp(-0.5 * u * u) * (1.0 / math.sqrt(2.0 * math.pi))
        stage[cols, :] = dot(transposed(z), e_ref[...]).astype(BF16)
        pltpu.make_async_copy(z_s.at[:, cols], z_out.at[:, cols], osem.at[0]).start()
        pltpu.make_async_copy(g_s.at[:, cols], g_out.at[:, cols], osem.at[1]).start()
        return carry

    for p in range(parts):
        waits[p]()
        lax.fori_loop(p * size // chunk, (p + 1) * size // chunk, step, 0)
    done = lay_out.store(me, stage, grads, gsem)
    pltpu.make_async_copy(z_s, z_out, osem.at[0]).wait()
    pltpu.make_async_copy(g_s, g_out, osem.at[1]).wait()
    done()


def inner_forward(lay, lay_out, h2, cotangent, blocks, hidden):
    tokens, width = h2.shape
    sds = jax.ShapeDtypeStruct
    grads = lay_out.out_shapes()
    return pl.pallas_call(
        functools.partial(inner_kernel, lay, lay_out, 512),
        out_shape=[sds((tokens, hidden), BF16), sds((tokens, hidden), F32)] + grads,
        in_specs=[VM] * 2 + [ANY] * len(blocks),
        out_specs=[ANY] * (2 + len(grads)),
        scratch_shapes=[
            pltpu.VMEM((width, hidden), BF16),
            pltpu.VMEM((tokens, hidden), BF16),
            pltpu.VMEM((tokens, hidden), F32),
            pltpu.VMEM((hidden, width), BF16),
            pltpu.SemaphoreType.DMA((4,)),
            pltpu.SemaphoreType.DMA((2,)),
            pltpu.SemaphoreType.DMA,
        ],
        compiler_params=pltpu.CompilerParams(vmem_limit_bytes=VMEM_LIMIT),
        cost_estimate=pl.CostEstimate(
            flops=4 * tokens * width * hidden, transcendentals=2 * tokens * hidden, bytes_accessed=32 * MIB
        ),
        name="feedforward_inner",
    )(h2, cotangent, *blocks)


def outer_kernel(lay_i, lay_f, lay_g, chunk, half, *refs):
    last = half == 1
    mi, mf = lay_i.count(), lay_f.count()
    e_ref, h2t_ref, g_in = refs[:3]
    at = 3
    if last:
        x1_ref, gain_ref, dh_ref = refs[3:6]
        contexts = refs[6:8]
        at = 8
    inner, outer = refs[at : at + mi], refs[at + mi : at + mi + mf]
    at += mi + mf
    dx1_ref, at = refs[at], at + 1
    if last:
        da_ref, dgain_ref = refs[at : at + 2]
        at += 2
    kg = len(lay_g.out_shapes())
    grads, at = refs[at : at + kg], at + kg
    wi, wf, g_s, stage, lsem, isem, gsem = refs[at:]
    me = lax.axis_index(AXIS)
    size = wi.shape[1]
    waits = [lay_f.load(me, outer, wf, lsem.at[0], half=half)]
    waits.append(lay_i.load(me, inner, wi, lsem.at[1], cols=(half * size, (half + 1) * size)))
    steps = size // chunk
    copies = []
    for c in range(steps):
        source = g_in.at[:, half * size + c * chunk : half * size + (c + 1) * chunk]
        copies.append(pltpu.make_async_copy(source, g_s.at[:, c * chunk : (c + 1) * chunk], isem.at[c]))
        copies[-1].start()
    for wait in waits:
        wait()
    e = e_ref[...]
    for c in range(steps):
        cols = slice(c * chunk, (c + 1) * chunk)
        copies[c].wait()
        du = (dot_nt(e, wf[cols, :]) * g_s[:, cols]).astype(BF16)
        stage[:, cols] = dot(h2t_ref[...], du).astype(BF16)
        part = dot_nt(du, wi[:, cols])
        if c == 0:
            dx1_ref[...] = part + dh_ref[...] if last else part
        else:
            dx1_ref[...] += part
    if last:
        dh2 = dx1_ref[...]
        x1 = x1_ref[...]
        gain = gain_ref[1:2, :]
        scale = row_scale(x1)
        dgain_ref[...] = jnp.broadcast_to(jnp.sum(dh2 * (x1 * scale), axis=0, keepdims=True), dgain_ref.shape)
        mean = jnp.mean(x1 * gain * dh2, axis=-1, keepdims=True)
        dx1 = e.astype(F32) + scale * gain * dh2 - x1 * (scale * scale * scale) * mean
        dx1_ref[...] = dx1
        da = dx1.astype(BF16)
        da_ref[...] = da
        rows = stage.shape[0] // 2
        for p, context in enumerate(contexts):
            stage[p * rows : (p + 1) * rows, size:] = dot(context[...], da).astype(BF16)
    lay_g.store(me, stage, grads, gsem)()


def outer_backward(lay_i, lay_f, lay_g, half, cotangent, h2t, g, inner, outer, more=()):
    tokens, width = cotangent.shape
    size = g.shape[1] // 2
    chunk = 512
    last = half == 1
    sds = jax.ShapeDtypeStruct
    out_shape = [sds((tokens, width), F32)]
    out_specs = [VM]
    if last:
        out_shape += [sds((tokens, width), BF16), sds((8, width), F32)]
        out_specs += [VM] * 2
    grads = lay_g.out_shapes()
    return pl.pallas_call(
        functools.partial(outer_kernel, lay_i, lay_f, lay_g, chunk, half),
        out_shape=out_shape + grads,
        in_specs=[VM, VM, ANY] + [VM] * len(more) + [ANY] * (len(inner) + len(outer)),
        out_specs=out_specs + [ANY] * len(grads),
        scratch_shapes=[
            pltpu.VMEM((width, size), BF16),
            pltpu.VMEM((size, width), BF16),
            pltpu.VMEM((tokens, size), F32),
            pltpu.VMEM((width, lay_g.cuts[-1]), BF16),
            pltpu.SemaphoreType.DMA((2,)),
            pltpu.SemaphoreType.DMA((size // chunk,)),
            pltpu.SemaphoreType.DMA,
        ],
        compiler_params=pltpu.CompilerParams(vmem_limit_bytes=VMEM_LIMIT),
        cost_estimate=pl.CostEstimate(
            flops=6 * tokens * width * size + 2 * last * tokens * width * width,
            transcendentals=tokens,
            bytes_accessed=24 * MIB,
        ),
        name="feedforward_outer_" + "ab"[half],
    )(cotangent, h2t, g, *more, *inner, *outer)


def scores_kernel(lay, seqs, width, steps, *refs):
    k = len(lay.out_shapes())
    da_ref, wo_ref, q_ref, k_ref, v_ref, p_ref, h1t_ref = refs[:7]
    dq_ref, dk_ref, dv_ref, table_ref = refs[7:11]
    grads = refs[11 : 11 + k]
    dc, stage, gsem = refs[11 + k :]
    step = pl.program_id(0)
    dc[...] = dot_nt(da_ref[...], wo_ref[...]).astype(BF16)
    first = lax.broadcasted_iota(jnp.int32, (SEQ, LANES), 1) < HEAD
    for p in range(GROUP // LANES):
        lanes = slice(p * LANES, (p + 1) * LANES)
        totals = [None, None]
        for s in range(seqs):
            rows = slice(s * SEQ, (s + 1) * SEQ)
            dc2, q2, k2, v2 = dc[rows, lanes], q_ref[rows, lanes], k_ref[rows, lanes], v_ref[rows, lanes]
            made = []
            for o in range(2):
                prob = p_ref[s, 2 * p + o]
                mine = jnp.where(first == (o == 0), dc2, jnp.zeros_like(dc2))
                dprob = dot_nt(mine, v2)
                inner = jnp.sum(prob * dprob, axis=-1, keepdims=True)
                ds = (prob * (dprob - inner)).astype(BF16)
                wide = ds.astype(F32)
                totals[o] = wide if totals[o] is None else totals[o] + wide
                made.append(
                    (dot(ds, k2), dot(transposed(ds), q2), dot(transposed(prob.astype(BF16)), dc2))
                )
            for ref, one, two in zip((dq_ref, dk_ref, dv_ref), *made):
                ref[rows, lanes] = jnp.where(first, one, two).astype(BF16)
        for o in range(2):
            table_ref[2 * p + o] = diagonals(totals[o])
    for j, ref in enumerate((dq_ref, dk_ref, dv_ref)):
        col = pl.ds(pl.multiple_of((3 * step + j) * GROUP, GROUP), GROUP)
        stage[:, col] = dot(h1t_ref[...], ref[...]).astype(BF16)

    @pl.when(step == steps - 1)
    def _():
        lay.store(lax.axis_index(AXIS), stage, grads, gsem)()


def scores_backward(lay, part, da, wa, q, k, v, p, h1t):
    tokens, width = da.shape
    count = q.shape[1] // GROUP
    seqs, heads = tokens // SEQ, GROUP // HEAD
    sds = jax.ShapeDtypeStruct
    grads = lay.out_shapes()
    share = count * GROUP
    return pl.pallas_call(
        functools.partial(scores_kernel, lay, seqs, width, count),
        grid=(count,),
        out_shape=[sds((tokens, share), BF16)] * 3 + [sds((count * heads, 8, SPAN), F32)] + grads,
        in_specs=[whole((tokens, width)), pl.BlockSpec((GROUP, width), lambda i: (part * count + i, 3))]
        + [pl.BlockSpec((tokens, GROUP), lambda i: (0, i))] * 3
        + [pl.BlockSpec((seqs, heads, SEQ, SEQ), lambda i: (0, i, 0, 0)), whole((width, tokens))],
        out_specs=[pl.BlockSpec((tokens, GROUP), lambda i: (0, i))] * 3
        + [pl.BlockSpec((heads, 8, SPAN), lambda i: (i, 0, 0))]
        + [ANY] * len(grads),
        scratch_shapes=[
            pltpu.VMEM((tokens, GROUP), BF16),
            pltpu.VMEM((width, 3 * share), BF16),
            pltpu.SemaphoreType.DMA,
        ],
        compiler_params=pltpu.CompilerParams(vmem_limit_bytes=VMEM_LIMIT),
        cost_estimate=pl.CostEstimate(
            flops=8 * tokens * width * share + 40 * tokens * SEQ * share,
            transcendentals=0,
            bytes_accessed=16 * MIB,
        ),
        name="attention_backward_" + "ab"[part],
    )(da, wa, q, k, v, p, h1t)


def inputs_kernel(width, parts, *refs):
    x_ref, dx1_ref, gain_ref = refs[:3]
    grads = refs[3 : 3 + 3 * parts]
    wa_in, dx_ref, dgain_ref, wa, dh, sem = refs[3 + 3 * parts :]
    copies = []
    for j in range(3):
        cols = slice(j * width, (j + 1) * width)
        copies.append(pltpu.make_async_copy(wa_in.at[:, cols], wa.at[:, cols], sem.at[j]))
        copies[-1].start()
    size = width // parts
    for j in range(3):
        copies[j].wait()
        for c in range(0, width, 512):
            for p in range(parts):
                low = j * width + p * size
                part = dot_nt(grads[3 * p + j][...], wa[c : c + 512, low : low + size])
                if j or p:
                    dh[:, c : c + 512] += part
                else:
                    dh[:, c : c + 512] = part
    x = x_ref[...].astype(F32)
    gain = gain_ref[0:1, :]
    scale = row_scale(x)
    dh1 = dh[...]
    dgain_ref[...] = jnp.broadcast_to(jnp.sum(dh1 * (x * scale), axis=0, keepdims=True), dgain_ref.shape)
    mean = jnp.mean(x * gain * dh1, axis=-1, keepdims=True)
    dx_ref[...] = (dx1_ref[...] + scale * gain * dh1 - x * (scale * scale * scale) * mean).astype(BF16)


def inputs_backward(x, dx1, gain, grads, wa):
    tokens, width = x.shape
    sds = jax.ShapeDtypeStruct
    return pl.pallas_call(
        functools.partial(inputs_kernel, width, len(grads) // 3),
        out_shape=[sds((tokens, width), BF16), sds((8, width), F32)],
        in_specs=[VM] * (3 + len(grads)) + [ANY],
        out_specs=[VM] * 2,
        scratch_shapes=[
            pltpu.VMEM((width, 3 * width), BF16),
            pltpu.VMEM((tokens, width), F32),
            pltpu.SemaphoreType.DMA((3,)),
        ],
        compiler_params=pltpu.CompilerParams(vmem_limit_bytes=VMEM_LIMIT),
        cost_estimate=pl.CostEstimate(
            flops=6 * tokens * width * width, transcendentals=tokens, bytes_accessed=16 * MIB
        ),
        name="inputs_backward",
    )(x, dx1, gain, *grads, wa)


def output_kernel(lay, *refs):
    m = lay.count()
    x1_ref, z_ref = refs[:2]
    blocks = refs[2 : 2 + m]
    out_ref, wf, sem = refs[2 + m :]
    lay.load(lax.axis_index(AXIS), blocks, wf, sem)()
    width = wf.shape[1]
    for c in range(0, width, 512):
        cols = slice(c, c + 512)
        out_ref[:, cols] = (x1_ref[:, cols] + dot(z_ref[...], wf[:, cols])).astype(BF16)


def layer_output(lay, x1, z, blocks):
    tokens, width = x1.shape
    hidden = z.shape[1]
    return pl.pallas_call(
        functools.partial(output_kernel, lay),
        out_shape=jax.ShapeDtypeStruct((tokens, width), BF16),
        in_specs=[VM] * 2 + [ANY] * len(blocks),
        out_specs=VM,
        scratch_shapes=[
            pltpu.VMEM((hidden, width), BF16),
            pltpu.SemaphoreType.DMA,
        ],
        compiler_params=pltpu.CompilerParams(vmem_limit_bytes=VMEM_LIMIT),
        cost_estimate=pl.CostEstimate(
            flops=2 * tokens * width * hidden, transcendentals=0, bytes_accessed=16 * MIB
        ),
        name="layer_output",
    )(x1, z, *blocks)


def per_device(
    n,
    tokens,
    attention_gain,
    query_weight,
    key_weight,
    value_weight,
    output_weight,
    feedforward_gain,
    inner_weight,
    outer_weight,
    bias_table,
    segment_ids,
    positions,
    cotangent,
):
    del positions
    width = tokens.shape[1]
    hidden = inner_weight.shape[1]
    rows = query_weight.shape[0]
    orders = bit_orders(n, rows, ORDERS)
    wide = outer_weight.shape[0]
    count = width // GROUP // 2
    half = hidden // 2
    all_a = 4 * width + LANES
    def split(columns, name):
        pairs = tuple(orders[key] for key in ORDERS if key[:-1] == name)
        if len(pairs) < 2 or pairs[0] is None:
            return (columns,), pairs[:1]
        return (SPLIT[name] * columns // LANES // 100 * LANES, columns), pairs

    lay_a = Layout(n, rows, *split(all_a, "a"))
    lay_i = Layout(n, rows, *split(hidden, "i"))
    lay_f = Layout(n, wide, *split(width, "f"))
    lay = {
        "g": Layout(n, wide, (width,), (orders["g"],)),
        "h": Layout(n, rows, (half,), (orders["h"],)),
        "j": Layout(n, rows, (half + width,), (orders["j"],)),
        "p": Layout(n, rows, (3 * width // 2,), (orders["p"],)),
        "q": Layout(n, rows, (3 * width // 2,), (orders["q"],)),
    }
    chains, v, state = {}, {}, {"last": []}
    weights = (query_weight, key_weight, value_weight, output_weight)
    packed = pack(lay_a, weights, (attention_gain, feedforward_gain))
    blocks = {
        "a": packed,
        "i": [inner_weight[:, low:high].astype(BF16) for low, high in lay_i.spans()],
        "f": [outer_weight[:, low:high].astype(BF16) for low, high in lay_f.spans()],
    }
    for name, layout in (("a", lay_a), ("i", lay_i), ("f", lay_f)):
        for k, (block, pair) in enumerate(zip(blocks[name], layout.orders)):
            if layout.paired:
                chains[name + str(k)] = Gather(block, pair, n, name != "a")
            else:
                v[name + str(k)] = lax.all_gather(block, AXIS, axis=0, tiled=True)
    lookup = offset_lookup()
    base = jnp.einsum("bkc,ch->hbk", lookup, bias_table, precision=HIGHEST)
    state["base"] = [base]

    def gathered(name, layout):
        if not layout.paired:
            return [v[name + "0"]]
        found = []
        for k in range(len(layout.cuts)):
            found += chains[name + str(k)].finish()
        return found

    def tied(value):
        return after(value, *state["last"])

    def scatter(name, parts):
        if lay[name].paired:
            chains[name] = Scatter(*parts, lay[name].orders[0], n)
        else:
            v[name] = lax.psum_scatter(parts[0].astype(F32), AXIS, scatter_dimension=0, tiled=True)

    def run(name):
        if name == "K1a":
            out = attention_early(lay_a, tied(tokens), segment_ids, base, gathered("a", lay_a), count)
            v["wa"], v["gain"], v["h1"], v["h1t"], *v["early"] = out
            return [out[8]]
        if name == "K1b":
            out = attention_late(
                tied(v["h1"]), v["wa"], segment_ids, base, count, tokens, v["gain"], v["early"][4]
            )
            v["late"], (v["x1"], v["h2"], v["h2t"]) = out[:6], out[6:]
            return [v["h2"]]
        if name == "K2a":
            out = inner_forward(lay_i, lay["g"], tied(v["h2"]), cotangent, gathered("i", lay_i), hidden)
            v["z"], v["slope"], *parts = out
            scatter("g", parts)
            return parts[:1]
        if name == "K2ba":
            out = outer_backward(
                lay_i, lay_f, lay["h"], 0, tied(cotangent), v["h2t"], v["slope"], gathered("i", lay_i), gathered("f", lay_f)
            )
            v["dh2"], *parts = out
            scatter("h", parts)
            return parts[:1]
        if name == "K2bb":
            more = (v["x1"], v["gain"], tied(v["dh2"]), v["early"][5], v["late"][5])
            out = outer_backward(
                lay_i, lay_f, lay["j"], 1, cotangent, v["h2t"], v["slope"], gathered("i", lay_i), gathered("f", lay_f), more
            )
            v["dx1"], v["da"], v["dgain2"], *parts = out
            scatter("j", parts)
            return parts[:1]
        if name in ("K3a", "K3b"):
            part, saved = (0, v["early"]) if name == "K3a" else (1, v["late"])
            target = "pq"[part]
            out = scores_backward(lay[target], part, tied(v["da"]), v["wa"], *saved[:4], v["h1t"])
            v["grads" + target], v["table" + target], parts = out[:3], out[3], out[4:]
            scatter(target, parts)
            return parts[:1]
        if name == "K4":
            grads = (*v["gradsp"], *v["gradsq"])
            v["dx"], dgain1 = inputs_backward(tokens, tied(v["dx1"]), v["gain"], grads, v["wa"])
            diagonal = jnp.concatenate([v["tablep"], v["tableq"]], axis=0)
            table = jnp.einsum("hbk,bkc->ch", diagonal, lookup, precision=HIGHEST)
            small = jnp.concatenate([dgain1[0], v["dgain2"][0], table.reshape(-1)]).reshape(-1, LANES)
            if n & (n - 1):
                v["s"] = lax.psum(small, AXIS)
            else:
                chains["s"] = SumAll(small, n)
            return [v["dx"]]
        v["out"] = layer_output(lay_f, v["x1"], tied(v["z"]), gathered("f", lay_f))
        return [v["out"]]

    def exchange(names):
        active = [chains[name] for name in names if name in chains]
        if not active:
            return []
        arrived = [flight for chain in active for flight in chain.waits()]
        arrived = list(lax.optimization_barrier((*arrived, *state["last"])))
        for chain in active:
            chain.flights = [arrived.pop(0) for _ in chain.waits()]
        jobs = [chain.job() for chain in active]
        wanted = [job for job in jobs if job]
        made = list(do_round(wanted)) if len(wanted) >= 3 else []
        sent = []
        for chain, job in zip(active, jobs):
            sent += chain.advance(made.pop(0) if job and made else None)
        return sent

    for names in SCHEDULE:
        if isinstance(names, str):
            state["last"] = run(names)
        else:
            state["last"] = list(exchange(names) or state["last"]) + state.pop("base", [])

    def total(name):
        if name not in chains:
            return v[name]
        return chains[name].finish()

    small = total("s").reshape(-1)
    start = lax.axis_index(AXIS) * rows
    joined = jnp.concatenate([total("p"), total("q")], axis=1)

    def projection(j):
        groups = range(j * GROUP, 3 * width, 3 * GROUP)
        return jnp.concatenate([joined[:, low : low + GROUP] for low in groups], axis=1)

    return (
        v["out"],
        v["dx"],
        lax.dynamic_slice(small, (start,), (rows,)),
        projection(0),
        projection(1),
        projection(2),
        total("j")[:, half:],
        lax.dynamic_slice(small, (width + start,), (rows,)),
        jnp.concatenate([total("h"), total("j")[:, :half]], axis=1),
        total("g"),
        small[2 * width :].reshape(NB, HEADS),
    )


def solution(mesh):
    n = mesh.shape[AXIS]
    matrix, vector = P(AXIS, None), P(AXIS)
    return jax.shard_map(
        functools.partial(per_device, n),
        mesh=mesh,
        in_specs=(
            matrix,
            vector,
            matrix,
            matrix,
            matrix,
            matrix,
            vector,
            matrix,
            matrix,
            P(),
            vector,
            vector,
            matrix,
        ),
        out_specs=(
            matrix,
            matrix,
            vector,
            matrix,
            matrix,
            matrix,
            matrix,
            vector,
            matrix,
            matrix,
            P(),
        ),
        check_vma=False,
    )
```

```python
import functools
import math

import jax
import jax.numpy as jnp
from jax import lax
from jax.experimental import pallas as pl
from jax.experimental.pallas import tpu as pltpu
from jax.sharding import PartitionSpec as P

AXIS = "fsdp"
HEADS = 16
HEAD = 64
NB = 32
SEQ = 256
SPAN = 2 * SEQ
LANES = 128
GROUP = 256
EPSILON = 1e-06
MASKED = -1000000000.0
LIMITS = (12, 16, 23, 32, 46, 64, 91)
HIGHEST = lax.Precision.HIGHEST
BF16 = jnp.bfloat16
F32 = jnp.float32
MIB = 1 << 20
VMEM_LIMIT = 62 * MIB
ORDERS = {
    "a0": ("zZyx", "Zzxy"),
    "a1": ("Zxzy", "xyZz"),
    "i0": ("yZxz", "xZzy"),
    "i1": ("Zzxy", "zxyZ"),
    "f0": ("zZxy", "Zyxz"),
    "g": ("xZzy", "yZxz"),
    "h": ("Zxzy", "Zxzy"),
    "j": ("zZyx", "Zzxy"),
    "p": ("Zxyz", "zyxZ"),
    "q": ("zZyx", "Zzxy"),
}
SPLIT = {"a": 67, "i": 67}
SCHEDULE = (
    ("a0", "a1"),
    ("a0", "a1", "i0", "i1"),
    ("a0", "a1", "i0", "i1", "f0"),
    ("a0", "a1"),
    ("a0", "a1", "i0", "i1", "f0"),
    "K1a",
    ("i0", "i1", "f0"),
    "K1b",
    ("i0", "i1", "f0"),
    "K2a",
    ("f0",),
    ("f0", "g"),
    "K2ba",
    ("g", "h"),
    "K2bb",
    ("g", "h", "j"),
    "K3a",
    ("g", "h", "j", "p"),
    "K3b",
    ("g", "h", "j", "p", "q"),
    "K4",
    ("g", "h", "j", "p", "q", "s"),
    "K5",
    ("h", "j", "p", "q", "s"),
    ("j", "p", "q", "s"),
    ("p", "q", "s"),
    ("q", "s"),
)
ANY = pl.BlockSpec(memory_space=pl.ANY)
VM = pl.BlockSpec(memory_space=pltpu.VMEM)


def bucket_of(relative):
    distance = jnp.abs(relative)
    counted = jnp.zeros_like(distance)
    for threshold in LIMITS:
        counted = counted + (distance >= threshold).astype(jnp.int32)
    inside = jnp.where(distance < 8, distance, 8 + counted)
    return inside + jnp.where(relative > 0, 16, 0).astype(jnp.int32)


def offset_lookup():
    k = lax.broadcasted_iota(jnp.int32, (8, SPAN, NB), 1)
    b = lax.broadcasted_iota(jnp.int32, (8, SPAN, NB), 0)
    c = lax.broadcasted_iota(jnp.int32, (8, SPAN, NB), 2)
    offset = k - b
    offset = jnp.where(offset >= SEQ, offset - SPAN, offset)
    return (bucket_of(offset) == c).astype(F32)


def bit_orders(n, rows, wanted):
    if n & (n - 1) or n < 8 or rows % 16:
        return {name: None for name in wanted}
    high = list(range(1, n.bit_length() - 1))
    if n == 32:
        number = {"x": 1, "y": 2, "z": 3, "Z": 4}
        return {name: tuple([number[c] for c in order] + [0] for order in pair) for name, pair in wanted.items()}
    return {name: (high + [0], high[1:] + high[:1] + [0]) for name in wanted}


def swap(array, bits, n):
    return lax.ppermute(array, AXIS, [(i, i ^ (1 << bits[i & 1])) for i in range(n)])


def relative(bits, t):
    return sum(1 << b for k, b in enumerate(bits) if (t >> k) & 1)


def block_row(me, orders, t, n, rows):
    one, two = (relative(order, t) for order in (orders if t < n // 2 else orders[::-1]))
    return pl.multiple_of((me ^ (one + (me & 1) * (two - one))) * rows, rows)


def after(value, *others):
    return lax.optimization_barrier((value, *others))[0] if others else value


def round_kernel(plan, *refs):
    count = sum(len(kinds) for _, kinds in plan)
    inputs, outs = list(refs[:count]), refs[count:]
    for (kind, kinds), out in zip(plan, outs):
        terms = [inputs.pop(0) for _ in kinds]
        if kind == "join":
            half = terms[0].shape[0]
            out[:half] = terms[0][...]
            out[half:] = terms[1][...]
        elif kind == "small" and len(terms) == 4:
            out[...] = (terms[0][...] + terms[1][...]) + (terms[2][...] + terms[3][...])
        else:
            total = terms[0][...].astype(F32)
            for term in terms[1:]:
                total = total + term[...].astype(F32)
            out[...] = total.astype(out.dtype)


def do_round(jobs):
    plan, specs, arrays, shapes, out_specs = [], [], [], [], []
    moved = 0
    for kind, terms, size, index, dtype in jobs:
        if kind == "small":
            specs += [pl.BlockSpec(term.shape, lambda i: (0, 0)) for term in terms]
            shapes.append(jax.ShapeDtypeStruct(terms[0].shape, dtype))
            out_specs.append(specs[-1])
        else:
            rows, cols = terms[0].shape[1] // 2, terms[0].shape[2]
            specs += [pl.BlockSpec((size, rows, cols), lambda i, k=index: (k, i, 0)) for _ in terms]
            made = 2 * size if kind == "join" else size
            shapes.append(jax.ShapeDtypeStruct((made, 2 * rows, cols), dtype))
            out_specs.append(pl.BlockSpec((made, rows, cols), lambda i: (0, i, 0)))
            moved += 2 * (len(terms) + 1) * size * 2 * rows * cols
        plan.append((kind, (0,) * len(terms)))
        arrays += terms
    return pl.pallas_call(
        functools.partial(round_kernel, tuple(plan)),
        grid=(2,),
        out_shape=shapes,
        in_specs=specs,
        out_specs=out_specs,
        compiler_params=pltpu.CompilerParams(vmem_limit_bytes=VMEM_LIMIT),
        cost_estimate=pl.CostEstimate(flops=moved, transcendentals=0, bytes_accessed=moved),
        name="exchange_round",
    )(*arrays)


class Gather:
    def __init__(self, own, orders, n, early):
        self.have, self.orders, self.n, self.last = own[None], orders, n, len(orders[0]) - 1
        self.step, self.parts, self.flights, self.early = 0, None, [self.have], early

    def waits(self):
        return self.flights

    def job(self):
        if 0 < self.step < self.last:
            return "join", [self.have, self.flights[0]], self.have.shape[0], 0, BF16
        return None

    def advance(self, made=None):
        if self.step > self.last:
            self.parts = [self.have, self.far, *self.near, *self.flights]
            return self.flights
        bits = [order[self.step] for order in self.orders]
        core = [order[self.last] for order in self.orders]
        if self.step == self.last:
            self.far, *self.near = self.flights
            self.flights = [swap(self.far, bits, self.n)]
            if not self.near:
                self.flights.insert(0, swap(after(self.have, self.far), bits, self.n))
        else:
            if self.step == 0:
                self.have = self.flights[0]
            else:
                self.have = jnp.concatenate([self.have, self.flights[0]], axis=0) if made is None else made
            self.flights = [swap(self.have, bits, self.n)]
            if self.early and self.step == self.last - 1:
                self.flights.append(swap(self.have, core, self.n))
        self.step += 1
        return [self.far if self.step > self.last else self.have]

    def finish(self):
        while self.parts is None:
            self.advance()
        return self.parts


class Scatter:
    def __init__(self, send, keep, orders, n):
        self.orders, self.n, self.step = orders, n, len(orders[0]) - 1
        self.terms, self.flights, self.result = [keep], [send], None
        self.first = self.step

    def waits(self):
        return self.flights

    def job(self):
        if self.step == self.first:
            return None
        half = 1 << max(self.step, 0)
        return "sum", self.terms + self.flights, half, int(self.step >= 0), BF16 if self.step >= 0 else F32

    def advance(self, made=None):
        send = self.flights[0]
        if self.step < self.first:
            _, terms, half, index, dtype = self.job()
            send = sum(term[half * index : half * (index + 1)].astype(F32) for term in terms) if made is None else made
            self.terms = terms
            if self.step < 0:
                self.result = send[0]
                return [send]
        send = send.astype(BF16)
        self.flights = [swap(send, [order[self.step] for order in self.orders], self.n)]
        self.step -= 1
        return [send]

    def finish(self):
        while self.result is None:
            self.advance()
        return self.result


class SumAll:
    def __init__(self, values, n):
        bits = list(range(n.bit_length() - 1))
        self.masks = [(1 << b,) for b in bits[:-2]] + [tuple(m << bits[-2] for m in (1, 2, 3))]
        self.values, self.n, self.step, self.result, self.flights = values, n, 0, None, [values]

    def waits(self):
        return self.flights

    def job(self):
        return ("small", [self.values, *self.flights], 0, 0, F32) if self.step else None

    def advance(self, made=None):
        if self.step == 0:
            (self.values,) = self.flights
        elif made is None:
            self.values = self.total()
        else:
            self.values = made
        if self.step == len(self.masks):
            self.result = self.values
        else:
            pairs = [[(i, i ^ mask) for i in range(self.n)] for mask in self.masks[self.step]]
            self.flights = [lax.ppermute(self.values, AXIS, pair) for pair in pairs]
        self.step += 1
        return [self.values]

    def total(self):
        if len(self.flights) == 1:
            return self.values + self.flights[0]
        one, two, three = self.flights
        return (self.values + one) + (two + three)

    def finish(self):
        while self.result is None:
            self.advance()
        return self.result


class Layout:
    def __init__(self, n, rows, cuts, orders):
        self.n, self.rows = n, rows
        self.cuts, self.orders = cuts, orders
        self.paired = orders[0] is not None

    def spans(self):
        return tuple(zip((0,) + tuple(self.cuts[:-1]), self.cuts))

    def count(self):
        return 4 * len(self.cuts) if self.paired else 1

    def load(self, me, refs, full, sems, first=0, cols=None, chunk=None):
        size = full.shape[0]
        begin, end = cols or (0, self.cuts[-1])
        chunk = chunk or size
        if not self.paired:
            waits = []
            for c in range(size // chunk):
                source = refs[0].at[first + c * chunk : first + (c + 1) * chunk, begin:end]
                copy = pltpu.make_async_copy(source, full.at[c * chunk : (c + 1) * chunk], sems.at[c])
                copy.start()
                waits.append(copy.wait)
            return waits
        whole_rows = size == self.n * self.rows
        for s, ((lo, hi), orders) in enumerate(zip(self.spans(), self.orders)):
            low, high = max(lo, begin), min(hi, end)
            if low >= high:
                continue
            for t in range(self.n):
                ref = refs[4 * s + t // (self.n // 4)].at[t % (self.n // 4), :, low - lo : high - lo]
                row = block_row(me, orders, t, self.n, self.rows)

                def start(row, ref=ref, low=low, high=high):
                    target = full.at[pl.ds(row, self.rows), low - begin : high - begin]
                    sem = sems.at[0 if chunk == size else lax.div(row, chunk)]
                    pltpu.make_async_copy(ref, target, sem).start()

                if whole_rows:
                    start(row)
                else:
                    row = pl.multiple_of(row - first, self.rows)
                    pl.when(jnp.logical_and(row >= 0, row < size))(functools.partial(start, row))
        def wait(c):
            view = full.at[c * chunk : (c + 1) * chunk]
            pltpu.make_async_copy(view, view, sems.at[c]).wait()

        return [functools.partial(wait, c) for c in range(size // chunk)]

    def out_shapes(self):
        if not self.paired:
            return [jax.ShapeDtypeStruct((self.n * self.rows, self.cuts[-1]), BF16)]
        return [jax.ShapeDtypeStruct((self.n // 2, self.rows, self.cuts[-1]), BF16)] * 2

    def store(self, me, stage, refs, sem, cols=None):
        begin, end = cols or (0, self.cuts[-1])
        if not self.paired:
            copy = pltpu.make_async_copy(stage.at[:, begin:end], refs[0].at[:, begin:end], sem)
            copy.start()
            return copy.wait
        half = self.n // 2
        for t in [*range(half, self.n), *range(half)]:
            row = block_row(me, self.orders[0], t, self.n, self.rows)
            target = refs[0 if t >= half else 1].at[t % half, :, begin:end]
            pltpu.make_async_copy(stage.at[pl.ds(row, self.rows), begin:end], target, sem).start()
        view = stage.at[:, begin:end]
        return pltpu.make_async_copy(view, view, sem).wait


def dot(a, b):
    return lax.dot_general(a, b, (((1,), (0,)), ((), ())), preferred_element_type=F32)


def dot_nt(a, b):
    return lax.dot_general(a, b, (((1,), (1,)), ((), ())), preferred_element_type=F32)


def dot_tn(a, b):
    return lax.dot_general(a, b, (((0,), (0,)), ((), ())), preferred_element_type=F32)


def row_scale(values):
    return lax.rsqrt(jnp.mean(values * values, axis=-1, keepdims=True) + EPSILON)


def toeplitz(base):
    return jnp.concatenate(
        [(pltpu.roll(base, 8 * a, 1) if a else base)[:, :SEQ] for a in range(SEQ // 8)], axis=0
    )


def diagonals(scores):
    total = None
    for a in range(SEQ // 8):
        rows = scores[8 * a : 8 * a + 8]
        rows = jnp.concatenate([rows, jnp.zeros((8, SPAN - SEQ), F32)], axis=1)
        if a:
            rows = pltpu.roll(rows, SPAN - 8 * a, 1)
        total = rows if total is None else total + rows
    return total


def transposed(values):
    return values.T


def copy_out(copies, sems, k, source, target):
    copy = pltpu.make_async_copy(source, target, sems.at[k])
    copy.start()
    copies.append(copy)


def pack_kernel(spans, *refs):
    q_ref, k_ref, v_ref, o_ref, one_ref, two_ref = refs[:6]
    rows, width = q_ref.shape
    line = lax.broadcasted_iota(jnp.int32, (LANES, rows), 0)
    gains = jnp.where(line == 0, one_ref[...], jnp.where(line == 1, two_ref[...], 0.0)).T
    for (low, high), out in zip(spans, refs[6:]):
        for k, ref in enumerate((q_ref, k_ref, v_ref, o_ref, gains)):
            begin, end = max(low, k * width), min(high, k * width + ref.shape[1])
            if begin < end:
                out[:, begin - low : end - low] = ref[:, begin - k * width : end - k * width].astype(BF16)


def pack(lay, weights, gains):
    rows = weights[0].shape[0]
    return pl.pallas_call(
        functools.partial(pack_kernel, lay.spans()),
        out_shape=[jax.ShapeDtypeStruct((rows, high - low), BF16) for low, high in lay.spans()],
        in_specs=[VM] * 6,
        out_specs=[VM] * len(lay.cuts),
        name="pack",
    )(*weights, *(gain.reshape(1, rows) for gain in gains))


def attend(seqs, h1, weights, segments_ref, base_ref, q_ref, k_ref, v_ref, p_ref, c_ref, ct_ref):
    for ref, weight in zip((q_ref, k_ref, v_ref), weights):
        ref[...] = dot(h1, weight).astype(BF16)
    first = lax.broadcasted_iota(jnp.int32, (SEQ, LANES), 1) < HEAD
    for p in range(GROUP // LANES):
        lanes = slice(p * LANES, (p + 1) * LANES)
        biases = [toeplitz(base_ref[2 * p + o]) for o in range(2)]
        for s in range(seqs):
            rows = slice(s * SEQ, (s + 1) * SEQ)
            q2, k2, v2 = q_ref[rows, lanes], k_ref[rows, lanes], v_ref[rows, lanes]
            line = jnp.broadcast_to(segments_ref[s : s + 1, :], (SEQ, SEQ))
            allowed = line.T == line
            made = []
            for o in range(2):
                mine = jnp.where(first == (o == 0), q2, jnp.zeros_like(q2))
                scores = jnp.where(allowed, dot_nt(mine, k2) + biases[o], MASKED)
                exponent = jnp.exp(scores - jnp.max(scores, axis=-1, keepdims=True))
                prob = exponent * (1.0 / jnp.sum(exponent, axis=-1, keepdims=True))
                p_ref[s, 2 * p + o] = prob
                made.append(dot(prob.astype(BF16), v2))
            c_ref[rows, lanes] = jnp.where(first, made[0], made[1]).astype(BF16)
    ct_ref[...] = transposed(c_ref[...])


def early_kernel(lay, seqs, width, steps, *refs):
    m = lay.count()
    x_ref, segments_ref, base_ref = refs[:3]
    blocks = refs[3 : 3 + m]
    wa_out, gain_ref, h1_ref, h1t_ref = refs[3 + m : 7 + m]
    outs = refs[7 + m : 13 + m]
    wa, gains_s, sems = refs[13 + m :]
    step = pl.program_id(0)

    @pl.when(step == 0)
    def _():
        me = lax.axis_index(AXIS)
        waits = lay.load(me, blocks, gains_s, sems.at[0:1], cols=(4 * width, 4 * width + LANES))
        for j in range(3):
            cols = (j * width, (j + 1) * width)
            waits += lay.load(me, blocks, wa.at[:, j * width : (j + 1) * width], sems.at[1 + j : 2 + j], cols=cols)
        waits[0]()
        gains = gains_s[...].astype(F32).T
        gain_ref[...] = gains[:8]
        x = x_ref[...].astype(F32)
        h1 = (x * row_scale(x) * gains[0:1]).astype(BF16)
        h1_ref[...] = h1
        h1t_ref[...] = transposed(h1)
        for wait in waits[1:]:
            wait()
        pltpu.make_async_copy(wa, wa_out, sems.at[0]).start()

    weights = [wa[:, pl.ds(pl.multiple_of(j * width + step * GROUP, GROUP), GROUP)] for j in range(3)]
    attend(seqs, h1_ref[...], weights, segments_ref, base_ref, *outs)

    @pl.when(step == steps - 1)
    def _():
        pltpu.make_async_copy(wa, wa_out, sems.at[0]).wait()


def late_kernel(lay, seqs, steps, *refs):
    m = lay.count()
    h1_ref, wq_ref, wk_ref, wv_ref, segments_ref, base_ref, x_ref, gain_ref, context_ref = refs[:9]
    blocks = refs[9 : 9 + m]
    outs, (x1_ref, h2_ref, h2t_ref, wo_out) = refs[9 + m : 15 + m], refs[15 + m : 19 + m]
    context, wo_ref, sems = refs[19 + m :]
    step = pl.program_id(0)
    width = x_ref.shape[1]

    @pl.when(step == 0)
    def _():
        lay.load(lax.axis_index(AXIS), blocks, wo_ref, sems.at[0:1], cols=(3 * width, 4 * width))

    attend(seqs, h1_ref[...], (wq_ref[...], wk_ref[...], wv_ref[...]), segments_ref, base_ref, *outs)
    context[:, pl.ds(pl.multiple_of(step * GROUP, GROUP), GROUP)] = outs[4][...]

    @pl.when(step == steps - 1)
    def _():
        pltpu.make_async_copy(wo_ref, wo_ref, sems.at[0]).wait()
        copy = pltpu.make_async_copy(wo_ref, wo_out, sems.at[1])
        copy.start()
        early = context_ref.shape[1]
        for c in range(0, width, 512):
            cols = slice(c, c + 512)
            x1_ref[:, cols] = (
                x_ref[:, cols].astype(F32)
                + dot(context_ref[...], wo_ref[:early, cols])
                + dot(context[...], wo_ref[early:, cols])
            )
        x1 = x1_ref[...]
        h2 = (x1 * row_scale(x1) * gain_ref[1:2, :]).astype(BF16)
        h2_ref[...] = h2
        h2t_ref[...] = transposed(h2)
        copy.wait()


def attention_outputs(tokens, width, count):
    sds = jax.ShapeDtypeStruct
    seqs, heads = tokens // SEQ, GROUP // HEAD
    shapes = [sds((tokens, count * GROUP), BF16)] * 3
    specs = [pl.BlockSpec((tokens, GROUP), lambda i: (0, i))] * 3
    shapes.append(sds((seqs, count * heads, SEQ, SEQ), F32))
    specs.append(pl.BlockSpec((seqs, heads, SEQ, SEQ), lambda i: (0, i, 0, 0)))
    shapes.append(sds((tokens, count * GROUP), BF16))
    specs.append(pl.BlockSpec((tokens, GROUP), lambda i: (0, i)))
    shapes.append(sds((count * GROUP, tokens), BF16))
    specs.append(pl.BlockSpec((GROUP, tokens), lambda i: (i, 0)))
    return shapes, specs


def whole(shape):
    return pl.BlockSpec(shape, lambda i: (0,) * len(shape))


def attention_cost(tokens, width, count):
    share = count * GROUP
    return pl.CostEstimate(
        flops=2 * tokens * width * 3 * share + 16 * tokens * SEQ * share,
        transcendentals=tokens * SEQ * share // HEAD,
        bytes_accessed=(6 * width * share + 8 * tokens * share + 4 * tokens * SEQ * share // HEAD),
    )


def attention_early(lay, x, segments, base, blocks, count):
    tokens, width = x.shape
    seqs, wide, heads = tokens // SEQ, 3 * width, GROUP // HEAD
    sds = jax.ShapeDtypeStruct
    shapes, specs = attention_outputs(tokens, width, count)
    return pl.pallas_call(
        functools.partial(early_kernel, lay, seqs, width, count),
        grid=(count,),
        out_shape=[sds((width, wide), BF16), sds((8, width), F32), sds((tokens, width), BF16), sds((width, tokens), BF16)]
        + shapes,
        in_specs=[
            whole((tokens, width)),
            whole((seqs, SEQ)),
            pl.BlockSpec((heads, 8, SPAN), lambda i: (i, 0, 0)),
        ]
        + [ANY] * len(blocks),
        out_specs=[ANY, whole((8, width)), whole((tokens, width)), whole((width, tokens))] + specs,
        scratch_shapes=[
            pltpu.VMEM((width, wide), BF16),
            pltpu.VMEM((width, LANES), BF16),
            pltpu.SemaphoreType.DMA((4,)),
        ],
        compiler_params=pltpu.CompilerParams(vmem_limit_bytes=VMEM_LIMIT),
        cost_estimate=attention_cost(tokens, width, count),
        name="attention_early",
    )(x, segments.reshape(seqs, SEQ), base, *blocks)


def attention_late(lay, h1, wa, segments, base, count, x, gain, context, blocks):
    tokens, width = h1.shape
    seqs, heads, skip = tokens // SEQ, GROUP // HEAD, width // GROUP - count
    shapes, specs = attention_outputs(tokens, width, count)
    per = width // GROUP
    sds = jax.ShapeDtypeStruct
    return pl.pallas_call(
        functools.partial(late_kernel, lay, seqs, count),
        grid=(count,),
        out_shape=shapes
        + [sds((tokens, width), F32), sds((tokens, width), BF16), sds((width, tokens), BF16), sds((width, width), BF16)],
        in_specs=[whole((tokens, width))]
        + [pl.BlockSpec((width, GROUP), lambda i, j=j: (0, j * per + skip + i)) for j in range(3)]
        + [
            whole((seqs, SEQ)),
            pl.BlockSpec((heads, 8, SPAN), lambda i: (skip + i, 0, 0)),
            whole((tokens, width)),
            whole((8, width)),
            whole(context.shape),
        ]
        + [ANY] * len(blocks),
        out_specs=specs + [whole((tokens, width)), whole((tokens, width)), whole((width, tokens)), ANY],
        scratch_shapes=[
            pltpu.VMEM((tokens, count * GROUP), BF16),
            pltpu.VMEM((width, width), BF16),
            pltpu.SemaphoreType.DMA((2,)),
        ],
        compiler_params=pltpu.CompilerParams(vmem_limit_bytes=VMEM_LIMIT),
        cost_estimate=attention_cost(tokens, width, count),
        name="attention_late",
    )(h1, wa, wa, wa, segments.reshape(seqs, SEQ), base, x, gain, context, *blocks)


def inner_kernel(lay, lay_out, chunk, *refs):
    m, k = lay.count(), len(lay_out.out_shapes())
    h2_ref, e_ref = refs[:2]
    blocks = refs[2 : 2 + m]
    z_out, g_out = refs[2 + m : 4 + m]
    grads = refs[4 + m : 4 + m + k]
    wi, z_s, g_s, stage, lsem, osem, gsem = refs[4 + m + k :]
    me = lax.axis_index(AXIS)
    hidden = wi.shape[1]
    parts = 4
    size = hidden // parts
    waits = []
    for p in range(parts):
        cols = (p * size, (p + 1) * size)
        waits += lay.load(me, blocks, wi.at[:, p * size : (p + 1) * size], lsem.at[p : p + 1], cols=cols)

    def step(c, carry):
        cols = pl.ds(pl.multiple_of(c * chunk, chunk), chunk)
        u = dot(h2_ref[...], wi[:, cols])
        cdf = 0.5 * (1.0 + lax.erf(u * (1.0 / math.sqrt(2.0))))
        z = (u * cdf).astype(BF16)
        z_s[:, cols] = z
        g_s[:, cols] = cdf + u * jnp.exp(-0.5 * u * u) * (1.0 / math.sqrt(2.0 * math.pi))
        stage[cols, :] = dot(transposed(z), e_ref[...]).astype(BF16)
        pltpu.make_async_copy(z_s.at[:, cols], z_out.at[:, cols], osem.at[0]).start()
        pltpu.make_async_copy(g_s.at[:, cols], g_out.at[:, cols], osem.at[1]).start()
        return carry

    for p in range(parts):
        waits[p]()
        lax.fori_loop(p * size // chunk, (p + 1) * size // chunk, step, 0)
    done = lay_out.store(me, stage, grads, gsem)
    pltpu.make_async_copy(z_s, z_out, osem.at[0]).wait()
    pltpu.make_async_copy(g_s, g_out, osem.at[1]).wait()
    done()


def inner_forward(lay, lay_out, h2, cotangent, blocks, hidden):
    tokens, width = h2.shape
    sds = jax.ShapeDtypeStruct
    grads = lay_out.out_shapes()
    return pl.pallas_call(
        functools.partial(inner_kernel, lay, lay_out, 512),
        out_shape=[sds((tokens, hidden), BF16), sds((tokens, hidden), F32)] + grads,
        in_specs=[VM] * 2 + [ANY] * len(blocks),
        out_specs=[ANY] * (2 + len(grads)),
        scratch_shapes=[
            pltpu.VMEM((width, hidden), BF16),
            pltpu.VMEM((tokens, hidden), BF16),
            pltpu.VMEM((tokens, hidden), F32),
            pltpu.VMEM((hidden, width), BF16),
            pltpu.SemaphoreType.DMA((4,)),
            pltpu.SemaphoreType.DMA((2,)),
            pltpu.SemaphoreType.DMA,
        ],
        compiler_params=pltpu.CompilerParams(vmem_limit_bytes=VMEM_LIMIT),
        cost_estimate=pl.CostEstimate(
            flops=4 * tokens * width * hidden, transcendentals=2 * tokens * hidden, bytes_accessed=32 * MIB
        ),
        name="feedforward_inner",
    )(h2, cotangent, *blocks)


def outer_kernel(lay_i, lay_f, lay_g, chunk, first, last, *refs):
    mi, mf = lay_i.count(), lay_f.count()
    e_ref, h2t_ref, g_in = refs[:3]
    at = 3
    if last:
        x1_ref, gain_ref, dh_ref = refs[3:6]
        contexts = refs[6:8]
        at = 8
    inner, outer = refs[at : at + mi], refs[at + mi : at + mi + mf]
    at += mi + mf
    dx1_ref, at = refs[at], at + 1
    if last:
        da_ref, dgain_ref = refs[at : at + 2]
        at += 2
    kg = len(lay_g.out_shapes())
    grads, at = refs[at : at + kg], at + kg
    wi, wf, g_s, stage, fsem, lsem, isem, gsem = refs[at:]
    me = lax.axis_index(AXIS)
    size = wi.shape[1]
    steps = size // chunk
    outer_waits = lay_f.load(me, outer, wf, fsem, first=first, chunk=chunk)
    copies, inner_waits = [], []
    for c in range(steps):
        source = g_in.at[:, first + c * chunk : first + (c + 1) * chunk]
        copies.append(pltpu.make_async_copy(source, g_s.at[:, c * chunk : (c + 1) * chunk], isem.at[c]))
        copies[-1].start()
    wide = 2 * chunk
    for c in range(size // wide):
        target = wi.at[:, c * wide : (c + 1) * wide]
        cols = (first + c * wide, first + (c + 1) * wide)
        inner_waits += lay_i.load(me, inner, target, lsem.at[c : c + 1], cols=cols)
    e = e_ref[...]
    for c in range(steps):
        cols = slice(c * chunk, (c + 1) * chunk)
        outer_waits[c]()
        copies[c].wait()
        du = (dot_nt(e, wf[cols, :]) * g_s[:, cols]).astype(BF16)
        stage[:, cols] = dot(h2t_ref[...], du).astype(BF16)
        if c % 2 == 0:
            inner_waits[c // 2]()
        part = dot_nt(du, wi[:, cols])
        if c == 0:
            dx1_ref[...] = part + dh_ref[...] if last else part
        else:
            dx1_ref[...] += part
    if last:
        dh2 = dx1_ref[...]
        x1 = x1_ref[...]
        gain = gain_ref[1:2, :]
        scale = row_scale(x1)
        dgain_ref[...] = jnp.broadcast_to(jnp.sum(dh2 * (x1 * scale), axis=0, keepdims=True), dgain_ref.shape)
        mean = jnp.mean(x1 * gain * dh2, axis=-1, keepdims=True)
        dx1 = e.astype(F32) + scale * gain * dh2 - x1 * (scale * scale * scale) * mean
        dx1_ref[...] = dx1
        da = dx1.astype(BF16)
        da_ref[...] = da
        rows = stage.shape[0] // 2
        for p, context in enumerate(contexts):
            stage[p * rows : (p + 1) * rows, size:] = dot(context[...], da).astype(BF16)
    lay_g.store(me, stage, grads, gsem)()


def outer_backward(lay_i, lay_f, lay_g, first, size, cotangent, h2t, g, inner, outer, more=()):
    tokens, width = cotangent.shape
    chunk = 512
    last = first > 0
    sds = jax.ShapeDtypeStruct
    out_shape = [sds((tokens, width), F32)]
    out_specs = [VM]
    if last:
        out_shape += [sds((tokens, width), BF16), sds((8, width), F32)]
        out_specs += [VM] * 2
    grads = lay_g.out_shapes()
    return pl.pallas_call(
        functools.partial(outer_kernel, lay_i, lay_f, lay_g, chunk, first, last),
        out_shape=out_shape + grads,
        in_specs=[VM, VM, ANY] + [VM] * len(more) + [ANY] * (len(inner) + len(outer)),
        out_specs=out_specs + [ANY] * len(grads),
        scratch_shapes=[
            pltpu.VMEM((width, size), BF16),
            pltpu.VMEM((size, width), BF16),
            pltpu.VMEM((tokens, size), F32),
            pltpu.VMEM((width, lay_g.cuts[-1]), BF16),
            pltpu.SemaphoreType.DMA((size // chunk,)),
            pltpu.SemaphoreType.DMA((size // chunk // 2,)),
            pltpu.SemaphoreType.DMA((size // chunk,)),
            pltpu.SemaphoreType.DMA,
        ],
        compiler_params=pltpu.CompilerParams(vmem_limit_bytes=VMEM_LIMIT),
        cost_estimate=pl.CostEstimate(
            flops=6 * tokens * width * size + 2 * last * tokens * width * width,
            transcendentals=tokens,
            bytes_accessed=24 * MIB,
        ),
        name="feedforward_outer_" + "ab"[last],
    )(cotangent, h2t, g, *more, *inner, *outer)


def scores_kernel(lay, seqs, width, steps, *refs):
    k = len(lay.out_shapes())
    da_ref, wo_ref, q_ref, k_ref, v_ref, p_ref, h1t_ref = refs[:7]
    dq_ref, dk_ref, dv_ref, table_ref = refs[7:11]
    grads = refs[11 : 11 + k]
    dc, stage, gsem = refs[11 + k :]
    step = pl.program_id(0)
    dc[...] = dot_nt(da_ref[...], wo_ref[...]).astype(BF16)
    first = lax.broadcasted_iota(jnp.int32, (SEQ, LANES), 1) < HEAD
    for p in range(GROUP // LANES):
        lanes = slice(p * LANES, (p + 1) * LANES)
        totals = [None, None]
        for s in range(seqs):
            rows = slice(s * SEQ, (s + 1) * SEQ)
            dc2, q2, k2, v2 = dc[rows, lanes], q_ref[rows, lanes], k_ref[rows, lanes], v_ref[rows, lanes]
            made = []
            for o in range(2):
                prob = p_ref[s, 2 * p + o]
                mine = jnp.where(first == (o == 0), dc2, jnp.zeros_like(dc2))
                dprob = dot_nt(mine, v2)
                inner = jnp.sum(prob * dprob, axis=-1, keepdims=True)
                ds = (prob * (dprob - inner)).astype(BF16)
                wide = ds.astype(F32)
                totals[o] = wide if totals[o] is None else totals[o] + wide
                made.append(
                    (dot(ds, k2), dot(transposed(ds), q2), dot(transposed(prob.astype(BF16)), dc2))
                )
            for ref, one, two in zip((dq_ref, dk_ref, dv_ref), *made):
                ref[rows, lanes] = jnp.where(first, one, two).astype(BF16)
        for o in range(2):
            table_ref[2 * p + o] = diagonals(totals[o])
    for j, ref in enumerate((dq_ref, dk_ref, dv_ref)):
        col = pl.ds(pl.multiple_of((3 * step + j) * GROUP, GROUP), GROUP)
        stage[:, col] = dot(h1t_ref[...], ref[...]).astype(BF16)

    @pl.when(step == steps - 1)
    def _():
        lay.store(lax.axis_index(AXIS), stage, grads, gsem)()


def scores_backward(lay, part, da, wo, q, k, v, p, h1t):
    tokens, width = da.shape
    count = q.shape[1] // GROUP
    seqs, heads = tokens // SEQ, GROUP // HEAD
    sds = jax.ShapeDtypeStruct
    grads = lay.out_shapes()
    share = count * GROUP
    return pl.pallas_call(
        functools.partial(scores_kernel, lay, seqs, width, count),
        grid=(count,),
        out_shape=[sds((tokens, share), BF16)] * 3 + [sds((count * heads, 8, SPAN), F32)] + grads,
        in_specs=[whole((tokens, width)), pl.BlockSpec((GROUP, width), lambda i: (part * count + i, 0))]
        + [pl.BlockSpec((tokens, GROUP), lambda i: (0, i))] * 3
        + [pl.BlockSpec((seqs, heads, SEQ, SEQ), lambda i: (0, i, 0, 0)), whole((width, tokens))],
        out_specs=[pl.BlockSpec((tokens, GROUP), lambda i: (0, i))] * 3
        + [pl.BlockSpec((heads, 8, SPAN), lambda i: (i, 0, 0))]
        + [ANY] * len(grads),
        scratch_shapes=[
            pltpu.VMEM((tokens, GROUP), BF16),
            pltpu.VMEM((width, 3 * share), BF16),
            pltpu.SemaphoreType.DMA,
        ],
        compiler_params=pltpu.CompilerParams(vmem_limit_bytes=VMEM_LIMIT),
        cost_estimate=pl.CostEstimate(
            flops=8 * tokens * width * share + 40 * tokens * SEQ * share,
            transcendentals=0,
            bytes_accessed=16 * MIB,
        ),
        name="attention_backward_" + "ab"[part],
    )(da, wo, q, k, v, p, h1t)


def inputs_kernel(width, parts, *refs):
    x_ref, dx1_ref, gain_ref = refs[:3]
    grads = refs[3 : 3 + 3 * parts]
    wa_in, dx_ref, dgain_ref, wa, dh, sem = refs[3 + 3 * parts :]
    copies = []
    for j in range(3):
        cols = slice(j * width, (j + 1) * width)
        copies.append(pltpu.make_async_copy(wa_in.at[:, cols], wa.at[:, cols], sem.at[j]))
        copies[-1].start()
    size = width // parts
    for j in range(3):
        copies[j].wait()
        for c in range(0, width, 512):
            for p in range(parts):
                low = j * width + p * size
                part = dot_nt(grads[3 * p + j][...], wa[c : c + 512, low : low + size])
                if j or p:
                    dh[:, c : c + 512] += part
                else:
                    dh[:, c : c + 512] = part
    x = x_ref[...].astype(F32)
    gain = gain_ref[0:1, :]
    scale = row_scale(x)
    dh1 = dh[...]
    dgain_ref[...] = jnp.broadcast_to(jnp.sum(dh1 * (x * scale), axis=0, keepdims=True), dgain_ref.shape)
    mean = jnp.mean(x * gain * dh1, axis=-1, keepdims=True)
    dx_ref[...] = (dx1_ref[...] + scale * gain * dh1 - x * (scale * scale * scale) * mean).astype(BF16)


def inputs_backward(x, dx1, gain, grads, wa):
    tokens, width = x.shape
    sds = jax.ShapeDtypeStruct
    return pl.pallas_call(
        functools.partial(inputs_kernel, width, len(grads) // 3),
        out_shape=[sds((tokens, width), BF16), sds((8, width), F32)],
        in_specs=[VM] * (3 + len(grads)) + [ANY],
        out_specs=[VM] * 2,
        scratch_shapes=[
            pltpu.VMEM((width, 3 * width), BF16),
            pltpu.VMEM((tokens, width), F32),
            pltpu.SemaphoreType.DMA((3,)),
        ],
        compiler_params=pltpu.CompilerParams(vmem_limit_bytes=VMEM_LIMIT),
        cost_estimate=pl.CostEstimate(
            flops=6 * tokens * width * width, transcendentals=tokens, bytes_accessed=16 * MIB
        ),
        name="inputs_backward",
    )(x, dx1, gain, *grads, wa)


def output_kernel(lay, *refs):
    m = lay.count()
    x1_ref, z_ref = refs[:2]
    blocks = refs[2 : 2 + m]
    out_ref, wf, sem = refs[2 + m :]
    lay.load(lax.axis_index(AXIS), blocks, wf, sem)[0]()
    width = wf.shape[1]
    for c in range(0, width, 512):
        cols = slice(c, c + 512)
        out_ref[:, cols] = (x1_ref[:, cols] + dot(z_ref[...], wf[:, cols])).astype(BF16)


def layer_output(lay, x1, z, blocks):
    tokens, width = x1.shape
    hidden = z.shape[1]
    return pl.pallas_call(
        functools.partial(output_kernel, lay),
        out_shape=jax.ShapeDtypeStruct((tokens, width), BF16),
        in_specs=[VM] * 2 + [ANY] * len(blocks),
        out_specs=VM,
        scratch_shapes=[
            pltpu.VMEM((hidden, width), BF16),
            pltpu.SemaphoreType.DMA((1,)),
        ],
        compiler_params=pltpu.CompilerParams(vmem_limit_bytes=VMEM_LIMIT),
        cost_estimate=pl.CostEstimate(
            flops=2 * tokens * width * hidden, transcendentals=0, bytes_accessed=16 * MIB
        ),
        name="layer_output",
    )(x1, z, *blocks)


def per_device(
    n,
    tokens,
    attention_gain,
    query_weight,
    key_weight,
    value_weight,
    output_weight,
    feedforward_gain,
    inner_weight,
    outer_weight,
    bias_table,
    segment_ids,
    positions,
    cotangent,
):
    del positions
    width = tokens.shape[1]
    hidden = inner_weight.shape[1]
    rows = query_weight.shape[0]
    orders = bit_orders(n, rows, ORDERS)
    wide = outer_weight.shape[0]
    count = width // GROUP // 2
    part = hidden // 4
    all_a = 4 * width + LANES
    def split(columns, name):
        pairs = tuple(orders[key] for key in ORDERS if key[:-1] == name)
        if len(pairs) < 2 or pairs[0] is None:
            return (columns,), pairs[:1]
        return (SPLIT[name] * columns // LANES // 100 * LANES, columns), pairs

    lay_a = Layout(n, rows, *split(all_a, "a"))
    lay_i = Layout(n, rows, *split(hidden, "i"))
    lay_f = Layout(n, wide, *split(width, "f"))
    lay = {
        "g": Layout(n, wide, (width,), (orders["g"],)),
        "h": Layout(n, rows, (part,), (orders["h"],)),
        "j": Layout(n, rows, (hidden - part + width,), (orders["j"],)),
        "p": Layout(n, rows, (3 * width // 2,), (orders["p"],)),
        "q": Layout(n, rows, (3 * width // 2,), (orders["q"],)),
    }
    chains, v, state = {}, {}, {"last": []}
    weights = (query_weight, key_weight, value_weight, output_weight)
    packed = pack(lay_a, weights, (attention_gain, feedforward_gain))
    blocks = {
        "a": packed,
        "i": [inner_weight[:, low:high].astype(BF16) for low, high in lay_i.spans()],
        "f": [outer_weight[:, low:high].astype(BF16) for low, high in lay_f.spans()],
    }
    for name, layout in (("a", lay_a), ("i", lay_i), ("f", lay_f)):
        for k, (block, pair) in enumerate(zip(blocks[name], layout.orders)):
            if layout.paired:
                chains[name + str(k)] = Gather(block, pair, n, name != "a")
            else:
                v[name + str(k)] = lax.all_gather(block, AXIS, axis=0, tiled=True)
    lookup = offset_lookup()
    base = jnp.einsum("bkc,ch->hbk", lookup, bias_table, precision=HIGHEST)
    state["base"] = [base]

    def gathered(name, layout):
        if not layout.paired:
            return [v[name + "0"]]
        found = []
        for k in range(len(layout.cuts)):
            found += chains[name + str(k)].finish()
        return found

    def tied(value):
        return after(value, *state["last"])

    def scatter(name, parts):
        if lay[name].paired:
            chains[name] = Scatter(*parts, lay[name].orders[0], n)
        else:
            v[name] = lax.psum_scatter(parts[0].astype(F32), AXIS, scatter_dimension=0, tiled=True)

    def run(name):
        if name == "K1a":
            out = attention_early(lay_a, tied(tokens), segment_ids, base, gathered("a", lay_a), count)
            v["wa"], v["gain"], v["h1"], v["h1t"], *v["early"] = out
            return [out[8]]
        if name == "K1b":
            context, blocks_a = v["early"][4], gathered("a", lay_a)
            out = attention_late(
                lay_a, tied(v["h1"]), v["wa"], segment_ids, base, count, tokens, v["gain"], context, blocks_a
            )
            v["late"], (v["x1"], v["h2"], v["h2t"], v["wo"]) = out[:6], out[6:]
            return [v["h2"]]
        if name == "K2a":
            out = inner_forward(lay_i, lay["g"], tied(v["h2"]), cotangent, gathered("i", lay_i), hidden)
            v["z"], v["slope"], *parts = out
            scatter("g", parts)
            return parts[:1]
        if name == "K2ba":
            inner, outer = gathered("i", lay_i), gathered("f", lay_f)
            out = outer_backward(lay_i, lay_f, lay["h"], 0, part, tied(cotangent), v["h2t"], v["slope"], inner, outer)
            v["dh2"], *parts = out
            scatter("h", parts)
            return parts[:1]
        if name == "K2bb":
            more = (v["x1"], v["gain"], tied(v["dh2"]), v["early"][5], v["late"][5])
            inner, outer = gathered("i", lay_i), gathered("f", lay_f)
            out = outer_backward(
                lay_i, lay_f, lay["j"], part, hidden - part, cotangent, v["h2t"], v["slope"], inner, outer, more
            )
            v["dx1"], v["da"], v["dgain2"], *parts = out
            scatter("j", parts)
            return parts[:1]
        if name in ("K3a", "K3b"):
            late = name == "K3b"
            saved, target = v["late" if late else "early"], "pq"[late]
            out = scores_backward(lay[target], int(late), tied(v["da"]), v["wo"], *saved[:4], v["h1t"])
            v["grads" + target], v["table" + target], parts = out[:3], out[3], out[4:]
            scatter(target, parts)
            return parts[:1]
        if name == "K4":
            grads = (*v["gradsp"], *v["gradsq"])
            v["dx"], dgain1 = inputs_backward(tokens, tied(v["dx1"]), v["gain"], grads, v["wa"])
            diagonal = jnp.concatenate([v["tablep"], v["tableq"]], axis=0)
            table = jnp.einsum("hbk,bkc->ch", diagonal, lookup, precision=HIGHEST)
            small = jnp.concatenate([dgain1[0], v["dgain2"][0], table.reshape(-1)]).reshape(-1, LANES)
            if n & (n - 1):
                v["s"] = lax.psum(small, AXIS)
            else:
                chains["s"] = SumAll(small, n)
            return [v["dx"]]
        v["out"] = layer_output(lay_f, v["x1"], tied(v["z"]), gathered("f", lay_f))
        return [v["out"]]

    def exchange(names):
        active = [chains[name] for name in names if name in chains]
        if not active:
            return []
        arrived = [flight for chain in active for flight in chain.waits()]
        arrived = list(lax.optimization_barrier((*arrived, *state["last"])))
        for chain in active:
            chain.flights = [arrived.pop(0) for _ in chain.waits()]
        jobs = [chain.job() for chain in active]
        wanted = [job for job in jobs if job]
        large = any(job[2] * math.prod(job[1][0].shape[1:]) >= MIB // 2 for job in wanted) and len(wanted) == 1
        made = list(do_round(wanted)) if len(wanted) >= 3 or large else []
        sent = []
        for chain, job in zip(active, jobs):
            sent += chain.advance(made.pop(0) if job and made else None)
        return sent

    for names in SCHEDULE:
        if isinstance(names, str):
            state["last"] = run(names)
        else:
            state["last"] = list(exchange(names) or state["last"]) + state.pop("base", [])

    def total(name):
        if name not in chains:
            return v[name]
        return chains[name].finish()

    small = total("s").reshape(-1)
    start = lax.axis_index(AXIS) * rows
    joined = jnp.concatenate([total("p"), total("q")], axis=1)

    def projection(j):
        groups = range(j * GROUP, 3 * width, 3 * GROUP)
        return jnp.concatenate([joined[:, low : low + GROUP] for low in groups], axis=1)

    return (
        v["out"],
        v["dx"],
        lax.dynamic_slice(small, (start,), (rows,)),
        projection(0),
        projection(1),
        projection(2),
        total("j")[:, hidden - part :],
        lax.dynamic_slice(small, (width + start,), (rows,)),
        jnp.concatenate([total("h"), total("j")[:, : hidden - part]], axis=1),
        total("g"),
        small[2 * width :].reshape(NB, HEADS),
    )


def solution(mesh):
    n = mesh.shape[AXIS]
    matrix, vector = P(AXIS, None), P(AXIS)
    return jax.shard_map(
        functools.partial(per_device, n),
        mesh=mesh,
        in_specs=(
            matrix,
            vector,
            matrix,
            matrix,
            matrix,
            matrix,
            vector,
            matrix,
            matrix,
            P(),
            vector,
            vector,
            matrix,
        ),
        out_specs=(
            matrix,
            matrix,
            vector,
            matrix,
            matrix,
            matrix,
            matrix,
            vector,
            matrix,
            matrix,
            P(),
        ),
        check_vma=False,
    )
```

```python
import functools
import math

import jax
import jax.numpy as jnp
from jax import lax
from jax.experimental import pallas as pl
from jax.experimental.pallas import tpu as pltpu
from jax.sharding import PartitionSpec as P

AXIS = "fsdp"
HEADS = 16
HEAD = 64
NB = 32
SEQ = 256
SPAN = 2 * SEQ
LANES = 128
GROUP = 256
EPSILON = 1e-06
MASKED = -1000000000.0
LIMITS = (12, 16, 23, 32, 46, 64, 91)
HIGHEST = lax.Precision.HIGHEST
BF16 = jnp.bfloat16
F32 = jnp.float32
MIB = 1 << 20
VMEM_LIMIT = 62 * MIB
ORDERS = {
    "a0": ("zZyx", "Zzxy"),
    "a1": ("Zxzy", "xyZz"),
    "i0": ("yZxz", "xZzy"),
    "i1": ("Zzxy", "zxyZ"),
    "f0": ("zZxy", "Zyxz"),
    "g": ("xZzy", "yZxz"),
    "h": ("Zxzy", "Zxzy"),
    "j": ("zZyx", "Zzxy"),
    "p": ("Zxyz", "zyxZ"),
    "q": ("zZyx", "Zzxy"),
}
SPLIT = {"a": 67, "i": 67}
SCHEDULE = (
    ("a0", "a1"),
    ("a0", "a1", "i0", "i1"),
    ("a0", "a1", "i0", "i1", "f0"),
    ("a0", "a1"),
    ("a0", "a1", "i0", "i1", "f0"),
    "K1a",
    ("i0", "i1", "f0"),
    "K1b",
    ("i0", "i1"),
    ("f0",),
    "K2a",
    ("f0",),
    ("f0", "g"),
    "K2ba",
    ("g", "h"),
    "K2bb",
    ("g", "h", "j"),
    "K3a",
    ("g", "h", "j", "p"),
    "K3b",
    ("h", "j", "p", "q"),
    ("g",),
    "K4",
    ("q", "g", "h", "j", "s"),
    ("p",),
    "K5",
    ("h", "j", "p", "q", "s"),
    ("j", "p", "q", "s"),
    ("p", "q", "s"),
    ("q", "s"),
)
ROUND_COST = pl.CostEstimate(flops=50_000_000_000, transcendentals=0, bytes_accessed=0)
ANY = pl.BlockSpec(memory_space=pl.ANY)
VM = pl.BlockSpec(memory_space=pltpu.VMEM)


def no_time(**_):
    return pl.CostEstimate(flops=0, transcendentals=0, bytes_accessed=0)


def bucket_of(relative):
    distance = jnp.abs(relative)
    counted = jnp.zeros_like(distance)
    for threshold in LIMITS:
        counted = counted + (distance >= threshold).astype(jnp.int32)
    inside = jnp.where(distance < 8, distance, 8 + counted)
    return inside + jnp.where(relative > 0, 16, 0).astype(jnp.int32)


def offset_lookup():
    k = lax.broadcasted_iota(jnp.int32, (8, SPAN, NB), 1)
    b = lax.broadcasted_iota(jnp.int32, (8, SPAN, NB), 0)
    c = lax.broadcasted_iota(jnp.int32, (8, SPAN, NB), 2)
    offset = k - b
    offset = jnp.where(offset >= SEQ, offset - SPAN, offset)
    return (bucket_of(offset) == c).astype(F32)


def bit_orders(n, rows, wanted):
    if n & (n - 1) or n < 8 or rows % 16:
        return {name: None for name in wanted}
    high = list(range(1, n.bit_length() - 1))
    if n == 32:
        number = {"x": 1, "y": 2, "z": 3, "Z": 4}
        return {name: tuple([number[c] for c in order] + [0] for order in pair) for name, pair in wanted.items()}
    return {name: (high + [0], high[1:] + high[:1] + [0]) for name in wanted}


def swap(array, bits, n):
    return lax.ppermute(array, AXIS, [(i, i ^ (1 << bits[i & 1])) for i in range(n)])


def relative(bits, t):
    return sum(1 << b for k, b in enumerate(bits) if (t >> k) & 1)


def block_row(me, orders, t, n, rows):
    one, two = (relative(order, t) for order in (orders if t < n // 2 else orders[::-1]))
    return pl.multiple_of((me ^ (one + (me & 1) * (two - one))) * rows, rows)


def after(value, *others):
    return lax.optimization_barrier((value, *others))[0] if others else value


def round_kernel(plan, *refs):
    count = sum(len(kinds) for _, kinds in plan)
    inputs, outs = list(refs[:count]), refs[count:]
    for (kind, kinds), out in zip(plan, outs):
        terms = [inputs.pop(0) for _ in kinds]
        if kind == "join":
            half = terms[0].shape[0]
            out[:half] = terms[0][...]
            out[half:] = terms[1][...]
        elif kind == "small" and len(terms) == 4:
            out[...] = (terms[0][...] + terms[1][...]) + (terms[2][...] + terms[3][...])
        else:
            total = terms[0][...].astype(F32)
            for term in terms[1:]:
                total = total + term[...].astype(F32)
            out[...] = total.astype(out.dtype)


def do_round(jobs):
    plan, specs, arrays, shapes, out_specs = [], [], [], [], []
    moved = 0
    for kind, terms, size, index, dtype in jobs:
        if kind == "small":
            specs += [pl.BlockSpec(term.shape, lambda i: (0, 0)) for term in terms]
            shapes.append(jax.ShapeDtypeStruct(terms[0].shape, dtype))
            out_specs.append(specs[-1])
        else:
            rows, cols = terms[0].shape[1] // 2, terms[0].shape[2]
            specs += [pl.BlockSpec((size, rows, cols), lambda i, k=index: (k, i, 0)) for _ in terms]
            made = 2 * size if kind == "join" else size
            shapes.append(jax.ShapeDtypeStruct((made, 2 * rows, cols), dtype))
            out_specs.append(pl.BlockSpec((made, rows, cols), lambda i: (0, i, 0)))
            moved += 2 * (len(terms) + 1) * size * 2 * rows * cols
        plan.append((kind, (0,) * len(terms)))
        arrays += terms
    return pl.pallas_call(
        functools.partial(round_kernel, tuple(plan)),
        grid=(2,),
        out_shape=shapes,
        in_specs=specs,
        out_specs=out_specs,
        compiler_params=pltpu.CompilerParams(vmem_limit_bytes=VMEM_LIMIT),
        cost_estimate=ROUND_COST,
        name="exchange_round",
    )(*arrays)


class Gather:
    def __init__(self, own, orders, n, early):
        self.have, self.orders, self.n, self.last = own[None], orders, n, len(orders[0]) - 1
        self.step, self.parts, self.flights, self.early = 0, None, [self.have], early

    def waits(self):
        return self.flights

    def job(self):
        if 0 < self.step < self.last:
            return "join", [self.have, self.flights[0]], self.have.shape[0], 0, BF16
        return None

    def advance(self, made=None):
        if self.step > self.last:
            self.parts = [self.have, self.far, *self.near, *self.flights]
            return self.flights
        bits = [order[self.step] for order in self.orders]
        core = [order[self.last] for order in self.orders]
        if self.step == self.last:
            self.far, *self.near = self.flights
            self.flights = [swap(self.far, bits, self.n)]
            if not self.near:
                self.flights.insert(0, swap(after(self.have, self.far), bits, self.n))
        else:
            if self.step == 0:
                self.have = self.flights[0]
            else:
                self.have = jnp.concatenate([self.have, self.flights[0]], axis=0) if made is None else made
            self.flights = [swap(self.have, bits, self.n)]
            if self.early and self.step == self.last - 1:
                self.flights.append(swap(self.have, core, self.n))
        self.step += 1
        return [self.far if self.step > self.last else self.have]

    def finish(self):
        while self.parts is None:
            self.advance()
        return self.parts


class Scatter:
    def __init__(self, send, keep, orders, n):
        self.orders, self.n, self.step = orders, n, len(orders[0]) - 1
        self.terms, self.flights, self.result = [keep], [send], None
        self.first = self.step

    def waits(self):
        return self.flights

    def job(self):
        if self.step == self.first:
            return None
        half = 1 << max(self.step, 0)
        return "sum", self.terms + self.flights, half, int(self.step >= 0), BF16 if self.step >= 0 else F32

    def advance(self, made=None):
        send = self.flights[0]
        if self.step < self.first:
            _, terms, half, index, dtype = self.job()
            send = sum(term[half * index : half * (index + 1)].astype(F32) for term in terms) if made is None else made
            self.terms = terms
            if self.step < 0:
                self.result = send[0]
                return [send]
        send = send.astype(BF16)
        self.flights = [swap(send, [order[self.step] for order in self.orders], self.n)]
        self.step -= 1
        return [send]

    def finish(self):
        while self.result is None:
            self.advance()
        return self.result


class SumAll:
    def __init__(self, values, n):
        bits = list(range(n.bit_length() - 1))
        self.masks = [(1 << b,) for b in bits[:-2]] + [tuple(m << bits[-2] for m in (1, 2, 3))]
        self.values, self.n, self.step, self.result, self.flights = values, n, 0, None, [values]

    def waits(self):
        return self.flights

    def job(self):
        return ("small", [self.values, *self.flights], 0, 0, F32) if self.step else None

    def advance(self, made=None):
        if self.step == 0:
            (self.values,) = self.flights
        elif made is None:
            self.values = self.total()
        else:
            self.values = made
        if self.step == len(self.masks):
            self.result = self.values
        else:
            pairs = [[(i, i ^ mask) for i in range(self.n)] for mask in self.masks[self.step]]
            self.flights = [lax.ppermute(self.values, AXIS, pair) for pair in pairs]
        self.step += 1
        return [self.values]

    def total(self):
        if len(self.flights) == 1:
            return self.values + self.flights[0]
        one, two, three = self.flights
        return (self.values + one) + (two + three)

    def finish(self):
        while self.result is None:
            self.advance()
        return self.result


class Layout:
    def __init__(self, n, rows, cuts, orders):
        self.n, self.rows = n, rows
        self.cuts, self.orders = cuts, orders
        self.paired = orders[0] is not None

    def spans(self):
        return tuple(zip((0,) + tuple(self.cuts[:-1]), self.cuts))

    def count(self):
        return 4 * len(self.cuts) if self.paired else 1

    def load(self, me, refs, full, sems, first=0, cols=None, chunk=None):
        size = full.shape[0]
        begin, end = cols or (0, self.cuts[-1])
        chunk = chunk or size
        if not self.paired:
            waits = []
            for c in range(size // chunk):
                source = refs[0].at[first + c * chunk : first + (c + 1) * chunk, begin:end]
                copy = pltpu.make_async_copy(source, full.at[c * chunk : (c + 1) * chunk], sems.at[c])
                copy.start()
                waits.append(copy.wait)
            return waits
        whole_rows = size == self.n * self.rows
        for s, ((lo, hi), orders) in enumerate(zip(self.spans(), self.orders)):
            low, high = max(lo, begin), min(hi, end)
            if low >= high:
                continue
            for t in range(self.n):
                ref = refs[4 * s + t // (self.n // 4)].at[t % (self.n // 4), :, low - lo : high - lo]
                row = block_row(me, orders, t, self.n, self.rows)

                def start(row, ref=ref, low=low, high=high):
                    target = full.at[pl.ds(row, self.rows), low - begin : high - begin]
                    sem = sems.at[0 if chunk == size else lax.div(row, chunk)]
                    pltpu.make_async_copy(ref, target, sem).start()

                if whole_rows:
                    start(row)
                else:
                    row = pl.multiple_of(row - first, self.rows)
                    pl.when(jnp.logical_and(row >= 0, row < size))(functools.partial(start, row))
        def wait(c):
            view = full.at[c * chunk : (c + 1) * chunk]
            pltpu.make_async_copy(view, view, sems.at[c]).wait()

        return [functools.partial(wait, c) for c in range(size // chunk)]

    def out_shapes(self):
        if not self.paired:
            return [jax.ShapeDtypeStruct((self.n * self.rows, self.cuts[-1]), BF16)]
        return [jax.ShapeDtypeStruct((self.n // 2, self.rows, self.cuts[-1]), BF16)] * 2

    def store(self, me, stage, refs, sem, cols=None):
        begin, end = cols or (0, self.cuts[-1])
        if not self.paired:
            copy = pltpu.make_async_copy(stage.at[:, begin:end], refs[0].at[:, begin:end], sem)
            copy.start()
            return copy.wait
        half = self.n // 2
        for t in [*range(half, self.n), *range(half)]:
            row = block_row(me, self.orders[0], t, self.n, self.rows)
            target = refs[0 if t >= half else 1].at[t % half, :, begin:end]
            pltpu.make_async_copy(stage.at[pl.ds(row, self.rows), begin:end], target, sem).start()
        view = stage.at[:, begin:end]
        return pltpu.make_async_copy(view, view, sem).wait


def dot(a, b):
    return lax.dot_general(a, b, (((1,), (0,)), ((), ())), preferred_element_type=F32)


def dot_nt(a, b):
    return lax.dot_general(a, b, (((1,), (1,)), ((), ())), preferred_element_type=F32)


def dot_tn(a, b):
    return lax.dot_general(a, b, (((0,), (0,)), ((), ())), preferred_element_type=F32)


def row_scale(values):
    return lax.rsqrt(jnp.mean(values * values, axis=-1, keepdims=True) + EPSILON)


def toeplitz(base):
    return jnp.concatenate(
        [(pltpu.roll(base, 8 * a, 1) if a else base)[:, :SEQ] for a in range(SEQ // 8)], axis=0
    )


def diagonals(scores):
    total = None
    for a in range(SEQ // 8):
        rows = scores[8 * a : 8 * a + 8]
        rows = jnp.concatenate([rows, jnp.zeros((8, SPAN - SEQ), F32)], axis=1)
        if a:
            rows = pltpu.roll(rows, SPAN - 8 * a, 1)
        total = rows if total is None else total + rows
    return total


def transposed(values):
    return values.T


def copy_out(copies, sems, k, source, target):
    copy = pltpu.make_async_copy(source, target, sems.at[k])
    copy.start()
    copies.append(copy)


def pack_kernel(spans, *refs):
    q_ref, k_ref, v_ref, o_ref, one_ref, two_ref = refs[:6]
    rows, width = q_ref.shape
    line = lax.broadcasted_iota(jnp.int32, (LANES, rows), 0)
    gains = jnp.where(line == 0, one_ref[...], jnp.where(line == 1, two_ref[...], 0.0)).T
    for (low, high), out in zip(spans, refs[6:]):
        for k, ref in enumerate((q_ref, k_ref, v_ref, o_ref, gains)):
            begin, end = max(low, k * width), min(high, k * width + ref.shape[1])
            if begin < end:
                out[:, begin - low : end - low] = ref[:, begin - k * width : end - k * width].astype(BF16)


def pack(lay, weights, gains):
    rows = weights[0].shape[0]
    return pl.pallas_call(
        functools.partial(pack_kernel, lay.spans()),
        out_shape=[jax.ShapeDtypeStruct((rows, high - low), BF16) for low, high in lay.spans()],
        in_specs=[VM] * 6,
        out_specs=[VM] * len(lay.cuts),
        name="pack",
    )(*weights, *(gain.reshape(1, rows) for gain in gains))


def attend(seqs, h1, weights, segments_ref, base_ref, q_ref, k_ref, v_ref, p_ref, c_ref, ct_ref):
    for ref, weight in zip((q_ref, k_ref, v_ref), weights):
        ref[...] = dot(h1, weight).astype(BF16)
    first = lax.broadcasted_iota(jnp.int32, (SEQ, LANES), 1) < HEAD
    for p in range(GROUP // LANES):
        lanes = slice(p * LANES, (p + 1) * LANES)
        biases = [toeplitz(base_ref[2 * p + o]) for o in range(2)]
        for s in range(seqs):
            rows = slice(s * SEQ, (s + 1) * SEQ)
            q2, k2, v2 = q_ref[rows, lanes], k_ref[rows, lanes], v_ref[rows, lanes]
            line = jnp.broadcast_to(segments_ref[s : s + 1, :], (SEQ, SEQ))
            allowed = line.T == line
            made = []
            for o in range(2):
                mine = jnp.where(first == (o == 0), q2, jnp.zeros_like(q2))
                scores = jnp.where(allowed, dot_nt(mine, k2) + biases[o], MASKED)
                exponent = jnp.exp(scores - jnp.max(scores, axis=-1, keepdims=True))
                prob = exponent * (1.0 / jnp.sum(exponent, axis=-1, keepdims=True))
                p_ref[s, 2 * p + o] = prob
                made.append(dot(prob.astype(BF16), v2))
            c_ref[rows, lanes] = jnp.where(first, made[0], made[1]).astype(BF16)
    ct_ref[...] = transposed(c_ref[...])


def early_kernel(lay, seqs, width, steps, *refs):
    m = lay.count()
    x_ref, segments_ref, base_ref = refs[:3]
    blocks = refs[3 : 3 + m]
    wa_out, gain_ref, h1_ref, h1t_ref = refs[3 + m : 7 + m]
    outs = refs[7 + m : 13 + m]
    wa, gains_s, sems = refs[13 + m :]
    step = pl.program_id(0)

    @pl.when(step == 0)
    def _():
        me = lax.axis_index(AXIS)
        waits = lay.load(me, blocks, gains_s, sems.at[0:1], cols=(4 * width, 4 * width + LANES))
        for j in range(3):
            cols = (j * width, (j + 1) * width)
            waits += lay.load(me, blocks, wa.at[:, j * width : (j + 1) * width], sems.at[1 + j : 2 + j], cols=cols)
        waits[0]()
        gains = gains_s[...].astype(F32).T
        gain_ref[...] = gains[:8]
        x = x_ref[...].astype(F32)
        h1 = (x * row_scale(x) * gains[0:1]).astype(BF16)
        h1_ref[...] = h1
        h1t_ref[...] = transposed(h1)
        for wait in waits[1:]:
            wait()
        pltpu.make_async_copy(wa, wa_out, sems.at[0]).start()

    weights = [wa[:, pl.ds(pl.multiple_of(j * width + step * GROUP, GROUP), GROUP)] for j in range(3)]
    attend(seqs, h1_ref[...], weights, segments_ref, base_ref, *outs)

    @pl.when(step == steps - 1)
    def _():
        pltpu.make_async_copy(wa, wa_out, sems.at[0]).wait()


def late_kernel(lay, seqs, steps, *refs):
    m = lay.count()
    h1_ref, wq_ref, wk_ref, wv_ref, segments_ref, base_ref, x_ref, gain_ref, context_ref = refs[:9]
    blocks = refs[9 : 9 + m]
    outs, (x1_ref, h2_ref, h2t_ref, wo_out) = refs[9 + m : 15 + m], refs[15 + m : 19 + m]
    context, wo_ref, sems = refs[19 + m :]
    step = pl.program_id(0)
    width = x_ref.shape[1]

    @pl.when(step == 0)
    def _():
        lay.load(lax.axis_index(AXIS), blocks, wo_ref, sems.at[0:1], cols=(3 * width, 4 * width))

    attend(seqs, h1_ref[...], (wq_ref[...], wk_ref[...], wv_ref[...]), segments_ref, base_ref, *outs)
    context[:, pl.ds(pl.multiple_of(step * GROUP, GROUP), GROUP)] = outs[4][...]

    @pl.when(step == steps - 1)
    def _():
        pltpu.make_async_copy(wo_ref, wo_ref, sems.at[0]).wait()
        copy = pltpu.make_async_copy(wo_ref, wo_out, sems.at[1])
        copy.start()
        early = context_ref.shape[1]
        for c in range(0, width, 512):
            cols = slice(c, c + 512)
            x1_ref[:, cols] = (
                x_ref[:, cols].astype(F32)
                + dot(context_ref[...], wo_ref[:early, cols])
                + dot(context[...], wo_ref[early:, cols])
            )
        x1 = x1_ref[...]
        h2 = (x1 * row_scale(x1) * gain_ref[1:2, :]).astype(BF16)
        h2_ref[...] = h2
        h2t_ref[...] = transposed(h2)
        copy.wait()


def attention_outputs(tokens, width, count):
    sds = jax.ShapeDtypeStruct
    seqs, heads = tokens // SEQ, GROUP // HEAD
    shapes = [sds((tokens, count * GROUP), BF16)] * 3
    specs = [pl.BlockSpec((tokens, GROUP), lambda i: (0, i))] * 3
    shapes.append(sds((seqs, count * heads, SEQ, SEQ), F32))
    specs.append(pl.BlockSpec((seqs, heads, SEQ, SEQ), lambda i: (0, i, 0, 0)))
    shapes.append(sds((tokens, count * GROUP), BF16))
    specs.append(pl.BlockSpec((tokens, GROUP), lambda i: (0, i)))
    shapes.append(sds((count * GROUP, tokens), BF16))
    specs.append(pl.BlockSpec((GROUP, tokens), lambda i: (i, 0)))
    return shapes, specs


def whole(shape):
    return pl.BlockSpec(shape, lambda i: (0,) * len(shape))


def attention_cost(tokens, width, count):
    share = count * GROUP
    return no_time(
        flops=2 * tokens * width * 3 * share + 16 * tokens * SEQ * share,
        transcendentals=tokens * SEQ * share // HEAD,
        bytes_accessed=(6 * width * share + 8 * tokens * share + 4 * tokens * SEQ * share // HEAD),
    )


def attention_early(lay, x, segments, base, blocks, count):
    tokens, width = x.shape
    seqs, wide, heads = tokens // SEQ, 3 * width, GROUP // HEAD
    sds = jax.ShapeDtypeStruct
    shapes, specs = attention_outputs(tokens, width, count)
    return pl.pallas_call(
        functools.partial(early_kernel, lay, seqs, width, count),
        grid=(count,),
        out_shape=[sds((width, wide), BF16), sds((8, width), F32), sds((tokens, width), BF16), sds((width, tokens), BF16)]
        + shapes,
        in_specs=[
            whole((tokens, width)),
            whole((seqs, SEQ)),
            pl.BlockSpec((heads, 8, SPAN), lambda i: (i, 0, 0)),
        ]
        + [ANY] * len(blocks),
        out_specs=[ANY, whole((8, width)), whole((tokens, width)), whole((width, tokens))] + specs,
        scratch_shapes=[
            pltpu.VMEM((width, wide), BF16),
            pltpu.VMEM((width, LANES), BF16),
            pltpu.SemaphoreType.DMA((4,)),
        ],
        compiler_params=pltpu.CompilerParams(vmem_limit_bytes=VMEM_LIMIT),
        cost_estimate=attention_cost(tokens, width, count),
        name="attention_early",
    )(x, segments.reshape(seqs, SEQ), base, *blocks)


def attention_late(lay, h1, wa, segments, base, count, x, gain, context, blocks):
    tokens, width = h1.shape
    seqs, heads, skip = tokens // SEQ, GROUP // HEAD, width // GROUP - count
    shapes, specs = attention_outputs(tokens, width, count)
    per = width // GROUP
    sds = jax.ShapeDtypeStruct
    return pl.pallas_call(
        functools.partial(late_kernel, lay, seqs, count),
        grid=(count,),
        out_shape=shapes
        + [sds((tokens, width), F32), sds((tokens, width), BF16), sds((width, tokens), BF16), sds((width, width), BF16)],
        in_specs=[whole((tokens, width))]
        + [pl.BlockSpec((width, GROUP), lambda i, j=j: (0, j * per + skip + i)) for j in range(3)]
        + [
            whole((seqs, SEQ)),
            pl.BlockSpec((heads, 8, SPAN), lambda i: (skip + i, 0, 0)),
            whole((tokens, width)),
            whole((8, width)),
            whole(context.shape),
        ]
        + [ANY] * len(blocks),
        out_specs=specs + [whole((tokens, width)), whole((tokens, width)), whole((width, tokens)), ANY],
        scratch_shapes=[
            pltpu.VMEM((tokens, count * GROUP), BF16),
            pltpu.VMEM((width, width), BF16),
            pltpu.SemaphoreType.DMA((2,)),
        ],
        compiler_params=pltpu.CompilerParams(vmem_limit_bytes=VMEM_LIMIT),
        cost_estimate=attention_cost(tokens, width, count),
        name="attention_late",
    )(h1, wa, wa, wa, segments.reshape(seqs, SEQ), base, x, gain, context, *blocks)


def inner_kernel(lay, lay_out, chunk, *refs):
    m, k = lay.count(), len(lay_out.out_shapes())
    h2_ref, e_ref = refs[:2]
    blocks = refs[2 : 2 + m]
    z_out, g_out = refs[2 + m : 4 + m]
    grads = refs[4 + m : 4 + m + k]
    wi, z_s, g_s, stage, lsem, osem, gsem = refs[4 + m + k :]
    me = lax.axis_index(AXIS)
    hidden = wi.shape[1]
    parts = 4
    size = hidden // parts
    waits = []
    for p in range(parts):
        cols = (p * size, (p + 1) * size)
        waits += lay.load(me, blocks, wi.at[:, p * size : (p + 1) * size], lsem.at[p : p + 1], cols=cols)

    def step(c, carry):
        cols = pl.ds(pl.multiple_of(c * chunk, chunk), chunk)
        u = dot(h2_ref[...], wi[:, cols])
        cdf = 0.5 * (1.0 + lax.erf(u * (1.0 / math.sqrt(2.0))))
        z = (u * cdf).astype(BF16)
        z_s[:, cols] = z
        g_s[:, cols] = cdf + u * jnp.exp(-0.5 * u * u) * (1.0 / math.sqrt(2.0 * math.pi))
        stage[cols, :] = dot(transposed(z), e_ref[...]).astype(BF16)
        pltpu.make_async_copy(z_s.at[:, cols], z_out.at[:, cols], osem.at[0]).start()
        pltpu.make_async_copy(g_s.at[:, cols], g_out.at[:, cols], osem.at[1]).start()
        return carry

    for p in range(parts):
        waits[p]()
        lax.fori_loop(p * size // chunk, (p + 1) * size // chunk, step, 0)
    done = lay_out.store(me, stage, grads, gsem)
    pltpu.make_async_copy(z_s, z_out, osem.at[0]).wait()
    pltpu.make_async_copy(g_s, g_out, osem.at[1]).wait()
    done()


def inner_forward(lay, lay_out, h2, cotangent, blocks, hidden):
    tokens, width = h2.shape
    sds = jax.ShapeDtypeStruct
    grads = lay_out.out_shapes()
    return pl.pallas_call(
        functools.partial(inner_kernel, lay, lay_out, 512),
        out_shape=[sds((tokens, hidden), BF16), sds((tokens, hidden), F32)] + grads,
        in_specs=[VM] * 2 + [ANY] * len(blocks),
        out_specs=[ANY] * (2 + len(grads)),
        scratch_shapes=[
            pltpu.VMEM((width, hidden), BF16),
            pltpu.VMEM((tokens, hidden), BF16),
            pltpu.VMEM((tokens, hidden), F32),
            pltpu.VMEM((hidden, width), BF16),
            pltpu.SemaphoreType.DMA((4,)),
            pltpu.SemaphoreType.DMA((2,)),
            pltpu.SemaphoreType.DMA,
        ],
        compiler_params=pltpu.CompilerParams(vmem_limit_bytes=VMEM_LIMIT),
        cost_estimate=no_time(
            flops=4 * tokens * width * hidden, transcendentals=2 * tokens * hidden, bytes_accessed=32 * MIB
        ),
        name="feedforward_inner",
    )(h2, cotangent, *blocks)


def outer_kernel(lay_i, lay_f, lay_g, chunk, first, last, *refs):
    mi, mf = lay_i.count(), lay_f.count()
    e_ref, h2t_ref, g_in = refs[:3]
    at = 3
    if last:
        x1_ref, gain_ref, dh_ref = refs[3:6]
        contexts = refs[6:8]
        at = 8
    inner, outer = refs[at : at + mi], refs[at + mi : at + mi + mf]
    at += mi + mf
    dx1_ref, at = refs[at], at + 1
    if last:
        da_ref, dgain_ref = refs[at : at + 2]
        at += 2
    kg = len(lay_g.out_shapes())
    grads, at = refs[at : at + kg], at + kg
    wi, wf, g_s, stage, fsem, lsem, isem, gsem = refs[at:]
    me = lax.axis_index(AXIS)
    size = wi.shape[1]
    steps = size // chunk
    outer_waits = lay_f.load(me, outer, wf, fsem, first=first, chunk=chunk)
    copies, inner_waits = [], []
    for c in range(steps):
        source = g_in.at[:, first + c * chunk : first + (c + 1) * chunk]
        copies.append(pltpu.make_async_copy(source, g_s.at[:, c * chunk : (c + 1) * chunk], isem.at[c]))
        copies[-1].start()
    wide = 2 * chunk
    for c in range(size // wide):
        target = wi.at[:, c * wide : (c + 1) * wide]
        cols = (first + c * wide, first + (c + 1) * wide)
        inner_waits += lay_i.load(me, inner, target, lsem.at[c : c + 1], cols=cols)
    e = e_ref[...]
    for c in range(steps):
        cols = slice(c * chunk, (c + 1) * chunk)
        outer_waits[c]()
        copies[c].wait()
        du = (dot_nt(e, wf[cols, :]) * g_s[:, cols]).astype(BF16)
        stage[:, cols] = dot(h2t_ref[...], du).astype(BF16)
        if c % 2 == 0:
            inner_waits[c // 2]()
        part = dot_nt(du, wi[:, cols])
        if c == 0:
            dx1_ref[...] = part + dh_ref[...] if last else part
        else:
            dx1_ref[...] += part
    if last:
        dh2 = dx1_ref[...]
        x1 = x1_ref[...]
        gain = gain_ref[1:2, :]
        scale = row_scale(x1)
        dgain_ref[...] = jnp.broadcast_to(jnp.sum(dh2 * (x1 * scale), axis=0, keepdims=True), dgain_ref.shape)
        mean = jnp.mean(x1 * gain * dh2, axis=-1, keepdims=True)
        dx1 = e.astype(F32) + scale * gain * dh2 - x1 * (scale * scale * scale) * mean
        dx1_ref[...] = dx1
        da = dx1.astype(BF16)
        da_ref[...] = da
        rows = stage.shape[0] // 2
        for p, context in enumerate(contexts):
            stage[p * rows : (p + 1) * rows, size:] = dot(context[...], da).astype(BF16)
    lay_g.store(me, stage, grads, gsem)()


def outer_backward(lay_i, lay_f, lay_g, first, size, cotangent, h2t, g, inner, outer, more=()):
    tokens, width = cotangent.shape
    chunk = 512
    last = first > 0
    sds = jax.ShapeDtypeStruct
    out_shape = [sds((tokens, width), F32)]
    out_specs = [VM]
    if last:
        out_shape += [sds((tokens, width), BF16), sds((8, width), F32)]
        out_specs += [VM] * 2
    grads = lay_g.out_shapes()
    return pl.pallas_call(
        functools.partial(outer_kernel, lay_i, lay_f, lay_g, chunk, first, last),
        out_shape=out_shape + grads,
        in_specs=[VM, VM, ANY] + [VM] * len(more) + [ANY] * (len(inner) + len(outer)),
        out_specs=out_specs + [ANY] * len(grads),
        scratch_shapes=[
            pltpu.VMEM((width, size), BF16),
            pltpu.VMEM((size, width), BF16),
            pltpu.VMEM((tokens, size), F32),
            pltpu.VMEM((width, lay_g.cuts[-1]), BF16),
            pltpu.SemaphoreType.DMA((size // chunk,)),
            pltpu.SemaphoreType.DMA((size // chunk // 2,)),
            pltpu.SemaphoreType.DMA((size // chunk,)),
            pltpu.SemaphoreType.DMA,
        ],
        compiler_params=pltpu.CompilerParams(vmem_limit_bytes=VMEM_LIMIT),
        cost_estimate=no_time(
            flops=6 * tokens * width * size + 2 * last * tokens * width * width,
            transcendentals=tokens,
            bytes_accessed=24 * MIB,
        ),
        name="feedforward_outer_" + "ab"[last],
    )(cotangent, h2t, g, *more, *inner, *outer)


def scores_kernel(lay, seqs, width, steps, *refs):
    k = len(lay.out_shapes())
    da_ref, wo_ref, q_ref, k_ref, v_ref, p_ref, h1t_ref = refs[:7]
    dq_ref, dk_ref, dv_ref, table_ref = refs[7:11]
    grads = refs[11 : 11 + k]
    dc, stage, gsem = refs[11 + k :]
    step = pl.program_id(0)
    dc[...] = dot_nt(da_ref[...], wo_ref[...]).astype(BF16)
    first = lax.broadcasted_iota(jnp.int32, (SEQ, LANES), 1) < HEAD
    for p in range(GROUP // LANES):
        lanes = slice(p * LANES, (p + 1) * LANES)
        totals = [None, None]
        for s in range(seqs):
            rows = slice(s * SEQ, (s + 1) * SEQ)
            dc2, q2, k2, v2 = dc[rows, lanes], q_ref[rows, lanes], k_ref[rows, lanes], v_ref[rows, lanes]
            made = []
            for o in range(2):
                prob = p_ref[s, 2 * p + o]
                mine = jnp.where(first == (o == 0), dc2, jnp.zeros_like(dc2))
                dprob = dot_nt(mine, v2)
                inner = jnp.sum(prob * dprob, axis=-1, keepdims=True)
                ds = (prob * (dprob - inner)).astype(BF16)
                wide = ds.astype(F32)
                totals[o] = wide if totals[o] is None else totals[o] + wide
                made.append(
                    (dot(ds, k2), dot(transposed(ds), q2), dot(transposed(prob.astype(BF16)), dc2))
                )
            for ref, one, two in zip((dq_ref, dk_ref, dv_ref), *made):
                ref[rows, lanes] = jnp.where(first, one, two).astype(BF16)
        for o in range(2):
            table_ref[2 * p + o] = diagonals(totals[o])
    for j, ref in enumerate((dq_ref, dk_ref, dv_ref)):
        col = pl.ds(pl.multiple_of((3 * step + j) * GROUP, GROUP), GROUP)
        stage[:, col] = dot(h1t_ref[...], ref[...]).astype(BF16)

    @pl.when(step == steps - 1)
    def _():
        lay.store(lax.axis_index(AXIS), stage, grads, gsem)()


def scores_backward(lay, part, da, wo, q, k, v, p, h1t):
    tokens, width = da.shape
    count = q.shape[1] // GROUP
    seqs, heads = tokens // SEQ, GROUP // HEAD
    sds = jax.ShapeDtypeStruct
    grads = lay.out_shapes()
    share = count * GROUP
    return pl.pallas_call(
        functools.partial(scores_kernel, lay, seqs, width, count),
        grid=(count,),
        out_shape=[sds((tokens, share), BF16)] * 3 + [sds((count * heads, 8, SPAN), F32)] + grads,
        in_specs=[whole((tokens, width)), pl.BlockSpec((GROUP, width), lambda i: (part * count + i, 0))]
        + [pl.BlockSpec((tokens, GROUP), lambda i: (0, i))] * 3
        + [pl.BlockSpec((seqs, heads, SEQ, SEQ), lambda i: (0, i, 0, 0)), whole((width, tokens))],
        out_specs=[pl.BlockSpec((tokens, GROUP), lambda i: (0, i))] * 3
        + [pl.BlockSpec((heads, 8, SPAN), lambda i: (i, 0, 0))]
        + [ANY] * len(grads),
        scratch_shapes=[
            pltpu.VMEM((tokens, GROUP), BF16),
            pltpu.VMEM((width, 3 * share), BF16),
            pltpu.SemaphoreType.DMA,
        ],
        compiler_params=pltpu.CompilerParams(vmem_limit_bytes=VMEM_LIMIT),
        cost_estimate=no_time(
            flops=8 * tokens * width * share + 40 * tokens * SEQ * share,
            transcendentals=0,
            bytes_accessed=16 * MIB,
        ),
        name="attention_backward_" + "ab"[part],
    )(da, wo, q, k, v, p, h1t)


def inputs_kernel(width, parts, *refs):
    x_ref, dx1_ref, gain_ref = refs[:3]
    grads = refs[3 : 3 + 3 * parts]
    wa_in, dx_ref, dgain_ref, wa, dh, sem = refs[3 + 3 * parts :]
    copies = []
    for j in range(3):
        cols = slice(j * width, (j + 1) * width)
        copies.append(pltpu.make_async_copy(wa_in.at[:, cols], wa.at[:, cols], sem.at[j]))
        copies[-1].start()
    size = width // parts
    for j in range(3):
        copies[j].wait()
        for c in range(0, width, 512):
            for p in range(parts):
                low = j * width + p * size
                part = dot_nt(grads[3 * p + j][...], wa[c : c + 512, low : low + size])
                if j or p:
                    dh[:, c : c + 512] += part
                else:
                    dh[:, c : c + 512] = part
    x = x_ref[...].astype(F32)
    gain = gain_ref[0:1, :]
    scale = row_scale(x)
    dh1 = dh[...]
    dgain_ref[...] = jnp.broadcast_to(jnp.sum(dh1 * (x * scale), axis=0, keepdims=True), dgain_ref.shape)
    mean = jnp.mean(x * gain * dh1, axis=-1, keepdims=True)
    dx_ref[...] = (dx1_ref[...] + scale * gain * dh1 - x * (scale * scale * scale) * mean).astype(BF16)


def inputs_backward(x, dx1, gain, grads, wa):
    tokens, width = x.shape
    sds = jax.ShapeDtypeStruct
    return pl.pallas_call(
        functools.partial(inputs_kernel, width, len(grads) // 3),
        out_shape=[sds((tokens, width), BF16), sds((8, width), F32)],
        in_specs=[VM] * (3 + len(grads)) + [ANY],
        out_specs=[VM] * 2,
        scratch_shapes=[
            pltpu.VMEM((width, 3 * width), BF16),
            pltpu.VMEM((tokens, width), F32),
            pltpu.SemaphoreType.DMA((3,)),
        ],
        compiler_params=pltpu.CompilerParams(vmem_limit_bytes=VMEM_LIMIT),
        cost_estimate=no_time(
            flops=6 * tokens * width * width, transcendentals=tokens, bytes_accessed=16 * MIB
        ),
        name="inputs_backward",
    )(x, dx1, gain, *grads, wa)


def output_kernel(lay, *refs):
    m = lay.count()
    x1_ref, z_ref = refs[:2]
    blocks = refs[2 : 2 + m]
    out_ref, wf, sem = refs[2 + m :]
    lay.load(lax.axis_index(AXIS), blocks, wf, sem)[0]()
    width = wf.shape[1]
    for c in range(0, width, 512):
        cols = slice(c, c + 512)
        out_ref[:, cols] = (x1_ref[:, cols] + dot(z_ref[...], wf[:, cols])).astype(BF16)


def layer_output(lay, x1, z, blocks):
    tokens, width = x1.shape
    hidden = z.shape[1]
    return pl.pallas_call(
        functools.partial(output_kernel, lay),
        out_shape=jax.ShapeDtypeStruct((tokens, width), BF16),
        in_specs=[VM] * 2 + [ANY] * len(blocks),
        out_specs=VM,
        scratch_shapes=[
            pltpu.VMEM((hidden, width), BF16),
            pltpu.SemaphoreType.DMA((1,)),
        ],
        compiler_params=pltpu.CompilerParams(vmem_limit_bytes=VMEM_LIMIT),
        cost_estimate=no_time(
            flops=2 * tokens * width * hidden, transcendentals=0, bytes_accessed=16 * MIB
        ),
        name="layer_output",
    )(x1, z, *blocks)


def per_device(
    n,
    tokens,
    attention_gain,
    query_weight,
    key_weight,
    value_weight,
    output_weight,
    feedforward_gain,
    inner_weight,
    outer_weight,
    bias_table,
    segment_ids,
    positions,
    cotangent,
):
    del positions
    width = tokens.shape[1]
    hidden = inner_weight.shape[1]
    rows = query_weight.shape[0]
    orders = bit_orders(n, rows, ORDERS)
    wide = outer_weight.shape[0]
    count = width // GROUP // 2
    part = hidden // 4
    all_a = 4 * width + LANES
    def split(columns, name):
        pairs = tuple(orders[key] for key in ORDERS if key[:-1] == name)
        if len(pairs) < 2 or pairs[0] is None:
            return (columns,), pairs[:1]
        return (SPLIT[name] * columns // LANES // 100 * LANES, columns), pairs

    lay_a = Layout(n, rows, *split(all_a, "a"))
    lay_i = Layout(n, rows, *split(hidden, "i"))
    lay_f = Layout(n, wide, *split(width, "f"))
    lay = {
        "g": Layout(n, wide, (width,), (orders["g"],)),
        "h": Layout(n, rows, (part,), (orders["h"],)),
        "j": Layout(n, rows, (hidden - part + width,), (orders["j"],)),
        "p": Layout(n, rows, (3 * width // 2,), (orders["p"],)),
        "q": Layout(n, rows, (3 * width // 2,), (orders["q"],)),
    }
    chains, v, state = {}, {}, {"last": []}
    weights = (query_weight, key_weight, value_weight, output_weight)
    packed = pack(lay_a, weights, (attention_gain, feedforward_gain))
    blocks = {
        "a": packed,
        "i": [inner_weight[:, low:high].astype(BF16) for low, high in lay_i.spans()],
        "f": [outer_weight[:, low:high].astype(BF16) for low, high in lay_f.spans()],
    }
    for name, layout in (("a", lay_a), ("i", lay_i), ("f", lay_f)):
        for k, (block, pair) in enumerate(zip(blocks[name], layout.orders)):
            if layout.paired:
                chains[name + str(k)] = Gather(block, pair, n, name != "a")
            else:
                v[name + str(k)] = lax.all_gather(block, AXIS, axis=0, tiled=True)
    lookup = offset_lookup()
    base = jnp.einsum("bkc,ch->hbk", lookup, bias_table, precision=HIGHEST)
    state["base"] = [base]

    def gathered(name, layout):
        if not layout.paired:
            return [v[name + "0"]]
        found = []
        for k in range(len(layout.cuts)):
            found += chains[name + str(k)].finish()
        return found

    def tied(value):
        return after(value, *state["last"])

    def scatter(name, parts):
        if lay[name].paired:
            chains[name] = Scatter(*parts, lay[name].orders[0], n)
        else:
            v[name] = lax.psum_scatter(parts[0].astype(F32), AXIS, scatter_dimension=0, tiled=True)

    def run(name):
        if name == "K1a":
            out = attention_early(lay_a, tied(tokens), segment_ids, base, gathered("a", lay_a), count)
            v["wa"], v["gain"], v["h1"], v["h1t"], *v["early"] = out
            return [out[8]]
        if name == "K1b":
            context, blocks_a = v["early"][4], gathered("a", lay_a)
            out = attention_late(
                lay_a, tied(v["h1"]), v["wa"], segment_ids, base, count, tokens, v["gain"], context, blocks_a
            )
            v["late"], (v["x1"], v["h2"], v["h2t"], v["wo"]) = out[:6], out[6:]
            return [v["h2"]]
        if name == "K2a":
            out = inner_forward(lay_i, lay["g"], tied(v["h2"]), cotangent, gathered("i", lay_i), hidden)
            v["z"], v["slope"], *parts = out
            scatter("g", parts)
            return parts[:1]
        if name == "K2ba":
            inner, outer = gathered("i", lay_i), gathered("f", lay_f)
            out = outer_backward(lay_i, lay_f, lay["h"], 0, part, tied(cotangent), v["h2t"], v["slope"], inner, outer)
            v["dh2"], *parts = out
            scatter("h", parts)
            return parts[:1]
        if name == "K2bb":
            more = (v["x1"], v["gain"], tied(v["dh2"]), v["early"][5], v["late"][5])
            inner, outer = gathered("i", lay_i), gathered("f", lay_f)
            out = outer_backward(
                lay_i, lay_f, lay["j"], part, hidden - part, cotangent, v["h2t"], v["slope"], inner, outer, more
            )
            v["dx1"], v["da"], v["dgain2"], *parts = out
            scatter("j", parts)
            return parts[:1]
        if name in ("K3a", "K3b"):
            late = name == "K3b"
            saved, target = v["late" if late else "early"], "pq"[late]
            out = scores_backward(lay[target], int(late), tied(v["da"]), v["wo"], *saved[:4], v["h1t"])
            v["grads" + target], v["table" + target], parts = out[:3], out[3], out[4:]
            scatter(target, parts)
            return parts[:1]
        if name == "K4":
            grads = (*v["gradsp"], *v["gradsq"])
            v["dx"], dgain1 = inputs_backward(tokens, tied(v["dx1"]), v["gain"], grads, v["wa"])
            diagonal = jnp.concatenate([v["tablep"], v["tableq"]], axis=0)
            table = jnp.einsum("hbk,bkc->ch", diagonal, lookup, precision=HIGHEST)
            small = jnp.concatenate([dgain1[0], v["dgain2"][0], table.reshape(-1)]).reshape(-1, LANES)
            if n & (n - 1):
                v["s"] = lax.psum(small, AXIS)
            else:
                chains["s"] = SumAll(small, n)
            return [v["dx"]]
        v["out"] = layer_output(lay_f, v["x1"], tied(v["z"]), gathered("f", lay_f))
        return [v["out"]]

    def exchange(names):
        active = [chains[name] for name in names if name in chains]
        if not active:
            return []
        arrived = [flight for chain in active for flight in chain.waits()]
        arrived = list(lax.optimization_barrier((*arrived, *state["last"])))
        for chain in active:
            chain.flights = [arrived.pop(0) for _ in chain.waits()]
        jobs = [chain.job() for chain in active]
        wanted = [job for job in jobs if job]
        apart = len(wanted) == 1 and wanted[0][0] == "sum" and wanted[0][4] == BF16
        large = len(wanted) == 1 and wanted[0][2] * math.prod(wanted[0][1][0].shape[1:]) >= MIB // 2
        made = list(do_round(wanted)) if len(wanted) >= 3 or large or apart else []
        sent = []
        for chain, job in zip(active, jobs):
            sent += chain.advance(made.pop(0) if job and made else None)
        return sent

    for names in SCHEDULE:
        if isinstance(names, str):
            state["last"] = run(names)
        else:
            state["last"] = list(exchange(names) or state["last"]) + state.pop("base", [])

    def total(name):
        if name not in chains:
            return v[name]
        return chains[name].finish()

    small = total("s").reshape(-1)
    start = lax.axis_index(AXIS) * rows
    joined = jnp.concatenate([total("p"), total("q")], axis=1)

    def projection(j):
        groups = range(j * GROUP, 3 * width, 3 * GROUP)
        return jnp.concatenate([joined[:, low : low + GROUP] for low in groups], axis=1)

    return (
        v["out"],
        v["dx"],
        lax.dynamic_slice(small, (start,), (rows,)),
        projection(0),
        projection(1),
        projection(2),
        total("j")[:, hidden - part :],
        lax.dynamic_slice(small, (width + start,), (rows,)),
        jnp.concatenate([total("h"), total("j")[:, : hidden - part]], axis=1),
        total("g"),
        small[2 * width :].reshape(NB, HEADS),
    )


def solution(mesh):
    n = mesh.shape[AXIS]
    matrix, vector = P(AXIS, None), P(AXIS)
    return jax.shard_map(
        functools.partial(per_device, n),
        mesh=mesh,
        in_specs=(
            matrix,
            vector,
            matrix,
            matrix,
            matrix,
            matrix,
            vector,
            matrix,
            matrix,
            P(),
            vector,
            vector,
            matrix,
        ),
        out_specs=(
            matrix,
            matrix,
            vector,
            matrix,
            matrix,
            matrix,
            matrix,
            vector,
            matrix,
            matrix,
            P(),
        ),
        check_vma=False,
    )
```

```python
import functools
import math

import jax
import jax.numpy as jnp
from jax import lax
from jax.experimental import pallas as pl
from jax.experimental.pallas import tpu as pltpu
from jax.sharding import PartitionSpec as P

AXIS = "fsdp"
HEADS = 16
HEAD = 64
NB = 32
SEQ = 256
SPAN = 2 * SEQ
LANES = 128
GROUP = 256
EPSILON = 1e-06
MASKED = -1000000000.0
LIMITS = (12, 16, 23, 32, 46, 64, 91)
HIGHEST = lax.Precision.HIGHEST
BF16 = jnp.bfloat16
F32 = jnp.float32
MIB = 1 << 20
VMEM_LIMIT = 62 * MIB
VMEM_ALL = 64 * MIB - MIB // 4
ORDERS = {
    "a0": ("zZyx", "Zzxy"),
    "a1": ("Zxzy", "xyZz"),
    "i0": ("yZxz", "xZzy"),
    "i1": ("Zzxy", "zxyZ"),
    "f0": ("zZxy", "Zyxz"),
    "g": ("xZzy", "yZxz"),
    "h": ("Zxzy", "Zxzy"),
    "j": ("zZyx", "Zzxy"),
    "p": ("Zxyz", "zyxZ"),
    "q": ("zZyx", "Zzxy"),
}
SPLIT = {"a": 67, "i": 67}
SCHEDULE = (
    ("a0", "a1"),
    ("a0", "a1", "i0", "i1"),
    ("a0", "a1", "i0", "i1", "f0"),
    ("a0", "a1"),
    ("a0", "a1", "i0", "i1", "f0"),
    "K1a",
    ("i0", "i1", "f0"),
    "K1b",
    ("i0", "i1"),
    ("f0",),
    "K2a",
    ("f0",),
    ("f0", "g"),
    "K2ba",
    ("g", "h"),
    "K2bb",
    ("g", "h", "j"),
    "K3a",
    ("g", "h", "j", "p"),
    "K3b",
    ("h", "j", "p", "q"),
    ("g",),
    "K4",
    ("q", "g", "h", "j", "s"),
    ("p",),
    "K5",
    ("h", "j", "p", "q", "s"),
    ("j", "p", "q", "s"),
    ("p", "q", "s"),
    ("s",),
)
ROUND_COST = pl.CostEstimate(flops=50_000_000_000, transcendentals=0, bytes_accessed=0)
ANY = pl.BlockSpec(memory_space=pl.ANY)
VM = pl.BlockSpec(memory_space=pltpu.VMEM)


def no_time(**_):
    return pl.CostEstimate(flops=0, transcendentals=0, bytes_accessed=0)


def bucket_of(relative):
    distance = jnp.abs(relative)
    counted = jnp.zeros_like(distance)
    for threshold in LIMITS:
        counted = counted + (distance >= threshold).astype(jnp.int32)
    inside = jnp.where(distance < 8, distance, 8 + counted)
    return inside + jnp.where(relative > 0, 16, 0).astype(jnp.int32)


def offset_lookup():
    k = lax.broadcasted_iota(jnp.int32, (8, SPAN, NB), 1)
    b = lax.broadcasted_iota(jnp.int32, (8, SPAN, NB), 0)
    c = lax.broadcasted_iota(jnp.int32, (8, SPAN, NB), 2)
    offset = k - b
    offset = jnp.where(offset >= SEQ, offset - SPAN, offset)
    return (bucket_of(offset) == c).astype(F32)


def bit_orders(n, rows, wanted):
    if n & (n - 1) or n < 8 or rows % 16:
        return {name: None for name in wanted}
    high = list(range(1, n.bit_length() - 1))
    if n == 32:
        number = {"x": 1, "y": 2, "z": 3, "Z": 4}
        return {name: tuple([number[c] for c in order] + [0] for order in pair) for name, pair in wanted.items()}
    return {name: (high + [0], high[1:] + high[:1] + [0]) for name in wanted}


def swap(array, bits, n):
    return lax.ppermute(array, AXIS, [(i, i ^ (1 << bits[i & 1])) for i in range(n)])


def relative(bits, t):
    return sum(1 << b for k, b in enumerate(bits) if (t >> k) & 1)


def block_row(me, orders, t, n, rows):
    one, two = (relative(order, t) for order in (orders if t < n // 2 else orders[::-1]))
    return pl.multiple_of((me ^ (one + (me & 1) * (two - one))) * rows, rows)


def after(value, *others):
    return lax.optimization_barrier((value, *others))[0] if others else value


def round_kernel(plan, *refs):
    count = sum(len(kinds) for _, kinds in plan)
    inputs, outs = list(refs[:count]), refs[count:]
    for (kind, kinds), out in zip(plan, outs):
        terms = [inputs.pop(0) for _ in kinds]
        if kind == "join":
            half = terms[0].shape[0]
            out[:half] = terms[0][...]
            out[half:] = terms[1][...]
        elif kind == "small" and len(terms) == 4:
            out[...] = (terms[0][...] + terms[1][...]) + (terms[2][...] + terms[3][...])
        else:
            total = terms[0][...].astype(F32)
            for term in terms[1:]:
                total = total + term[...].astype(F32)
            out[...] = total.astype(out.dtype)


def do_round(jobs):
    plan, specs, arrays, shapes, out_specs = [], [], [], [], []
    moved = 0
    for kind, terms, size, index, dtype in jobs:
        if kind == "small":
            specs += [pl.BlockSpec(term.shape, lambda i: (0, 0)) for term in terms]
            shapes.append(jax.ShapeDtypeStruct(terms[0].shape, dtype))
            out_specs.append(specs[-1])
        else:
            rows, cols = terms[0].shape[1] // 2, terms[0].shape[2]
            specs += [pl.BlockSpec((size, rows, cols), lambda i, k=index: (k, i, 0)) for _ in terms]
            made = 2 * size if kind == "join" else size
            shapes.append(jax.ShapeDtypeStruct((made, 2 * rows, cols), dtype))
            out_specs.append(pl.BlockSpec((made, rows, cols), lambda i: (0, i, 0)))
            moved += 2 * (len(terms) + 1) * size * 2 * rows * cols
        plan.append((kind, (0,) * len(terms)))
        arrays += terms
    return pl.pallas_call(
        functools.partial(round_kernel, tuple(plan)),
        grid=(2,),
        out_shape=shapes,
        in_specs=specs,
        out_specs=out_specs,
        compiler_params=pltpu.CompilerParams(vmem_limit_bytes=VMEM_LIMIT),
        cost_estimate=ROUND_COST,
        name="exchange_round",
    )(*arrays)


class Gather:
    def __init__(self, own, orders, n, early):
        self.have, self.orders, self.n, self.last = own[None], orders, n, len(orders[0]) - 1
        self.step, self.parts, self.flights, self.early = 0, None, [self.have], early

    def waits(self):
        return self.flights

    def job(self):
        if 0 < self.step < self.last:
            return "join", [self.have, self.flights[0]], self.have.shape[0], 0, BF16
        return None

    def advance(self, made=None):
        if self.step > self.last:
            self.parts = [self.have, self.far, *self.near, *self.flights]
            return self.flights
        bits = [order[self.step] for order in self.orders]
        core = [order[self.last] for order in self.orders]
        if self.step == self.last:
            self.far, *self.near = self.flights
            self.flights = [swap(self.far, bits, self.n)]
            if not self.near:
                self.flights.insert(0, swap(after(self.have, self.far), bits, self.n))
        else:
            if self.step == 0:
                self.have = self.flights[0]
            else:
                self.have = jnp.concatenate([self.have, self.flights[0]], axis=0) if made is None else made
            self.flights = [swap(self.have, bits, self.n)]
            if self.early and self.step == self.last - 1:
                self.flights.append(swap(self.have, core, self.n))
        self.step += 1
        return [self.far if self.step > self.last else self.have]

    def finish(self):
        while self.parts is None:
            self.advance()
        return self.parts


class Scatter:
    def __init__(self, send, keep, orders, n):
        self.orders, self.n, self.step = orders, n, len(orders[0]) - 1
        self.terms, self.flights, self.result = [keep], [send], None
        self.first = self.step

    def waits(self):
        return self.flights

    def job(self):
        if self.step == self.first:
            return None
        half = 1 << max(self.step, 0)
        return "sum", self.terms + self.flights, half, int(self.step >= 0), BF16 if self.step >= 0 else F32

    def advance(self, made=None):
        send = self.flights[0]
        if self.step < self.first:
            _, terms, half, index, dtype = self.job()
            send = sum(term[half * index : half * (index + 1)].astype(F32) for term in terms) if made is None else made
            self.terms = terms
            if self.step < 0:
                self.result = send[0]
                return [send]
        send = send.astype(BF16)
        self.flights = [swap(send, [order[self.step] for order in self.orders], self.n)]
        self.step -= 1
        return [send]

    def finish(self):
        while self.result is None:
            self.advance()
        return self.result


class SumAll:
    def __init__(self, values, n):
        bits = list(range(n.bit_length() - 1))
        self.masks = [(1 << b,) for b in bits[:-3]] + [tuple(m << bits[-3] for m in (1, 2, 3)), (1 << bits[-1],)]
        self.values, self.n, self.step, self.result, self.flights = values, n, 0, None, [values]

    def waits(self):
        return self.flights

    def job(self):
        return ("small", [self.values, *self.flights], 0, 0, F32) if self.step else None

    def advance(self, made=None):
        if self.step == 0:
            (self.values,) = self.flights
        elif made is None:
            self.values = self.total()
        else:
            self.values = made
        if self.step == len(self.masks):
            self.result = self.values
        else:
            pairs = [[(i, i ^ mask) for i in range(self.n)] for mask in self.masks[self.step]]
            self.flights = [lax.ppermute(self.values, AXIS, pair) for pair in pairs]
        self.step += 1
        return [self.values]

    def total(self):
        if len(self.flights) == 1:
            return self.values + self.flights[0]
        one, two, three = self.flights
        return (self.values + one) + (two + three)

    def finish(self):
        while self.result is None:
            self.advance()
        return self.result


class Layout:
    def __init__(self, n, rows, cuts, orders):
        self.n, self.rows = n, rows
        self.cuts, self.orders = cuts, orders
        self.paired = orders[0] is not None

    def spans(self):
        return tuple(zip((0,) + tuple(self.cuts[:-1]), self.cuts))

    def count(self):
        return 4 * len(self.cuts) if self.paired else 1

    def load(self, me, refs, full, sems, first=0, cols=None, chunk=None):
        size = full.shape[0]
        begin, end = cols or (0, self.cuts[-1])
        chunk = chunk or size
        if not self.paired:
            waits = []
            for c in range(size // chunk):
                source = refs[0].at[first + c * chunk : first + (c + 1) * chunk, begin:end]
                copy = pltpu.make_async_copy(source, full.at[c * chunk : (c + 1) * chunk], sems.at[c])
                copy.start()
                waits.append(copy.wait)
            return waits
        whole_rows = size == self.n * self.rows
        for s, ((lo, hi), orders) in enumerate(zip(self.spans(), self.orders)):
            low, high = max(lo, begin), min(hi, end)
            if low >= high:
                continue
            for t in range(self.n):
                ref = refs[4 * s + t // (self.n // 4)].at[t % (self.n // 4), :, low - lo : high - lo]
                row = block_row(me, orders, t, self.n, self.rows)

                def start(row, ref=ref, low=low, high=high):
                    target = full.at[pl.ds(row, self.rows), low - begin : high - begin]
                    sem = sems.at[0 if chunk == size else lax.div(row, chunk)]
                    pltpu.make_async_copy(ref, target, sem).start()

                if whole_rows:
                    start(row)
                else:
                    row = pl.multiple_of(row - first, self.rows)
                    pl.when(jnp.logical_and(row >= 0, row < size))(functools.partial(start, row))
        def wait(c):
            view = full.at[c * chunk : (c + 1) * chunk]
            pltpu.make_async_copy(view, view, sems.at[c]).wait()

        return [functools.partial(wait, c) for c in range(size // chunk)]

    def out_shapes(self):
        if not self.paired:
            return [jax.ShapeDtypeStruct((self.n * self.rows, self.cuts[-1]), BF16)]
        return [jax.ShapeDtypeStruct((self.n // 2, self.rows, self.cuts[-1]), BF16)] * 2

    def store(self, me, stage, refs, sem, cols=None):
        begin, end = cols or (0, self.cuts[-1])
        if not self.paired:
            copy = pltpu.make_async_copy(stage.at[:, begin:end], refs[0].at[:, begin:end], sem)
            copy.start()
            return copy.wait
        half = self.n // 2
        for t in [*range(half, self.n), *range(half)]:
            row = block_row(me, self.orders[0], t, self.n, self.rows)
            target = refs[0 if t >= half else 1].at[t % half, :, begin:end]
            pltpu.make_async_copy(stage.at[pl.ds(row, self.rows), begin:end], target, sem).start()
        view = stage.at[:, begin:end]
        return pltpu.make_async_copy(view, view, sem).wait


def dot(a, b):
    return lax.dot_general(a, b, (((1,), (0,)), ((), ())), preferred_element_type=F32)


def dot_nt(a, b):
    return lax.dot_general(a, b, (((1,), (1,)), ((), ())), preferred_element_type=F32)


def dot_tn(a, b):
    return lax.dot_general(a, b, (((0,), (0,)), ((), ())), preferred_element_type=F32)


def row_scale(values):
    return lax.rsqrt(jnp.mean(values * values, axis=-1, keepdims=True) + EPSILON)


def toeplitz(base):
    return jnp.concatenate(
        [(pltpu.roll(base, 8 * a, 1) if a else base)[:, :SEQ] for a in range(SEQ // 8)], axis=0
    )


def diagonals(scores):
    total = None
    for a in range(SEQ // 8):
        rows = scores[8 * a : 8 * a + 8]
        rows = jnp.concatenate([rows, jnp.zeros((8, SPAN - SEQ), F32)], axis=1)
        if a:
            rows = pltpu.roll(rows, SPAN - 8 * a, 1)
        total = rows if total is None else total + rows
    return total


def transposed(values):
    return values.T


def copy_out(copies, sems, k, source, target):
    copy = pltpu.make_async_copy(source, target, sems.at[k])
    copy.start()
    copies.append(copy)


def pack_kernel(spans, *refs):
    q_ref, k_ref, v_ref, o_ref, one_ref, two_ref = refs[:6]
    rows, width = q_ref.shape
    line = lax.broadcasted_iota(jnp.int32, (LANES, rows), 0)
    gains = jnp.where(line == 0, one_ref[...], jnp.where(line == 1, two_ref[...], 0.0)).T
    for (low, high), out in zip(spans, refs[6:]):
        for k, ref in enumerate((q_ref, k_ref, v_ref, o_ref, gains)):
            begin, end = max(low, k * width), min(high, k * width + ref.shape[1])
            if begin < end:
                out[:, begin - low : end - low] = ref[:, begin - k * width : end - k * width].astype(BF16)


def pack(lay, weights, gains):
    rows = weights[0].shape[0]
    return pl.pallas_call(
        functools.partial(pack_kernel, lay.spans()),
        out_shape=[jax.ShapeDtypeStruct((rows, high - low), BF16) for low, high in lay.spans()],
        in_specs=[VM] * 6,
        out_specs=[VM] * len(lay.cuts),
        name="pack",
    )(*weights, *(gain.reshape(1, rows) for gain in gains))


def attend(seqs, h1, weights, segments_ref, base_ref, q_ref, k_ref, v_ref, p_ref, c_ref, ct_ref):
    for ref, weight in zip((q_ref, k_ref, v_ref), weights):
        ref[...] = dot(h1, weight).astype(BF16)
    first = lax.broadcasted_iota(jnp.int32, (SEQ, LANES), 1) < HEAD
    for p in range(GROUP // LANES):
        lanes = slice(p * LANES, (p + 1) * LANES)
        biases = [toeplitz(base_ref[2 * p + o]) for o in range(2)]
        for s in range(seqs):
            rows = slice(s * SEQ, (s + 1) * SEQ)
            q2, k2, v2 = q_ref[rows, lanes], k_ref[rows, lanes], v_ref[rows, lanes]
            line = jnp.broadcast_to(segments_ref[s : s + 1, :], (SEQ, SEQ))
            allowed = line.T == line
            made = []
            for o in range(2):
                mine = jnp.where(first == (o == 0), q2, jnp.zeros_like(q2))
                scores = jnp.where(allowed, dot_nt(mine, k2) + biases[o], MASKED)
                exponent = jnp.exp(scores - jnp.max(scores, axis=-1, keepdims=True))
                prob = exponent * (1.0 / jnp.sum(exponent, axis=-1, keepdims=True))
                p_ref[s, 2 * p + o] = prob
                made.append(dot(prob.astype(BF16), v2))
            c_ref[rows, lanes] = jnp.where(first, made[0], made[1]).astype(BF16)
    ct_ref[...] = transposed(c_ref[...])


def early_kernel(lay, seqs, width, steps, *refs):
    m = lay.count()
    x_ref, segments_ref, base_ref = refs[:3]
    blocks = refs[3 : 3 + m]
    wa_out, gain_ref, h1_ref, h1t_ref = refs[3 + m : 7 + m]
    outs = refs[7 + m : 13 + m]
    wa, gains_s, sems = refs[13 + m :]
    step = pl.program_id(0)

    @pl.when(step == 0)
    def _():
        me = lax.axis_index(AXIS)
        waits = lay.load(me, blocks, gains_s, sems.at[0:1], cols=(4 * width, 4 * width + LANES))
        for j in range(3):
            cols = (j * width, (j + 1) * width)
            waits += lay.load(me, blocks, wa.at[:, j * width : (j + 1) * width], sems.at[1 + j : 2 + j], cols=cols)
        waits[0]()
        gains = gains_s[...].astype(F32).T
        gain_ref[...] = gains[:8]
        x = x_ref[...].astype(F32)
        h1 = (x * row_scale(x) * gains[0:1]).astype(BF16)
        h1_ref[...] = h1
        h1t_ref[...] = transposed(h1)
        for wait in waits[1:]:
            wait()
        pltpu.make_async_copy(wa, wa_out, sems.at[0]).start()

    weights = [wa[:, pl.ds(pl.multiple_of(j * width + step * GROUP, GROUP), GROUP)] for j in range(3)]
    attend(seqs, h1_ref[...], weights, segments_ref, base_ref, *outs)

    @pl.when(step == steps - 1)
    def _():
        pltpu.make_async_copy(wa, wa_out, sems.at[0]).wait()


def late_kernel(lay, seqs, steps, *refs):
    m = lay.count()
    h1_ref, wq_ref, wk_ref, wv_ref, segments_ref, base_ref, x_ref, gain_ref, context_ref = refs[:9]
    blocks = refs[9 : 9 + m]
    outs, (x1_ref, h2_ref, h2t_ref, wo_out) = refs[9 + m : 15 + m], refs[15 + m : 19 + m]
    context, wo_ref, sems = refs[19 + m :]
    step = pl.program_id(0)
    width = x_ref.shape[1]

    @pl.when(step == 0)
    def _():
        lay.load(lax.axis_index(AXIS), blocks, wo_ref, sems.at[0:1], cols=(3 * width, 4 * width))

    attend(seqs, h1_ref[...], (wq_ref[...], wk_ref[...], wv_ref[...]), segments_ref, base_ref, *outs)
    context[:, pl.ds(pl.multiple_of(step * GROUP, GROUP), GROUP)] = outs[4][...]

    @pl.when(step == steps - 1)
    def _():
        pltpu.make_async_copy(wo_ref, wo_ref, sems.at[0]).wait()
        copy = pltpu.make_async_copy(wo_ref, wo_out, sems.at[1])
        copy.start()
        early = context_ref.shape[1]
        for c in range(0, width, 512):
            cols = slice(c, c + 512)
            x1_ref[:, cols] = (
                x_ref[:, cols].astype(F32)
                + dot(context_ref[...], wo_ref[:early, cols])
                + dot(context[...], wo_ref[early:, cols])
            )
        x1 = x1_ref[...]
        h2 = (x1 * row_scale(x1) * gain_ref[1:2, :]).astype(BF16)
        h2_ref[...] = h2
        h2t_ref[...] = transposed(h2)
        copy.wait()


def attention_outputs(tokens, width, count):
    sds = jax.ShapeDtypeStruct
    seqs, heads = tokens // SEQ, GROUP // HEAD
    shapes = [sds((tokens, count * GROUP), BF16)] * 3
    specs = [pl.BlockSpec((tokens, GROUP), lambda i: (0, i))] * 3
    shapes.append(sds((seqs, count * heads, SEQ, SEQ), F32))
    specs.append(pl.BlockSpec((seqs, heads, SEQ, SEQ), lambda i: (0, i, 0, 0)))
    shapes.append(sds((tokens, count * GROUP), BF16))
    specs.append(pl.BlockSpec((tokens, GROUP), lambda i: (0, i)))
    shapes.append(sds((count * GROUP, tokens), BF16))
    specs.append(pl.BlockSpec((GROUP, tokens), lambda i: (i, 0)))
    return shapes, specs


def whole(shape):
    return pl.BlockSpec(shape, lambda i: (0,) * len(shape))


def attention_cost(tokens, width, count):
    share = count * GROUP
    return no_time(
        flops=2 * tokens * width * 3 * share + 16 * tokens * SEQ * share,
        transcendentals=tokens * SEQ * share // HEAD,
        bytes_accessed=(6 * width * share + 8 * tokens * share + 4 * tokens * SEQ * share // HEAD),
    )


def attention_early(lay, x, segments, base, blocks, count):
    tokens, width = x.shape
    seqs, wide, heads = tokens // SEQ, 3 * width, GROUP // HEAD
    sds = jax.ShapeDtypeStruct
    shapes, specs = attention_outputs(tokens, width, count)
    return pl.pallas_call(
        functools.partial(early_kernel, lay, seqs, width, count),
        grid=(count,),
        out_shape=[sds((width, wide), BF16), sds((8, width), F32), sds((tokens, width), BF16), sds((width, tokens), BF16)]
        + shapes,
        in_specs=[
            whole((tokens, width)),
            whole((seqs, SEQ)),
            pl.BlockSpec((heads, 8, SPAN), lambda i: (i, 0, 0)),
        ]
        + [ANY] * len(blocks),
        out_specs=[ANY, whole((8, width)), whole((tokens, width)), whole((width, tokens))] + specs,
        scratch_shapes=[
            pltpu.VMEM((width, wide), BF16),
            pltpu.VMEM((width, LANES), BF16),
            pltpu.SemaphoreType.DMA((4,)),
        ],
        compiler_params=pltpu.CompilerParams(vmem_limit_bytes=VMEM_LIMIT),
        cost_estimate=attention_cost(tokens, width, count),
        name="attention_early",
    )(x, segments.reshape(seqs, SEQ), base, *blocks)


def attention_late(lay, h1, wa, segments, base, count, x, gain, context, blocks):
    tokens, width = h1.shape
    seqs, heads, skip = tokens // SEQ, GROUP // HEAD, width // GROUP - count
    shapes, specs = attention_outputs(tokens, width, count)
    per = width // GROUP
    sds = jax.ShapeDtypeStruct
    return pl.pallas_call(
        functools.partial(late_kernel, lay, seqs, count),
        grid=(count,),
        out_shape=shapes
        + [sds((tokens, width), F32), sds((tokens, width), BF16), sds((width, tokens), BF16), sds((width, width), BF16)],
        in_specs=[whole((tokens, width))]
        + [pl.BlockSpec((width, GROUP), lambda i, j=j: (0, j * per + skip + i)) for j in range(3)]
        + [
            whole((seqs, SEQ)),
            pl.BlockSpec((heads, 8, SPAN), lambda i: (skip + i, 0, 0)),
            whole((tokens, width)),
            whole((8, width)),
            whole(context.shape),
        ]
        + [ANY] * len(blocks),
        out_specs=specs + [whole((tokens, width)), whole((tokens, width)), whole((width, tokens)), ANY],
        scratch_shapes=[
            pltpu.VMEM((tokens, count * GROUP), BF16),
            pltpu.VMEM((width, width), BF16),
            pltpu.SemaphoreType.DMA((2,)),
        ],
        compiler_params=pltpu.CompilerParams(vmem_limit_bytes=VMEM_LIMIT),
        cost_estimate=attention_cost(tokens, width, count),
        name="attention_late",
    )(h1, wa, wa, wa, segments.reshape(seqs, SEQ), base, x, gain, context, *blocks)


def inner_kernel(lay, lay_out, chunk, *refs):
    m, k = lay.count(), len(lay_out.out_shapes())
    h2_ref, e_ref = refs[:2]
    blocks = refs[2 : 2 + m]
    z_out, g_out = refs[2 + m : 4 + m]
    grads = refs[4 + m : 4 + m + k]
    wi, z_s, g_s, stage, lsem, osem, gsem = refs[4 + m + k :]
    me = lax.axis_index(AXIS)
    hidden = wi.shape[1]
    parts = 4
    size = hidden // parts
    waits = []
    for p in range(parts):
        cols = (p * size, (p + 1) * size)
        waits += lay.load(me, blocks, wi.at[:, p * size : (p + 1) * size], lsem.at[p : p + 1], cols=cols)

    def step(c, carry):
        cols = pl.ds(pl.multiple_of(c * chunk, chunk), chunk)
        u = dot(h2_ref[...], wi[:, cols])
        cdf = 0.5 * (1.0 + lax.erf(u * (1.0 / math.sqrt(2.0))))
        z = (u * cdf).astype(BF16)
        z_s[:, cols] = z
        g_s[:, cols] = cdf + u * jnp.exp(-0.5 * u * u) * (1.0 / math.sqrt(2.0 * math.pi))
        stage[cols, :] = dot(transposed(z), e_ref[...]).astype(BF16)
        pltpu.make_async_copy(z_s.at[:, cols], z_out.at[:, cols], osem.at[0]).start()
        pltpu.make_async_copy(g_s.at[:, cols], g_out.at[:, cols], osem.at[1]).start()
        return carry

    for p in range(parts):
        waits[p]()
        lax.fori_loop(p * size // chunk, (p + 1) * size // chunk, step, 0)
    done = lay_out.store(me, stage, grads, gsem)
    pltpu.make_async_copy(z_s, z_out, osem.at[0]).wait()
    pltpu.make_async_copy(g_s, g_out, osem.at[1]).wait()
    done()


def inner_forward(lay, lay_out, h2, cotangent, blocks, hidden):
    tokens, width = h2.shape
    sds = jax.ShapeDtypeStruct
    grads = lay_out.out_shapes()
    return pl.pallas_call(
        functools.partial(inner_kernel, lay, lay_out, 512),
        out_shape=[sds((tokens, hidden), BF16), sds((tokens, hidden), F32)] + grads,
        in_specs=[VM] * 2 + [ANY] * len(blocks),
        out_specs=[ANY] * (2 + len(grads)),
        scratch_shapes=[
            pltpu.VMEM((width, hidden), BF16),
            pltpu.VMEM((tokens, hidden), BF16),
            pltpu.VMEM((tokens, hidden), F32),
            pltpu.VMEM((hidden, width), BF16),
            pltpu.SemaphoreType.DMA((4,)),
            pltpu.SemaphoreType.DMA((2,)),
            pltpu.SemaphoreType.DMA,
        ],
        compiler_params=pltpu.CompilerParams(vmem_limit_bytes=VMEM_LIMIT),
        cost_estimate=no_time(
            flops=4 * tokens * width * hidden, transcendentals=2 * tokens * hidden, bytes_accessed=32 * MIB
        ),
        name="feedforward_inner",
    )(h2, cotangent, *blocks)


def outer_kernel(lay_i, lay_f, lay_g, chunk, first, last, *refs):
    mi, mf = lay_i.count(), lay_f.count()
    e_ref, h2t_ref, g_in = refs[:3]
    at = 3
    if last:
        x1_ref, gain_ref, dh_ref = refs[3:6]
        contexts = refs[6:8]
        at = 8
    inner, outer = refs[at : at + mi], refs[at + mi : at + mi + mf]
    at += mi + mf
    dx1_ref, at = refs[at], at + 1
    if last:
        da_ref, dgain_ref = refs[at : at + 2]
        at += 2
    kg = len(lay_g.out_shapes())
    grads, at = refs[at : at + kg], at + kg
    wi, wf, g_s, stage, fsem, lsem, isem, gsem = refs[at:]
    me = lax.axis_index(AXIS)
    size = wi.shape[1]
    steps = size // chunk
    outer_waits = lay_f.load(me, outer, wf, fsem, first=first, chunk=chunk)
    copies, inner_waits = [], []
    for c in range(steps):
        source = g_in.at[:, first + c * chunk : first + (c + 1) * chunk]
        copies.append(pltpu.make_async_copy(source, g_s.at[:, c * chunk : (c + 1) * chunk], isem.at[c]))
        copies[-1].start()
    wide = 2 * chunk
    for c in range(size // wide):
        target = wi.at[:, c * wide : (c + 1) * wide]
        cols = (first + c * wide, first + (c + 1) * wide)
        inner_waits += lay_i.load(me, inner, target, lsem.at[c : c + 1], cols=cols)
    e = e_ref[...]
    for c in range(steps):
        cols = slice(c * chunk, (c + 1) * chunk)
        outer_waits[c]()
        copies[c].wait()
        du = (dot_nt(e, wf[cols, :]) * g_s[:, cols]).astype(BF16)
        stage[:, cols] = dot(h2t_ref[...], du).astype(BF16)
        if c % 2 == 0:
            inner_waits[c // 2]()
        part = dot_nt(du, wi[:, cols])
        if c == 0:
            dx1_ref[...] = part + dh_ref[...] if last else part
        else:
            dx1_ref[...] += part
    if last:
        dh2 = dx1_ref[...]
        x1 = x1_ref[...]
        gain = gain_ref[1:2, :]
        scale = row_scale(x1)
        dgain_ref[...] = jnp.broadcast_to(jnp.sum(dh2 * (x1 * scale), axis=0, keepdims=True), dgain_ref.shape)
        mean = jnp.mean(x1 * gain * dh2, axis=-1, keepdims=True)
        dx1 = e.astype(F32) + scale * gain * dh2 - x1 * (scale * scale * scale) * mean
        dx1_ref[...] = dx1
        da = dx1.astype(BF16)
        da_ref[...] = da
        rows = stage.shape[0] // 2
        for p, context in enumerate(contexts):
            stage[p * rows : (p + 1) * rows, size:] = dot(context[...], da).astype(BF16)
    lay_g.store(me, stage, grads, gsem)()


def outer_backward(lay_i, lay_f, lay_g, first, size, cotangent, h2t, g, inner, outer, more=()):
    tokens, width = cotangent.shape
    chunk = 512
    last = first > 0
    sds = jax.ShapeDtypeStruct
    out_shape = [sds((tokens, width), F32)]
    out_specs = [VM]
    if last:
        out_shape += [sds((tokens, width), BF16), sds((8, width), F32)]
        out_specs += [VM] * 2
    grads = lay_g.out_shapes()
    return pl.pallas_call(
        functools.partial(outer_kernel, lay_i, lay_f, lay_g, chunk, first, last),
        out_shape=out_shape + grads,
        in_specs=[VM, VM, ANY] + [VM] * len(more) + [ANY] * (len(inner) + len(outer)),
        out_specs=out_specs + [ANY] * len(grads),
        scratch_shapes=[
            pltpu.VMEM((width, size), BF16),
            pltpu.VMEM((size, width), BF16),
            pltpu.VMEM((tokens, size), F32),
            pltpu.VMEM((width, lay_g.cuts[-1]), BF16),
            pltpu.SemaphoreType.DMA((size // chunk,)),
            pltpu.SemaphoreType.DMA((size // chunk // 2,)),
            pltpu.SemaphoreType.DMA((size // chunk,)),
            pltpu.SemaphoreType.DMA,
        ],
        compiler_params=pltpu.CompilerParams(vmem_limit_bytes=VMEM_LIMIT),
        cost_estimate=no_time(
            flops=6 * tokens * width * size + 2 * last * tokens * width * width,
            transcendentals=tokens,
            bytes_accessed=24 * MIB,
        ),
        name="feedforward_outer_" + "ab"[last],
    )(cotangent, h2t, g, *more, *inner, *outer)


def scores_kernel(lay, seqs, width, steps, *refs):
    k = len(lay.out_shapes())
    da_ref, wo_ref, q_ref, k_ref, v_ref, p_ref, h1t_ref = refs[:7]
    dq_ref, dk_ref, dv_ref, table_ref = refs[7:11]
    grads = refs[11 : 11 + k]
    dc, stage, gsem = refs[11 + k :]
    step = pl.program_id(0)
    dc[...] = dot_nt(da_ref[...], wo_ref[...]).astype(BF16)
    first = lax.broadcasted_iota(jnp.int32, (SEQ, LANES), 1) < HEAD
    for p in range(GROUP // LANES):
        lanes = slice(p * LANES, (p + 1) * LANES)
        totals = [None, None]
        for s in range(seqs):
            rows = slice(s * SEQ, (s + 1) * SEQ)
            dc2, q2, k2, v2 = dc[rows, lanes], q_ref[rows, lanes], k_ref[rows, lanes], v_ref[rows, lanes]
            made = []
            for o in range(2):
                prob = p_ref[s, 2 * p + o]
                mine = jnp.where(first == (o == 0), dc2, jnp.zeros_like(dc2))
                dprob = dot_nt(mine, v2)
                inner = jnp.sum(prob * dprob, axis=-1, keepdims=True)
                ds = (prob * (dprob - inner)).astype(BF16)
                wide = ds.astype(F32)
                totals[o] = wide if totals[o] is None else totals[o] + wide
                made.append(
                    (dot(ds, k2), dot(transposed(ds), q2), dot(transposed(prob.astype(BF16)), dc2))
                )
            for ref, one, two in zip((dq_ref, dk_ref, dv_ref), *made):
                ref[rows, lanes] = jnp.where(first, one, two).astype(BF16)
        for o in range(2):
            table_ref[2 * p + o] = diagonals(totals[o])
    for j, ref in enumerate((dq_ref, dk_ref, dv_ref)):
        col = pl.ds(pl.multiple_of((3 * step + j) * GROUP, GROUP), GROUP)
        stage[:, col] = dot(h1t_ref[...], ref[...]).astype(BF16)

    @pl.when(step == steps - 1)
    def _():
        lay.store(lax.axis_index(AXIS), stage, grads, gsem)()


def scores_backward(lay, part, da, wo, q, k, v, p, h1t):
    tokens, width = da.shape
    count = q.shape[1] // GROUP
    seqs, heads = tokens // SEQ, GROUP // HEAD
    sds = jax.ShapeDtypeStruct
    grads = lay.out_shapes()
    share = count * GROUP
    return pl.pallas_call(
        functools.partial(scores_kernel, lay, seqs, width, count),
        grid=(count,),
        out_shape=[sds((tokens, share), BF16)] * 3 + [sds((count * heads, 8, SPAN), F32)] + grads,
        in_specs=[whole((tokens, width)), pl.BlockSpec((GROUP, width), lambda i: (part * count + i, 0))]
        + [pl.BlockSpec((tokens, GROUP), lambda i: (0, i))] * 3
        + [pl.BlockSpec((seqs, heads, SEQ, SEQ), lambda i: (0, i, 0, 0)), whole((width, tokens))],
        out_specs=[pl.BlockSpec((tokens, GROUP), lambda i: (0, i))] * 3
        + [pl.BlockSpec((heads, 8, SPAN), lambda i: (i, 0, 0))]
        + [ANY] * len(grads),
        scratch_shapes=[
            pltpu.VMEM((tokens, GROUP), BF16),
            pltpu.VMEM((width, 3 * share), BF16),
            pltpu.SemaphoreType.DMA,
        ],
        compiler_params=pltpu.CompilerParams(vmem_limit_bytes=VMEM_ALL if part else VMEM_LIMIT),
        cost_estimate=no_time(
            flops=8 * tokens * width * share + 40 * tokens * SEQ * share,
            transcendentals=0,
            bytes_accessed=16 * MIB,
        ),
        name="attention_backward_" + "ab"[part],
    )(da, wo, q, k, v, p, h1t)


def inputs_kernel(width, parts, *refs):
    x_ref, dx1_ref, gain_ref = refs[:3]
    grads = refs[3 : 3 + 3 * parts]
    wa_in, dx_ref, dgain_ref, wa, dh, sem = refs[3 + 3 * parts :]
    copies = []
    for j in range(3):
        cols = slice(j * width, (j + 1) * width)
        copies.append(pltpu.make_async_copy(wa_in.at[:, cols], wa.at[:, cols], sem.at[j]))
        copies[-1].start()
    size = width // parts
    for j in range(3):
        copies[j].wait()
        for c in range(0, width, 512):
            for p in range(parts):
                low = j * width + p * size
                part = dot_nt(grads[3 * p + j][...], wa[c : c + 512, low : low + size])
                if j or p:
                    dh[:, c : c + 512] += part
                else:
                    dh[:, c : c + 512] = part
    x = x_ref[...].astype(F32)
    gain = gain_ref[0:1, :]
    scale = row_scale(x)
    dh1 = dh[...]
    dgain_ref[...] = jnp.broadcast_to(jnp.sum(dh1 * (x * scale), axis=0, keepdims=True), dgain_ref.shape)
    mean = jnp.mean(x * gain * dh1, axis=-1, keepdims=True)
    dx_ref[...] = (dx1_ref[...] + scale * gain * dh1 - x * (scale * scale * scale) * mean).astype(BF16)


def inputs_backward(x, dx1, gain, grads, wa):
    tokens, width = x.shape
    sds = jax.ShapeDtypeStruct
    return pl.pallas_call(
        functools.partial(inputs_kernel, width, len(grads) // 3),
        out_shape=[sds((tokens, width), BF16), sds((8, width), F32)],
        in_specs=[VM] * (3 + len(grads)) + [ANY],
        out_specs=[VM] * 2,
        scratch_shapes=[
            pltpu.VMEM((width, 3 * width), BF16),
            pltpu.VMEM((tokens, width), F32),
            pltpu.SemaphoreType.DMA((3,)),
        ],
        compiler_params=pltpu.CompilerParams(vmem_limit_bytes=VMEM_ALL),
        cost_estimate=no_time(
            flops=6 * tokens * width * width, transcendentals=tokens, bytes_accessed=16 * MIB
        ),
        name="inputs_backward",
    )(x, dx1, gain, *grads, wa)


def output_kernel(lay, *refs):
    m = lay.count()
    x1_ref, z_ref = refs[:2]
    blocks = refs[2 : 2 + m]
    out_ref, wf, sem = refs[2 + m :]
    lay.load(lax.axis_index(AXIS), blocks, wf, sem)[0]()
    width = wf.shape[1]
    for c in range(0, width, 512):
        cols = slice(c, c + 512)
        out_ref[:, cols] = (x1_ref[:, cols] + dot(z_ref[...], wf[:, cols])).astype(BF16)


def layer_output(lay, x1, z, blocks):
    tokens, width = x1.shape
    hidden = z.shape[1]
    return pl.pallas_call(
        functools.partial(output_kernel, lay),
        out_shape=jax.ShapeDtypeStruct((tokens, width), BF16),
        in_specs=[VM] * 2 + [ANY] * len(blocks),
        out_specs=VM,
        scratch_shapes=[
            pltpu.VMEM((hidden, width), BF16),
            pltpu.SemaphoreType.DMA((1,)),
        ],
        compiler_params=pltpu.CompilerParams(vmem_limit_bytes=VMEM_ALL),
        cost_estimate=no_time(
            flops=2 * tokens * width * hidden, transcendentals=0, bytes_accessed=16 * MIB
        ),
        name="layer_output",
    )(x1, z, *blocks)


def closing_kernel(count, *refs):
    terms, early_ref, outs = refs[:-4], refs[-4], refs[-3:]
    total = None
    for term in terms:
        value = term[0].astype(F32)
        total = value if total is None else total + value
    for j, out in enumerate(outs):
        for i in range(count):
            group = slice((3 * i + j) * GROUP, (3 * i + j + 1) * GROUP)
            out[:, i * GROUP : (i + 1) * GROUP] = early_ref[:, group]
            out[:, (count + i) * GROUP : (count + i + 1) * GROUP] = total[:, group]


def closing(terms, early):
    rows, share = early.shape
    count = share // (3 * GROUP)
    block = pl.BlockSpec((1, rows, share), lambda i: (0, 0, 0))
    width = 2 * count * GROUP
    return pl.pallas_call(
        functools.partial(closing_kernel, count),
        grid=(1,),
        out_shape=[jax.ShapeDtypeStruct((rows, width), F32)] * 3,
        in_specs=[block] * len(terms) + [whole((rows, share))],
        out_specs=[whole((rows, width))] * 3,
        cost_estimate=no_time(),
        name="projection_gradients",
    )(*terms, early)


def per_device(
    n,
    tokens,
    attention_gain,
    query_weight,
    key_weight,
    value_weight,
    output_weight,
    feedforward_gain,
    inner_weight,
    outer_weight,
    bias_table,
    segment_ids,
    positions,
    cotangent,
):
    del positions
    width = tokens.shape[1]
    hidden = inner_weight.shape[1]
    rows = query_weight.shape[0]
    orders = bit_orders(n, rows, ORDERS)
    wide = outer_weight.shape[0]
    count = width // GROUP // 2
    part = hidden // 4
    all_a = 4 * width + LANES
    def split(columns, name):
        pairs = tuple(orders[key] for key in ORDERS if key[:-1] == name)
        if len(pairs) < 2 or pairs[0] is None:
            return (columns,), pairs[:1]
        return (SPLIT[name] * columns // LANES // 100 * LANES, columns), pairs

    lay_a = Layout(n, rows, *split(all_a, "a"))
    lay_i = Layout(n, rows, *split(hidden, "i"))
    lay_f = Layout(n, wide, *split(width, "f"))
    lay = {
        "g": Layout(n, wide, (width,), (orders["g"],)),
        "h": Layout(n, rows, (part,), (orders["h"],)),
        "j": Layout(n, rows, (hidden - part + width,), (orders["j"],)),
        "p": Layout(n, rows, (3 * width // 2,), (orders["p"],)),
        "q": Layout(n, rows, (3 * width // 2,), (orders["q"],)),
    }
    chains, v, state = {}, {}, {"last": []}
    weights = (query_weight, key_weight, value_weight, output_weight)
    packed = pack(lay_a, weights, (attention_gain, feedforward_gain))
    blocks = {
        "a": packed,
        "i": [inner_weight[:, low:high].astype(BF16) for low, high in lay_i.spans()],
        "f": [outer_weight[:, low:high].astype(BF16) for low, high in lay_f.spans()],
    }
    for name, layout in (("a", lay_a), ("i", lay_i), ("f", lay_f)):
        for k, (block, pair) in enumerate(zip(blocks[name], layout.orders)):
            if layout.paired:
                chains[name + str(k)] = Gather(block, pair, n, name != "a")
            else:
                v[name + str(k)] = lax.all_gather(block, AXIS, axis=0, tiled=True)
    lookup = offset_lookup()
    base = jnp.einsum("bkc,ch->hbk", lookup, bias_table, precision=HIGHEST)
    state["base"] = [base]

    def gathered(name, layout):
        if not layout.paired:
            return [v[name + "0"]]
        found = []
        for k in range(len(layout.cuts)):
            found += chains[name + str(k)].finish()
        return found

    def tied(value):
        return after(value, *state["last"])

    def scatter(name, parts):
        if lay[name].paired:
            chains[name] = Scatter(*parts, lay[name].orders[0], n)
        else:
            v[name] = lax.psum_scatter(parts[0].astype(F32), AXIS, scatter_dimension=0, tiled=True)

    def run(name):
        if name == "K1a":
            out = attention_early(lay_a, tied(tokens), segment_ids, base, gathered("a", lay_a), count)
            v["wa"], v["gain"], v["h1"], v["h1t"], *v["early"] = out
            return [out[8]]
        if name == "K1b":
            context, blocks_a = v["early"][4], gathered("a", lay_a)
            out = attention_late(
                lay_a, tied(v["h1"]), v["wa"], segment_ids, base, count, tokens, v["gain"], context, blocks_a
            )
            v["late"], (v["x1"], v["h2"], v["h2t"], v["wo"]) = out[:6], out[6:]
            return [v["h2"]]
        if name == "K2a":
            out = inner_forward(lay_i, lay["g"], tied(v["h2"]), cotangent, gathered("i", lay_i), hidden)
            v["z"], v["slope"], *parts = out
            scatter("g", parts)
            return parts[:1]
        if name == "K2ba":
            inner, outer = gathered("i", lay_i), gathered("f", lay_f)
            out = outer_backward(lay_i, lay_f, lay["h"], 0, part, tied(cotangent), v["h2t"], v["slope"], inner, outer)
            v["dh2"], *parts = out
            scatter("h", parts)
            return parts[:1]
        if name == "K2bb":
            more = (v["x1"], v["gain"], tied(v["dh2"]), v["early"][5], v["late"][5])
            inner, outer = gathered("i", lay_i), gathered("f", lay_f)
            out = outer_backward(
                lay_i, lay_f, lay["j"], part, hidden - part, cotangent, v["h2t"], v["slope"], inner, outer, more
            )
            v["dx1"], v["da"], v["dgain2"], *parts = out
            scatter("j", parts)
            return parts[:1]
        if name in ("K3a", "K3b"):
            late = name == "K3b"
            saved, target = v["late" if late else "early"], "pq"[late]
            out = scores_backward(lay[target], int(late), tied(v["da"]), v["wo"], *saved[:4], v["h1t"])
            v["grads" + target], v["table" + target], parts = out[:3], out[3], out[4:]
            scatter(target, parts)
            return parts[:1]
        if name == "K4":
            grads = (*v["gradsp"], *v["gradsq"])
            v["dx"], dgain1 = inputs_backward(tokens, tied(v["dx1"]), v["gain"], grads, v["wa"])
            diagonal = jnp.concatenate([v["tablep"], v["tableq"]], axis=0)
            table = jnp.einsum("hbk,bkc->ch", diagonal, lookup, precision=HIGHEST)
            small = jnp.concatenate([dgain1[0], v["dgain2"][0], table.reshape(-1)]).reshape(-1, LANES)
            if n & (n - 1):
                v["s"] = lax.psum(small, AXIS)
            else:
                chains["s"] = SumAll(small, n)
            return [v["dx"]]
        v["out"] = layer_output(lay_f, v["x1"], tied(v["z"]), gathered("f", lay_f))
        return [v["out"]]

    def exchange(names):
        active = [chains[name] for name in names if name in chains]
        if not active:
            return []
        arrived = [flight for chain in active for flight in chain.waits()]
        arrived = list(lax.optimization_barrier((*arrived, *state["last"])))
        for chain in active:
            chain.flights = [arrived.pop(0) for _ in chain.waits()]
        jobs = [chain.job() for chain in active]
        wanted = [job for job in jobs if job]
        apart = len(wanted) == 1 and wanted[0][0] == "sum" and wanted[0][4] == BF16
        large = len(wanted) == 1 and wanted[0][2] * math.prod(wanted[0][1][0].shape[1:]) >= MIB // 2
        made = list(do_round(wanted)) if len(wanted) >= 3 or large or apart else []
        sent = []
        for chain, job in zip(active, jobs):
            sent += chain.advance(made.pop(0) if job and made else None)
        return sent

    for names in SCHEDULE:
        if isinstance(names, str):
            state["last"] = run(names)
        else:
            state["last"] = list(exchange(names) or state["last"]) + state.pop("base", [])

    def total(name):
        if name not in chains:
            return v[name]
        return chains[name].finish()

    small = total("s").reshape(-1)
    start = lax.axis_index(AXIS) * rows
    if "q" in chains and chains["q"].step < 0:
        projections = closing(chains["q"].terms + chains["q"].flights, total("p"))
    else:
        joined = jnp.concatenate([total("p"), total("q")], axis=1)
        groups = [range(j * GROUP, 3 * width, 3 * GROUP) for j in range(3)]
        projections = [jnp.concatenate([joined[:, low : low + GROUP] for low in lows], axis=1) for lows in groups]

    return (
        v["out"],
        v["dx"],
        lax.dynamic_slice(small, (start,), (rows,)),
        *projections,
        total("j")[:, hidden - part :],
        lax.dynamic_slice(small, (width + start,), (rows,)),
        jnp.concatenate([total("h"), total("j")[:, : hidden - part]], axis=1),
        total("g"),
        small[2 * width :].reshape(NB, HEADS),
    )


def solution(mesh):
    n = mesh.shape[AXIS]
    matrix, vector = P(AXIS, None), P(AXIS)
    return jax.shard_map(
        functools.partial(per_device, n),
        mesh=mesh,
        in_specs=(
            matrix,
            vector,
            matrix,
            matrix,
            matrix,
            matrix,
            vector,
            matrix,
            matrix,
            P(),
            vector,
            vector,
            matrix,
        ),
        out_specs=(
            matrix,
            matrix,
            vector,
            matrix,
            matrix,
            matrix,
            matrix,
            vector,
            matrix,
            matrix,
            P(),
        ),
        check_vma=False,
    )
```

```python
import functools
import math

import jax
import jax.numpy as jnp
from jax import lax
from jax.experimental import pallas as pl
from jax.experimental.pallas import tpu as pltpu
from jax.sharding import PartitionSpec as P

AXIS = "fsdp"
HEADS = 16
HEAD = 64
NB = 32
SEQ = 256
SPAN = 2 * SEQ
LANES = 128
GROUP = 256
EPSILON = 1e-06
MASKED = -1000000000.0
LIMITS = (12, 16, 23, 32, 46, 64, 91)
HIGHEST = lax.Precision.HIGHEST
BF16 = jnp.bfloat16
F32 = jnp.float32
MIB = 1 << 20
VMEM_LIMIT = 62 * MIB
VMEM_ALL = 64 * MIB - MIB // 4
ORDERS = {
    "a0": ("zZyx", "Zzxy"),
    "a1": ("Zxzy", "xyZz"),
    "i0": ("yZxz", "xZzy"),
    "i1": ("Zzxy", "zxyZ"),
    "f0": ("zZxy", "Zyxz"),
    "g": ("xZzy", "yZxz"),
    "h": ("Zxzy", "Zxzy"),
    "j": ("zZyx", "Zzxy"),
    "p": ("Zxyz", "zyxZ"),
    "q": ("zZyx", "Zzxy"),
}
SPLIT = {"a": 67, "i": 67}
SCHEDULE = (
    ("a0", "a1"),
    ("a0", "a1", "i0", "i1"),
    ("a0", "a1", "i0", "i1", "f0"),
    ("a0", "a1"),
    ("a0", "a1", "i0", "i1", "f0"),
    "K1a",
    ("i0", "i1", "f0"),
    "K1b",
    ("i0", "i1"),
    ("f0",),
    "K2a",
    ("f0",),
    ("f0", "g"),
    "K2ba",
    ("g", "h"),
    "K2bb",
    ("g", "h", "j"),
    "K3a",
    ("g", "h", "j", "p"),
    "K3b",
    ("h", "j", "p", "q"),
    ("g",),
    "K4",
    ("q", "g", "h", "j", "s"),
    ("p",),
    "K5",
    ("h", "j", "p", "q", "s"),
    ("j", "p", "q", "s"),
    ("p", "q", "s"),
    ("s",),
)
ROUND_COST = pl.CostEstimate(flops=50_000_000_000, transcendentals=0, bytes_accessed=0)
ANY = pl.BlockSpec(memory_space=pl.ANY)
VM = pl.BlockSpec(memory_space=pltpu.VMEM)


def no_time(**_):
    return pl.CostEstimate(flops=0, transcendentals=0, bytes_accessed=0)


def bucket_of(relative):
    distance = jnp.abs(relative)
    counted = jnp.zeros_like(distance)
    for threshold in LIMITS:
        counted = counted + (distance >= threshold).astype(jnp.int32)
    inside = jnp.where(distance < 8, distance, 8 + counted)
    return inside + jnp.where(relative > 0, 16, 0).astype(jnp.int32)


def offset_lookup():
    k = lax.broadcasted_iota(jnp.int32, (8, SPAN, NB), 1)
    b = lax.broadcasted_iota(jnp.int32, (8, SPAN, NB), 0)
    c = lax.broadcasted_iota(jnp.int32, (8, SPAN, NB), 2)
    offset = k - b
    offset = jnp.where(offset >= SEQ, offset - SPAN, offset)
    return (bucket_of(offset) == c).astype(F32)


def bit_orders(n, rows, wanted):
    if n & (n - 1) or n < 8 or rows % 16:
        return {name: None for name in wanted}
    high = list(range(1, n.bit_length() - 1))
    if n == 32:
        number = {"x": 1, "y": 2, "z": 3, "Z": 4}
        return {name: tuple([number[c] for c in order] + [0] for order in pair) for name, pair in wanted.items()}
    return {name: (high + [0], high[1:] + high[:1] + [0]) for name in wanted}


def swap(array, bits, n):
    return lax.ppermute(array, AXIS, [(i, i ^ (1 << bits[i & 1])) for i in range(n)])


def relative(bits, t):
    return sum(1 << b for k, b in enumerate(bits) if (t >> k) & 1)


def block_row(me, orders, t, n, rows):
    one, two = (relative(order, t) for order in (orders if t < n // 2 else orders[::-1]))
    return pl.multiple_of((me ^ (one + (me & 1) * (two - one))) * rows, rows)


def after(value, *others):
    return lax.optimization_barrier((value, *others))[0] if others else value


def round_kernel(plan, *refs):
    count = sum(len(kinds) for _, kinds in plan)
    inputs, outs = list(refs[:count]), refs[count:]
    for (kind, kinds), out in zip(plan, outs):
        terms = [inputs.pop(0) for _ in kinds]
        if kind == "join":
            half = terms[0].shape[0]
            out[:half] = terms[0][...]
            out[half:] = terms[1][...]
        elif kind == "small" and len(terms) == 4:
            out[...] = (terms[0][...] + terms[1][...]) + (terms[2][...] + terms[3][...])
        else:
            total = terms[0][...].astype(F32)
            for term in terms[1:]:
                total = total + term[...].astype(F32)
            out[...] = total.astype(out.dtype)


def do_round(jobs):
    plan, specs, arrays, shapes, out_specs = [], [], [], [], []
    moved = 0
    for kind, terms, size, index, dtype in jobs:
        if kind == "small":
            specs += [pl.BlockSpec(term.shape, lambda i: (0, 0)) for term in terms]
            shapes.append(jax.ShapeDtypeStruct(terms[0].shape, dtype))
            out_specs.append(specs[-1])
        else:
            rows, cols = terms[0].shape[1] // 2, terms[0].shape[2]
            specs += [pl.BlockSpec((size, rows, cols), lambda i, k=index: (k, i, 0)) for _ in terms]
            made = 2 * size if kind == "join" else size
            shapes.append(jax.ShapeDtypeStruct((made, 2 * rows, cols), dtype))
            out_specs.append(pl.BlockSpec((made, rows, cols), lambda i: (0, i, 0)))
            moved += 2 * (len(terms) + 1) * size * 2 * rows * cols
        plan.append((kind, (0,) * len(terms)))
        arrays += terms
    return pl.pallas_call(
        functools.partial(round_kernel, tuple(plan)),
        grid=(2,),
        out_shape=shapes,
        in_specs=specs,
        out_specs=out_specs,
        compiler_params=pltpu.CompilerParams(vmem_limit_bytes=VMEM_LIMIT),
        cost_estimate=ROUND_COST,
        name="exchange_round",
    )(*arrays)


class Gather:
    def __init__(self, own, orders, n, early):
        self.have, self.orders, self.n, self.last = own[None], orders, n, len(orders[0]) - 1
        self.step, self.parts, self.flights, self.early = 0, None, [self.have], early

    def waits(self):
        return self.flights

    def job(self):
        if 0 < self.step < self.last:
            return "join", [self.have, self.flights[0]], self.have.shape[0], 0, BF16
        return None

    def advance(self, made=None):
        if self.step > self.last:
            self.parts = [self.have, self.far, *self.near, *self.flights]
            return self.flights
        bits = [order[self.step] for order in self.orders]
        core = [order[self.last] for order in self.orders]
        if self.step == self.last:
            self.far, *self.near = self.flights
            self.flights = [swap(self.far, bits, self.n)]
            if not self.near:
                self.flights.insert(0, swap(after(self.have, self.far), bits, self.n))
        else:
            if self.step == 0:
                self.have = self.flights[0]
            else:
                self.have = jnp.concatenate([self.have, self.flights[0]], axis=0) if made is None else made
            self.flights = [swap(self.have, bits, self.n)]
            if self.early and self.step == self.last - 1:
                self.flights.append(swap(self.have, core, self.n))
        self.step += 1
        return [self.far if self.step > self.last else self.have]

    def finish(self):
        while self.parts is None:
            self.advance()
        return self.parts


class Scatter:
    def __init__(self, send, keep, orders, n):
        self.orders, self.n, self.step = orders, n, len(orders[0]) - 1
        self.terms, self.flights, self.result = [keep], [send], None
        self.first = self.step

    def waits(self):
        return self.flights

    def job(self):
        if self.step == self.first:
            return None
        half = 1 << max(self.step, 0)
        return "sum", self.terms + self.flights, half, int(self.step >= 0), BF16 if self.step >= 0 else F32

    def advance(self, made=None):
        send = self.flights[0]
        if self.step < self.first:
            _, terms, half, index, dtype = self.job()
            send = sum(term[half * index : half * (index + 1)].astype(F32) for term in terms) if made is None else made
            self.terms = terms
            if self.step < 0:
                self.result = send[0]
                return [send]
        send = send.astype(BF16)
        self.flights = [swap(send, [order[self.step] for order in self.orders], self.n)]
        self.step -= 1
        return [send]

    def finish(self):
        while self.result is None:
            self.advance()
        return self.result


class SumAll:
    def __init__(self, values, n):
        bits = list(range(n.bit_length() - 1))
        self.masks = [(1 << b,) for b in bits[:-3]] + [tuple(m << bits[-3] for m in (1, 2, 3)), (1 << bits[-1],)]
        self.values, self.n, self.step, self.result, self.flights = values, n, 0, None, [values]

    def waits(self):
        return self.flights

    def job(self):
        return ("small", [self.values, *self.flights], 0, 0, F32) if self.step else None

    def advance(self, made=None):
        if self.step == 0:
            (self.values,) = self.flights
        elif made is None:
            self.values = self.total()
        else:
            self.values = made
        if self.step == len(self.masks):
            self.result = self.values
        else:
            pairs = [[(i, i ^ mask) for i in range(self.n)] for mask in self.masks[self.step]]
            self.flights = [lax.ppermute(self.values, AXIS, pair) for pair in pairs]
        self.step += 1
        return [self.values]

    def total(self):
        if len(self.flights) == 1:
            return self.values + self.flights[0]
        one, two, three = self.flights
        return (self.values + one) + (two + three)

    def finish(self):
        while self.result is None:
            self.advance()
        return self.result


class Layout:
    def __init__(self, n, rows, cuts, orders):
        self.n, self.rows = n, rows
        self.cuts, self.orders = cuts, orders
        self.paired = orders[0] is not None

    def spans(self):
        return tuple(zip((0,) + tuple(self.cuts[:-1]), self.cuts))

    def count(self):
        return 4 * len(self.cuts) if self.paired else 1

    def load(self, me, refs, full, sems, first=0, cols=None, chunk=None):
        size = full.shape[0]
        begin, end = cols or (0, self.cuts[-1])
        chunk = chunk or size
        if not self.paired:
            waits = []
            for c in range(size // chunk):
                source = refs[0].at[first + c * chunk : first + (c + 1) * chunk, begin:end]
                copy = pltpu.make_async_copy(source, full.at[c * chunk : (c + 1) * chunk], sems.at[c])
                copy.start()
                waits.append(copy.wait)
            return waits
        whole_rows = size == self.n * self.rows
        for s, ((lo, hi), orders) in enumerate(zip(self.spans(), self.orders)):
            low, high = max(lo, begin), min(hi, end)
            if low >= high:
                continue
            for t in range(self.n):
                ref = refs[4 * s + t // (self.n // 4)].at[t % (self.n // 4), :, low - lo : high - lo]
                row = block_row(me, orders, t, self.n, self.rows)

                def start(row, ref=ref, low=low, high=high):
                    target = full.at[pl.ds(row, self.rows), low - begin : high - begin]
                    sem = sems.at[0 if chunk == size else lax.div(row, chunk)]
                    pltpu.make_async_copy(ref, target, sem).start()

                if whole_rows:
                    start(row)
                else:
                    row = pl.multiple_of(row - first, self.rows)
                    pl.when(jnp.logical_and(row >= 0, row < size))(functools.partial(start, row))
        def wait(c):
            view = full.at[c * chunk : (c + 1) * chunk]
            pltpu.make_async_copy(view, view, sems.at[c]).wait()

        return [functools.partial(wait, c) for c in range(size // chunk)]

    def out_shapes(self):
        if not self.paired:
            return [jax.ShapeDtypeStruct((self.n * self.rows, self.cuts[-1]), BF16)]
        return [jax.ShapeDtypeStruct((self.n // 2, self.rows, self.cuts[-1]), BF16)] * 2

    def store(self, me, stage, refs, sem, cols=None):
        begin, end = cols or (0, self.cuts[-1])
        if not self.paired:
            copy = pltpu.make_async_copy(stage.at[:, begin:end], refs[0].at[:, begin:end], sem)
            copy.start()
            return copy.wait
        half = self.n // 2
        for t in [*range(half, self.n), *range(half)]:
            row = block_row(me, self.orders[0], t, self.n, self.rows)
            target = refs[0 if t >= half else 1].at[t % half, :, begin:end]
            pltpu.make_async_copy(stage.at[pl.ds(row, self.rows), begin:end], target, sem).start()
        view = stage.at[:, begin:end]
        return pltpu.make_async_copy(view, view, sem).wait


def dot(a, b):
    return lax.dot_general(a, b, (((1,), (0,)), ((), ())), preferred_element_type=F32)


def dot_nt(a, b):
    return lax.dot_general(a, b, (((1,), (1,)), ((), ())), preferred_element_type=F32)


def dot_tn(a, b):
    return lax.dot_general(a, b, (((0,), (0,)), ((), ())), preferred_element_type=F32)


def row_scale(values):
    return lax.rsqrt(jnp.mean(values * values, axis=-1, keepdims=True) + EPSILON)


def toeplitz(base):
    return jnp.concatenate(
        [(pltpu.roll(base, 8 * a, 1) if a else base)[:, :SEQ] for a in range(SEQ // 8)], axis=0
    )


def diagonals(scores):
    total = None
    for a in range(SEQ // 8):
        rows = scores[8 * a : 8 * a + 8]
        rows = jnp.concatenate([rows, jnp.zeros((8, SPAN - SEQ), F32)], axis=1)
        if a:
            rows = pltpu.roll(rows, SPAN - 8 * a, 1)
        total = rows if total is None else total + rows
    return total


def transposed(values):
    return values.T


def copy_out(copies, sems, k, source, target):
    copy = pltpu.make_async_copy(source, target, sems.at[k])
    copy.start()
    copies.append(copy)


def pack_kernel(spans, *refs):
    q_ref, k_ref, v_ref, o_ref, one_ref, two_ref = refs[:6]
    rows, width = q_ref.shape
    line = lax.broadcasted_iota(jnp.int32, (LANES, rows), 0)
    gains = jnp.where(line == 0, one_ref[...], jnp.where(line == 1, two_ref[...], 0.0)).T
    for (low, high), out in zip(spans, refs[6:]):
        for k, ref in enumerate((q_ref, k_ref, v_ref, o_ref, gains)):
            begin, end = max(low, k * width), min(high, k * width + ref.shape[1])
            if begin < end:
                out[:, begin - low : end - low] = ref[:, begin - k * width : end - k * width].astype(BF16)


def pack(lay, weights, gains):
    rows = weights[0].shape[0]
    return pl.pallas_call(
        functools.partial(pack_kernel, lay.spans()),
        out_shape=[jax.ShapeDtypeStruct((rows, high - low), BF16) for low, high in lay.spans()],
        in_specs=[VM] * 6,
        out_specs=[VM] * len(lay.cuts),
        name="pack",
    )(*weights, *(gain.reshape(1, rows) for gain in gains))


def attend(seqs, h1, weights, segments_ref, base_ref, q_ref, k_ref, v_ref, p_ref, c_ref, ct_ref):
    for ref, weight in zip((q_ref, k_ref, v_ref), weights):
        ref[...] = dot(h1, weight).astype(BF16)
    first = lax.broadcasted_iota(jnp.int32, (SEQ, LANES), 1) < HEAD
    for p in range(GROUP // LANES):
        lanes = slice(p * LANES, (p + 1) * LANES)
        biases = [toeplitz(base_ref[2 * p + o]) for o in range(2)]
        for s in range(seqs):
            rows = slice(s * SEQ, (s + 1) * SEQ)
            q2, k2, v2 = q_ref[rows, lanes], k_ref[rows, lanes], v_ref[rows, lanes]
            line = jnp.broadcast_to(segments_ref[s : s + 1, :], (SEQ, SEQ))
            allowed = line.T == line
            made = []
            for o in range(2):
                mine = jnp.where(first == (o == 0), q2, jnp.zeros_like(q2))
                scores = jnp.where(allowed, dot_nt(mine, k2) + biases[o], MASKED)
                exponent = jnp.exp(scores - jnp.max(scores, axis=-1, keepdims=True))
                prob = exponent * (1.0 / jnp.sum(exponent, axis=-1, keepdims=True))
                p_ref[s, 2 * p + o] = prob
                made.append(dot(prob.astype(BF16), v2))
            c_ref[rows, lanes] = jnp.where(first, made[0], made[1]).astype(BF16)
    ct_ref[...] = transposed(c_ref[...])


def early_kernel(lay, seqs, width, steps, *refs):
    m = lay.count()
    x_ref, segments_ref, base_ref = refs[:3]
    blocks = refs[3 : 3 + m]
    wa_out, gain_ref, h1_ref, h1t_ref = refs[3 + m : 7 + m]
    outs = refs[7 + m : 13 + m]
    wa, gains_s, sems = refs[13 + m :]
    step = pl.program_id(0)

    @pl.when(step == 0)
    def _():
        me = lax.axis_index(AXIS)
        waits = lay.load(me, blocks, gains_s, sems.at[0:1], cols=(4 * width, 4 * width + LANES))
        for j in range(3):
            cols = (j * width, (j + 1) * width)
            waits += lay.load(me, blocks, wa.at[:, j * width : (j + 1) * width], sems.at[1 + j : 2 + j], cols=cols)
        waits[0]()
        gains = gains_s[...].astype(F32).T
        gain_ref[...] = gains[:8]
        x = x_ref[...].astype(F32)
        h1 = (x * row_scale(x) * gains[0:1]).astype(BF16)
        h1_ref[...] = h1
        h1t_ref[...] = transposed(h1)
        for wait in waits[1:]:
            wait()
        pltpu.make_async_copy(wa, wa_out, sems.at[0]).start()

    weights = [wa[:, pl.ds(pl.multiple_of(j * width + step * GROUP, GROUP), GROUP)] for j in range(3)]
    attend(seqs, h1_ref[...], weights, segments_ref, base_ref, *outs)

    @pl.when(step == steps - 1)
    def _():
        pltpu.make_async_copy(wa, wa_out, sems.at[0]).wait()


def late_kernel(lay, seqs, steps, *refs):
    m = lay.count()
    h1_ref, wq_ref, wk_ref, wv_ref, segments_ref, base_ref, x_ref, gain_ref, context_ref = refs[:9]
    blocks = refs[9 : 9 + m]
    outs, (x1_ref, h2_ref, h2t_ref, wo_out) = refs[9 + m : 15 + m], refs[15 + m : 19 + m]
    context, wo_ref, sems = refs[19 + m :]
    step = pl.program_id(0)
    width = x_ref.shape[1]

    @pl.when(step == 0)
    def _():
        lay.load(lax.axis_index(AXIS), blocks, wo_ref, sems.at[0:1], cols=(3 * width, 4 * width))

    attend(seqs, h1_ref[...], (wq_ref[...], wk_ref[...], wv_ref[...]), segments_ref, base_ref, *outs)
    context[:, pl.ds(pl.multiple_of(step * GROUP, GROUP), GROUP)] = outs[4][...]

    @pl.when(step == steps - 1)
    def _():
        pltpu.make_async_copy(wo_ref, wo_ref, sems.at[0]).wait()
        copy = pltpu.make_async_copy(wo_ref, wo_out, sems.at[1])
        copy.start()
        early = context_ref.shape[1]
        for c in range(0, width, 512):
            cols = slice(c, c + 512)
            x1_ref[:, cols] = (
                x_ref[:, cols].astype(F32)
                + dot(context_ref[...], wo_ref[:early, cols])
                + dot(context[...], wo_ref[early:, cols])
            )
        x1 = x1_ref[...]
        h2 = (x1 * row_scale(x1) * gain_ref[1:2, :]).astype(BF16)
        h2_ref[...] = h2
        h2t_ref[...] = transposed(h2)
        copy.wait()


def attention_outputs(tokens, width, count):
    sds = jax.ShapeDtypeStruct
    seqs, heads = tokens // SEQ, GROUP // HEAD
    shapes = [sds((tokens, count * GROUP), BF16)] * 3
    specs = [pl.BlockSpec((tokens, GROUP), lambda i: (0, i))] * 3
    shapes.append(sds((seqs, count * heads, SEQ, SEQ), F32))
    specs.append(pl.BlockSpec((seqs, heads, SEQ, SEQ), lambda i: (0, i, 0, 0)))
    shapes.append(sds((tokens, count * GROUP), BF16))
    specs.append(pl.BlockSpec((tokens, GROUP), lambda i: (0, i)))
    shapes.append(sds((count * GROUP, tokens), BF16))
    specs.append(pl.BlockSpec((GROUP, tokens), lambda i: (i, 0)))
    return shapes, specs


def whole(shape):
    return pl.BlockSpec(shape, lambda i: (0,) * len(shape))


def attention_cost(tokens, width, count):
    share = count * GROUP
    return no_time(
        flops=2 * tokens * width * 3 * share + 16 * tokens * SEQ * share,
        transcendentals=tokens * SEQ * share // HEAD,
        bytes_accessed=(6 * width * share + 8 * tokens * share + 4 * tokens * SEQ * share // HEAD),
    )


def attention_early(lay, x, segments, base, blocks, count):
    tokens, width = x.shape
    seqs, wide, heads = tokens // SEQ, 3 * width, GROUP // HEAD
    sds = jax.ShapeDtypeStruct
    shapes, specs = attention_outputs(tokens, width, count)
    return pl.pallas_call(
        functools.partial(early_kernel, lay, seqs, width, count),
        grid=(count,),
        out_shape=[sds((width, wide), BF16), sds((8, width), F32), sds((tokens, width), BF16), sds((width, tokens), BF16)]
        + shapes,
        in_specs=[
            whole((tokens, width)),
            whole((seqs, SEQ)),
            pl.BlockSpec((heads, 8, SPAN), lambda i: (i, 0, 0)),
        ]
        + [ANY] * len(blocks),
        out_specs=[ANY, whole((8, width)), whole((tokens, width)), whole((width, tokens))] + specs,
        scratch_shapes=[
            pltpu.VMEM((width, wide), BF16),
            pltpu.VMEM((width, LANES), BF16),
            pltpu.SemaphoreType.DMA((4,)),
        ],
        compiler_params=pltpu.CompilerParams(vmem_limit_bytes=VMEM_LIMIT),
        cost_estimate=attention_cost(tokens, width, count),
        name="attention_early",
    )(x, segments.reshape(seqs, SEQ), base, *blocks)


def attention_late(lay, h1, wa, segments, base, count, x, gain, context, blocks):
    tokens, width = h1.shape
    seqs, heads, skip = tokens // SEQ, GROUP // HEAD, width // GROUP - count
    shapes, specs = attention_outputs(tokens, width, count)
    per = width // GROUP
    sds = jax.ShapeDtypeStruct
    return pl.pallas_call(
        functools.partial(late_kernel, lay, seqs, count),
        grid=(count,),
        out_shape=shapes
        + [sds((tokens, width), F32), sds((tokens, width), BF16), sds((width, tokens), BF16), sds((width, width), BF16)],
        in_specs=[whole((tokens, width))]
        + [pl.BlockSpec((width, GROUP), lambda i, j=j: (0, j * per + skip + i)) for j in range(3)]
        + [
            whole((seqs, SEQ)),
            pl.BlockSpec((heads, 8, SPAN), lambda i: (skip + i, 0, 0)),
            whole((tokens, width)),
            whole((8, width)),
            whole(context.shape),
        ]
        + [ANY] * len(blocks),
        out_specs=specs + [whole((tokens, width)), whole((tokens, width)), whole((width, tokens)), ANY],
        scratch_shapes=[
            pltpu.VMEM((tokens, count * GROUP), BF16),
            pltpu.VMEM((width, width), BF16),
            pltpu.SemaphoreType.DMA((2,)),
        ],
        compiler_params=pltpu.CompilerParams(vmem_limit_bytes=VMEM_LIMIT),
        cost_estimate=attention_cost(tokens, width, count),
        name="attention_late",
    )(h1, wa, wa, wa, segments.reshape(seqs, SEQ), base, x, gain, context, *blocks)


def inner_kernel(lay, lay_out, chunk, *refs):
    m, k = lay.count(), len(lay_out.out_shapes())
    h2_ref, e_ref = refs[:2]
    blocks = refs[2 : 2 + m]
    z_out, g_out = refs[2 + m : 4 + m]
    grads = refs[4 + m : 4 + m + k]
    wi, z_s, g_s, stage, lsem, osem, gsem = refs[4 + m + k :]
    me = lax.axis_index(AXIS)
    hidden = wi.shape[1]
    parts = 4
    size = hidden // parts
    waits = []
    for p in range(parts):
        cols = (p * size, (p + 1) * size)
        waits += lay.load(me, blocks, wi.at[:, p * size : (p + 1) * size], lsem.at[p : p + 1], cols=cols)

    def step(c, carry):
        cols = pl.ds(pl.multiple_of(c * chunk, chunk), chunk)
        u = dot(h2_ref[...], wi[:, cols])
        cdf = 0.5 * (1.0 + lax.erf(u * (1.0 / math.sqrt(2.0))))
        z = (u * cdf).astype(BF16)
        z_s[:, cols] = z
        g_s[:, cols] = cdf + u * jnp.exp(-0.5 * u * u) * (1.0 / math.sqrt(2.0 * math.pi))
        stage[cols, :] = dot(transposed(z), e_ref[...]).astype(BF16)
        pltpu.make_async_copy(z_s.at[:, cols], z_out.at[:, cols], osem.at[0]).start()
        pltpu.make_async_copy(g_s.at[:, cols], g_out.at[:, cols], osem.at[1]).start()
        return carry

    for p in range(parts):
        waits[p]()
        lax.fori_loop(p * size // chunk, (p + 1) * size // chunk, step, 0)
    done = lay_out.store(me, stage, grads, gsem)
    pltpu.make_async_copy(z_s, z_out, osem.at[0]).wait()
    pltpu.make_async_copy(g_s, g_out, osem.at[1]).wait()
    done()


def inner_forward(lay, lay_out, h2, cotangent, blocks, hidden):
    tokens, width = h2.shape
    sds = jax.ShapeDtypeStruct
    grads = lay_out.out_shapes()
    return pl.pallas_call(
        functools.partial(inner_kernel, lay, lay_out, 512),
        out_shape=[sds((tokens, hidden), BF16), sds((tokens, hidden), F32)] + grads,
        in_specs=[VM] * 2 + [ANY] * len(blocks),
        out_specs=[ANY] * (2 + len(grads)),
        scratch_shapes=[
            pltpu.VMEM((width, hidden), BF16),
            pltpu.VMEM((tokens, hidden), BF16),
            pltpu.VMEM((tokens, hidden), F32),
            pltpu.VMEM((hidden, width), BF16),
            pltpu.SemaphoreType.DMA((4,)),
            pltpu.SemaphoreType.DMA((2,)),
            pltpu.SemaphoreType.DMA,
        ],
        compiler_params=pltpu.CompilerParams(vmem_limit_bytes=VMEM_LIMIT),
        cost_estimate=no_time(
            flops=4 * tokens * width * hidden, transcendentals=2 * tokens * hidden, bytes_accessed=32 * MIB
        ),
        name="feedforward_inner",
    )(h2, cotangent, *blocks)


def outer_kernel(lay_i, lay_f, lay_g, chunk, first, last, *refs):
    mi, mf = lay_i.count(), lay_f.count()
    e_ref, h2t_ref, g_in = refs[:3]
    at = 3
    if last:
        x1_ref, gain_ref, dh_ref = refs[3:6]
        contexts = refs[6:8]
        at = 8
    inner, outer = refs[at : at + mi], refs[at + mi : at + mi + mf]
    at += mi + mf
    dx1_ref, at = refs[at], at + 1
    if last:
        da_ref, dgain_ref = refs[at : at + 2]
        at += 2
    kg = len(lay_g.out_shapes())
    grads, at = refs[at : at + kg], at + kg
    wi, wf, g_s, stage, fsem, lsem, isem, gsem = refs[at:]
    me = lax.axis_index(AXIS)
    size = wi.shape[1]
    steps = size // chunk
    outer_waits = lay_f.load(me, outer, wf, fsem, first=first, chunk=chunk)
    copies, inner_waits = [], []
    for c in range(steps):
        source = g_in.at[:, first + c * chunk : first + (c + 1) * chunk]
        copies.append(pltpu.make_async_copy(source, g_s.at[:, c * chunk : (c + 1) * chunk], isem.at[c]))
        copies[-1].start()
    wide = 2 * chunk
    for c in range(size // wide):
        target = wi.at[:, c * wide : (c + 1) * wide]
        cols = (first + c * wide, first + (c + 1) * wide)
        inner_waits += lay_i.load(me, inner, target, lsem.at[c : c + 1], cols=cols)
    e = e_ref[...]
    for c in range(steps):
        cols = slice(c * chunk, (c + 1) * chunk)
        outer_waits[c]()
        copies[c].wait()
        du = (dot_nt(e, wf[cols, :]) * g_s[:, cols]).astype(BF16)
        stage[:, cols] = dot(h2t_ref[...], du).astype(BF16)
        if c % 2 == 0:
            inner_waits[c // 2]()
        part = dot_nt(du, wi[:, cols])
        if c == 0:
            dx1_ref[...] = part + dh_ref[...] if last else part
        else:
            dx1_ref[...] += part
    if last:
        dh2 = dx1_ref[...]
        x1 = x1_ref[...]
        gain = gain_ref[1:2, :]
        scale = row_scale(x1)
        dgain_ref[...] = jnp.broadcast_to(jnp.sum(dh2 * (x1 * scale), axis=0, keepdims=True), dgain_ref.shape)
        mean = jnp.mean(x1 * gain * dh2, axis=-1, keepdims=True)
        dx1 = e.astype(F32) + scale * gain * dh2 - x1 * (scale * scale * scale) * mean
        dx1_ref[...] = dx1
        da = dx1.astype(BF16)
        da_ref[...] = da
        rows = stage.shape[0] // 2
        for p, context in enumerate(contexts):
            stage[p * rows : (p + 1) * rows, size:] = dot(context[...], da).astype(BF16)
    lay_g.store(me, stage, grads, gsem)()


def outer_backward(lay_i, lay_f, lay_g, first, size, cotangent, h2t, g, inner, outer, more=()):
    tokens, width = cotangent.shape
    chunk = 512
    last = first > 0
    sds = jax.ShapeDtypeStruct
    out_shape = [sds((tokens, width), F32)]
    out_specs = [VM]
    if last:
        out_shape += [sds((tokens, width), BF16), sds((8, width), F32)]
        out_specs += [VM] * 2
    grads = lay_g.out_shapes()
    return pl.pallas_call(
        functools.partial(outer_kernel, lay_i, lay_f, lay_g, chunk, first, last),
        out_shape=out_shape + grads,
        in_specs=[VM, VM, ANY] + [VM] * len(more) + [ANY] * (len(inner) + len(outer)),
        out_specs=out_specs + [ANY] * len(grads),
        scratch_shapes=[
            pltpu.VMEM((width, size), BF16),
            pltpu.VMEM((size, width), BF16),
            pltpu.VMEM((tokens, size), F32),
            pltpu.VMEM((width, lay_g.cuts[-1]), BF16),
            pltpu.SemaphoreType.DMA((size // chunk,)),
            pltpu.SemaphoreType.DMA((size // chunk // 2,)),
            pltpu.SemaphoreType.DMA((size // chunk,)),
            pltpu.SemaphoreType.DMA,
        ],
        compiler_params=pltpu.CompilerParams(vmem_limit_bytes=VMEM_LIMIT),
        cost_estimate=no_time(
            flops=6 * tokens * width * size + 2 * last * tokens * width * width,
            transcendentals=tokens,
            bytes_accessed=24 * MIB,
        ),
        name="feedforward_outer_" + "ab"[last],
    )(cotangent, h2t, g, *more, *inner, *outer)


def scores_kernel(lay, seqs, width, steps, *refs):
    k = len(lay.out_shapes())
    da_ref, wo_ref, q_ref, k_ref, v_ref, p_ref, h1t_ref = refs[:7]
    dq_ref, dk_ref, dv_ref, table_ref = refs[7:11]
    grads = refs[11 : 11 + k]
    dc, stage, gsem = refs[11 + k :]
    step = pl.program_id(0)
    dc[...] = dot_nt(da_ref[...], wo_ref[...]).astype(BF16)
    first = lax.broadcasted_iota(jnp.int32, (SEQ, LANES), 1) < HEAD
    for p in range(GROUP // LANES):
        lanes = slice(p * LANES, (p + 1) * LANES)
        totals = [None, None]
        for s in range(seqs):
            rows = slice(s * SEQ, (s + 1) * SEQ)
            dc2, q2, k2, v2 = dc[rows, lanes], q_ref[rows, lanes], k_ref[rows, lanes], v_ref[rows, lanes]
            made = []
            for o in range(2):
                prob = p_ref[s, 2 * p + o]
                mine = jnp.where(first == (o == 0), dc2, jnp.zeros_like(dc2))
                dprob = dot_nt(mine, v2)
                inner = jnp.sum(prob * dprob, axis=-1, keepdims=True)
                ds = (prob * (dprob - inner)).astype(BF16)
                wide = ds.astype(F32)
                totals[o] = wide if totals[o] is None else totals[o] + wide
                made.append(
                    (dot(ds, k2), dot(transposed(ds), q2), dot(transposed(prob.astype(BF16)), dc2))
                )
            for ref, one, two in zip((dq_ref, dk_ref, dv_ref), *made):
                ref[rows, lanes] = jnp.where(first, one, two).astype(BF16)
        for o in range(2):
            table_ref[2 * p + o] = diagonals(totals[o])
    for j, ref in enumerate((dq_ref, dk_ref, dv_ref)):
        col = pl.ds(pl.multiple_of((3 * step + j) * GROUP, GROUP), GROUP)
        stage[:, col] = dot(h1t_ref[...], ref[...]).astype(BF16)

    @pl.when(step == steps - 1)
    def _():
        lay.store(lax.axis_index(AXIS), stage, grads, gsem)()


def scores_backward(lay, part, da, wo, q, k, v, p, h1t):
    tokens, width = da.shape
    count = q.shape[1] // GROUP
    seqs, heads = tokens // SEQ, GROUP // HEAD
    sds = jax.ShapeDtypeStruct
    grads = lay.out_shapes()
    share = count * GROUP
    return pl.pallas_call(
        functools.partial(scores_kernel, lay, seqs, width, count),
        grid=(count,),
        out_shape=[sds((tokens, share), BF16)] * 3 + [sds((count * heads, 8, SPAN), F32)] + grads,
        in_specs=[whole((tokens, width)), pl.BlockSpec((GROUP, width), lambda i: (part * count + i, 0))]
        + [pl.BlockSpec((tokens, GROUP), lambda i: (0, i))] * 3
        + [pl.BlockSpec((seqs, heads, SEQ, SEQ), lambda i: (0, i, 0, 0)), whole((width, tokens))],
        out_specs=[pl.BlockSpec((tokens, GROUP), lambda i: (0, i))] * 3
        + [pl.BlockSpec((heads, 8, SPAN), lambda i: (i, 0, 0))]
        + [ANY] * len(grads),
        scratch_shapes=[
            pltpu.VMEM((tokens, GROUP), BF16),
            pltpu.VMEM((width, 3 * share), BF16),
            pltpu.SemaphoreType.DMA,
        ],
        compiler_params=pltpu.CompilerParams(vmem_limit_bytes=VMEM_ALL),
        cost_estimate=no_time(
            flops=8 * tokens * width * share + 40 * tokens * SEQ * share,
            transcendentals=0,
            bytes_accessed=16 * MIB,
        ),
        name="attention_backward_" + "ab"[part],
    )(da, wo, q, k, v, p, h1t)


def inputs_kernel(width, parts, *refs):
    x_ref, dx1_ref, gain_ref = refs[:3]
    grads = refs[3 : 3 + 3 * parts]
    wa_in, dx_ref, dgain_ref, wa, dh, sem = refs[3 + 3 * parts :]
    copies = []
    for j in range(3):
        cols = slice(j * width, (j + 1) * width)
        copies.append(pltpu.make_async_copy(wa_in.at[:, cols], wa.at[:, cols], sem.at[j]))
        copies[-1].start()
    size = width // parts
    for j in range(3):
        copies[j].wait()
        for c in range(0, width, 512):
            for p in range(parts):
                low = j * width + p * size
                part = dot_nt(grads[3 * p + j][...], wa[c : c + 512, low : low + size])
                if j or p:
                    dh[:, c : c + 512] += part
                else:
                    dh[:, c : c + 512] = part
    x = x_ref[...].astype(F32)
    gain = gain_ref[0:1, :]
    scale = row_scale(x)
    dh1 = dh[...]
    dgain_ref[...] = jnp.broadcast_to(jnp.sum(dh1 * (x * scale), axis=0, keepdims=True), dgain_ref.shape)
    mean = jnp.mean(x * gain * dh1, axis=-1, keepdims=True)
    dx_ref[...] = (dx1_ref[...] + scale * gain * dh1 - x * (scale * scale * scale) * mean).astype(BF16)


def inputs_backward(x, dx1, gain, grads, wa):
    tokens, width = x.shape
    sds = jax.ShapeDtypeStruct
    return pl.pallas_call(
        functools.partial(inputs_kernel, width, len(grads) // 3),
        out_shape=[sds((tokens, width), BF16), sds((8, width), F32)],
        in_specs=[VM] * (3 + len(grads)) + [ANY],
        out_specs=[VM] * 2,
        scratch_shapes=[
            pltpu.VMEM((width, 3 * width), BF16),
            pltpu.VMEM((tokens, width), F32),
            pltpu.SemaphoreType.DMA((3,)),
        ],
        compiler_params=pltpu.CompilerParams(vmem_limit_bytes=VMEM_ALL),
        cost_estimate=no_time(
            flops=6 * tokens * width * width, transcendentals=tokens, bytes_accessed=16 * MIB
        ),
        name="inputs_backward",
    )(x, dx1, gain, *grads, wa)


def output_kernel(lay, *refs):
    m = lay.count()
    x1_ref, z_ref = refs[:2]
    blocks = refs[2 : 2 + m]
    out_ref, wf, sem = refs[2 + m :]
    lay.load(lax.axis_index(AXIS), blocks, wf, sem)[0]()
    width = wf.shape[1]
    for c in range(0, width, 512):
        cols = slice(c, c + 512)
        out_ref[:, cols] = (x1_ref[:, cols] + dot(z_ref[...], wf[:, cols])).astype(BF16)


def layer_output(lay, x1, z, blocks):
    tokens, width = x1.shape
    hidden = z.shape[1]
    return pl.pallas_call(
        functools.partial(output_kernel, lay),
        out_shape=jax.ShapeDtypeStruct((tokens, width), BF16),
        in_specs=[VM] * 2 + [ANY] * len(blocks),
        out_specs=VM,
        scratch_shapes=[
            pltpu.VMEM((hidden, width), BF16),
            pltpu.SemaphoreType.DMA((1,)),
        ],
        compiler_params=pltpu.CompilerParams(vmem_limit_bytes=VMEM_ALL),
        cost_estimate=no_time(
            flops=2 * tokens * width * hidden, transcendentals=0, bytes_accessed=16 * MIB
        ),
        name="layer_output",
    )(x1, z, *blocks)


def closing_kernel(count, *refs):
    terms, early_ref, outs = refs[:-4], refs[-4], refs[-3:]
    total = None
    for term in terms:
        value = term[0].astype(F32)
        total = value if total is None else total + value
    for j, out in enumerate(outs):
        for i in range(count):
            group = slice((3 * i + j) * GROUP, (3 * i + j + 1) * GROUP)
            out[:, i * GROUP : (i + 1) * GROUP] = early_ref[:, group]
            out[:, (count + i) * GROUP : (count + i + 1) * GROUP] = total[:, group]


def closing(terms, early):
    rows, share = early.shape
    count = share // (3 * GROUP)
    block = pl.BlockSpec((1, rows, share), lambda i: (0, 0, 0))
    width = 2 * count * GROUP
    return pl.pallas_call(
        functools.partial(closing_kernel, count),
        grid=(1,),
        out_shape=[jax.ShapeDtypeStruct((rows, width), F32)] * 3,
        in_specs=[block] * len(terms) + [whole((rows, share))],
        out_specs=[whole((rows, width))] * 3,
        cost_estimate=no_time(),
        name="projection_gradients",
    )(*terms, early)


def per_device(
    n,
    tokens,
    attention_gain,
    query_weight,
    key_weight,
    value_weight,
    output_weight,
    feedforward_gain,
    inner_weight,
    outer_weight,
    bias_table,
    segment_ids,
    positions,
    cotangent,
):
    del positions
    width = tokens.shape[1]
    hidden = inner_weight.shape[1]
    rows = query_weight.shape[0]
    orders = bit_orders(n, rows, ORDERS)
    wide = outer_weight.shape[0]
    count = width // GROUP // 2
    part = hidden // 4
    all_a = 4 * width + LANES
    def split(columns, name):
        pairs = tuple(orders[key] for key in ORDERS if key[:-1] == name)
        if len(pairs) < 2 or pairs[0] is None:
            return (columns,), pairs[:1]
        return (SPLIT[name] * columns // LANES // 100 * LANES, columns), pairs

    lay_a = Layout(n, rows, *split(all_a, "a"))
    lay_i = Layout(n, rows, *split(hidden, "i"))
    lay_f = Layout(n, wide, *split(width, "f"))
    lay = {
        "g": Layout(n, wide, (width,), (orders["g"],)),
        "h": Layout(n, rows, (part,), (orders["h"],)),
        "j": Layout(n, rows, (hidden - part + width,), (orders["j"],)),
        "p": Layout(n, rows, (3 * width // 2,), (orders["p"],)),
        "q": Layout(n, rows, (3 * width // 2,), (orders["q"],)),
    }
    chains, v, state = {}, {}, {"last": []}
    weights = (query_weight, key_weight, value_weight, output_weight)
    packed = pack(lay_a, weights, (attention_gain, feedforward_gain))
    blocks = {
        "a": packed,
        "i": [inner_weight[:, low:high].astype(BF16) for low, high in lay_i.spans()],
        "f": [outer_weight[:, low:high].astype(BF16) for low, high in lay_f.spans()],
    }
    for name, layout in (("a", lay_a), ("i", lay_i), ("f", lay_f)):
        for k, (block, pair) in enumerate(zip(blocks[name], layout.orders)):
            if layout.paired:
                chains[name + str(k)] = Gather(block, pair, n, name != "a")
            else:
                v[name + str(k)] = lax.all_gather(block, AXIS, axis=0, tiled=True)
    lookup = offset_lookup()
    base = jnp.einsum("bkc,ch->hbk", lookup, bias_table, precision=HIGHEST)
    state["base"] = [base]

    def gathered(name, layout):
        if not layout.paired:
            return [v[name + "0"]]
        found = []
        for k in range(len(layout.cuts)):
            found += chains[name + str(k)].finish()
        return found

    def tied(value):
        return after(value, *state["last"])

    def scatter(name, parts):
        if lay[name].paired:
            chains[name] = Scatter(*parts, lay[name].orders[0], n)
        else:
            v[name] = lax.psum_scatter(parts[0].astype(F32), AXIS, scatter_dimension=0, tiled=True)

    def run(name):
        if name == "K1a":
            out = attention_early(lay_a, tied(tokens), segment_ids, base, gathered("a", lay_a), count)
            v["wa"], v["gain"], v["h1"], v["h1t"], *v["early"] = out
            return [out[8]]
        if name == "K1b":
            context, blocks_a = v["early"][4], gathered("a", lay_a)
            out = attention_late(
                lay_a, tied(v["h1"]), v["wa"], segment_ids, base, count, tokens, v["gain"], context, blocks_a
            )
            v["late"], (v["x1"], v["h2"], v["h2t"], v["wo"]) = out[:6], out[6:]
            return [v["h2"]]
        if name == "K2a":
            out = inner_forward(lay_i, lay["g"], tied(v["h2"]), cotangent, gathered("i", lay_i), hidden)
            v["z"], v["slope"], *parts = out
            scatter("g", parts)
            return parts[:1]
        if name == "K2ba":
            inner, outer = gathered("i", lay_i), gathered("f", lay_f)
            out = outer_backward(lay_i, lay_f, lay["h"], 0, part, tied(cotangent), v["h2t"], v["slope"], inner, outer)
            v["dh2"], *parts = out
            scatter("h", parts)
            return parts[:1]
        if name == "K2bb":
            more = (v["x1"], v["gain"], tied(v["dh2"]), v["early"][5], v["late"][5])
            inner, outer = gathered("i", lay_i), gathered("f", lay_f)
            out = outer_backward(
                lay_i, lay_f, lay["j"], part, hidden - part, cotangent, v["h2t"], v["slope"], inner, outer, more
            )
            v["dx1"], v["da"], v["dgain2"], *parts = out
            scatter("j", parts)
            return parts[:1]
        if name in ("K3a", "K3b"):
            late = name == "K3b"
            saved, target = v["late" if late else "early"], "pq"[late]
            out = scores_backward(lay[target], int(late), tied(v["da"]), v["wo"], *saved[:4], v["h1t"])
            v["grads" + target], v["table" + target], parts = out[:3], out[3], out[4:]
            scatter(target, parts)
            return parts[:1]
        if name == "K4":
            grads = (*v["gradsp"], *v["gradsq"])
            v["dx"], dgain1 = inputs_backward(tokens, tied(v["dx1"]), v["gain"], grads, v["wa"])
            diagonal = jnp.concatenate([v["tablep"], v["tableq"]], axis=0)
            table = jnp.einsum("hbk,bkc->ch", diagonal, lookup, precision=HIGHEST)
            small = jnp.concatenate([dgain1[0], v["dgain2"][0], table.reshape(-1)]).reshape(-1, LANES)
            if n & (n - 1):
                v["s"] = lax.psum(small, AXIS)
            else:
                chains["s"] = SumAll(small, n)
            return [v["dx"]]
        v["out"] = layer_output(lay_f, v["x1"], tied(v["z"]), gathered("f", lay_f))
        return [v["out"]]

    def exchange(names):
        active = [chains[name] for name in names if name in chains]
        if not active:
            return []
        arrived = [flight for chain in active for flight in chain.waits()]
        arrived = list(lax.optimization_barrier((*arrived, *state["last"])))
        for chain in active:
            chain.flights = [arrived.pop(0) for _ in chain.waits()]
        jobs = [chain.job() for chain in active]
        wanted = [job for job in jobs if job]
        apart = len(wanted) == 1 and wanted[0][0] == "sum" and wanted[0][4] == BF16
        large = len(wanted) == 1 and wanted[0][2] * math.prod(wanted[0][1][0].shape[1:]) >= MIB // 2
        made = list(do_round(wanted)) if len(wanted) >= 3 or large or apart else []
        sent = []
        for chain, job in zip(active, jobs):
            sent += chain.advance(made.pop(0) if job and made else None)
        return sent

    for names in SCHEDULE:
        if isinstance(names, str):
            state["last"] = run(names)
        else:
            state["last"] = list(exchange(names) or state["last"]) + state.pop("base", [])

    def total(name):
        if name not in chains:
            return v[name]
        return chains[name].finish()

    small = total("s").reshape(-1)
    start = lax.axis_index(AXIS) * rows
    if "q" in chains and chains["q"].step < 0:
        projections = closing(chains["q"].terms + chains["q"].flights, total("p"))
    else:
        joined = jnp.concatenate([total("p"), total("q")], axis=1)
        groups = [range(j * GROUP, 3 * width, 3 * GROUP) for j in range(3)]
        projections = [jnp.concatenate([joined[:, low : low + GROUP] for low in lows], axis=1) for lows in groups]

    return (
        v["out"],
        v["dx"],
        lax.dynamic_slice(small, (start,), (rows,)),
        *projections,
        total("j")[:, hidden - part :],
        lax.dynamic_slice(small, (width + start,), (rows,)),
        jnp.concatenate([total("h"), total("j")[:, : hidden - part]], axis=1),
        total("g"),
        small[2 * width :].reshape(NB, HEADS),
    )


def solution(mesh):
    n = mesh.shape[AXIS]
    matrix, vector = P(AXIS, None), P(AXIS)
    return jax.shard_map(
        functools.partial(per_device, n),
        mesh=mesh,
        in_specs=(
            matrix,
            vector,
            matrix,
            matrix,
            matrix,
            matrix,
            vector,
            matrix,
            matrix,
            P(),
            vector,
            vector,
            matrix,
        ),
        out_specs=(
            matrix,
            matrix,
            vector,
            matrix,
            matrix,
            matrix,
            matrix,
            vector,
            matrix,
            matrix,
            P(),
        ),
        check_vma=False,
    )
```
